32 devices in a mesh: batch: 2 (over y), fsdp: 16 (over z, x, core).
Axes of the slice: x: 2, y: 2, z: 4, core: 2. Of those that a mesh axis runs over, the one named last changes fastest.
Arguments:
- trunk: bfloat16 [6144, 4096], P('fsdp', 'batch'), may hold values from -0.75 to 0.75
- pre_act: bfloat16 [4096, 1024], P(('batch', 'fsdp')), may hold values from -6 to 6
- proj_weight: bfloat16 [6144, 1024], P('fsdp'), may hold values from -0.1875 to 0.1875
- codebook: bfloat16 [2048, 1024], P('fsdp'), may hold values from -1.6 to 1.6
- value_weight: bfloat16 [1024, 601], P('fsdp'), may hold values from -1.6 to 1.6
- code_target: int32 [4096], P(('batch', 'fsdp')), may hold values from 0 to 2047
- value_bin: int32 [4096], P(('batch', 'fsdp')), may hold values from 0 to 599
- value_frac: int32 [4096], P(('batch', 'fsdp')), may hold values from 0 to 1024
Outputs:
- grad_trunk: bfloat16 [6144, 4096], P('fsdp', 'batch')
- grad_proj: float32 [6144, 1024], P('fsdp')
- grad_codebook: float32 [2048, 1024], P('fsdp')
- grad_value: float32 [1024, 601], P('fsdp')
The draws below stay inside these ranges and needn't reach their ends.
All inputs are finite; a program needn't handle non-finite values.
Results may differ from the reference program's by a relative error of at most 0.012.
Values may be sent and summed in bfloat16 or wider, within the bound.
A program may use at most 64 MiB of HBM per device.

```python
import math
import jax
import jax.numpy as jnp
from jax import lax

WIDTH = 6144
CODE_DIM = 1024
CODES = 2048
BINS = 601
ROWS_DEV = 128
POSITIONS = 4096
N_BATCH = 2
N_FSDP = 16


def draw_pre_act(key, part):
    entries = jnp.clip(jax.random.normal(jax.random.fold_in(key, 4), (POSITIONS, CODE_DIM), jnp.float32), -6.0, 6.0)
    return entries.astype(jnp.bfloat16)


def draw_codebook(key, part):
    spread = 5.0 / math.sqrt(CODE_DIM)
    entries = jnp.clip(jax.random.normal(jax.random.fold_in(key, 6), (CODES, CODE_DIM), jnp.float32), -4.0, 4.0) * spread
    return entries.astype(jnp.bfloat16)


def draw_value_weight(key, part):
    spread = 5.0 / math.sqrt(CODE_DIM)
    entries = jnp.clip(jax.random.normal(jax.random.fold_in(key, 9), (CODE_DIM, BINS), jnp.float32), -4.0, 4.0) * spread
    return entries.astype(jnp.bfloat16)


def place_ends(drawn, key, low, high):
    spot = [jax.random.randint(jax.random.fold_in(key, axis), (), 0, length) for axis, length in enumerate(drawn.shape)]
    longest = drawn.shape.index(max(drawn.shape))
    beside = spot[:longest] + [(spot[longest] + 1) % drawn.shape[longest]] + spot[longest + 1:]
    return drawn.at[tuple(spot)].set(low).at[tuple(beside)].set(high)


def shard_levels(stream_key, shape, split, least, high):
    factor_of = 1.0
    for axis_at, shards_of in split:
        heights = jax.random.uniform(jax.random.fold_in(jax.random.fold_in(stream_key, 6), axis_at), (shards_of,), jnp.float32, least / len(split), high / len(split))
        factor_of = factor_of * jnp.repeat(jnp.exp(heights), shape[axis_at] // shards_of).reshape((-1,) + (1,) * (len(shape) - 1 - axis_at))
    return factor_of


def normal_values(own_key, extent, scale, reach, shards=(), kind=jnp.bfloat16):
    values = jax.random.normal(own_key, extent, jnp.float32) * scale
    if len(shards) > 0:
        values = shard_levels(own_key, extent, shards, -0.22, 0.18) * values
    return jnp.clip(values, min=-reach, max=reach).astype(kind)


def setup_inputs(seed: int = 0) -> dict:
    key_of = jax.random.split(jax.random.key(seed), 9)
    trunk = normal_values(key_of[0], (WIDTH, POSITIONS), 0.05, 0.75, ((0, 16), (1, 2)))
    pre_act = draw_pre_act(jax.random.fold_in(key_of[8], 71), 0)
    proj_weight = normal_values(key_of[2], (WIDTH, CODE_DIM), CODE_DIM ** -0.5, 0.1875, ((0, 16),))
    codebook = draw_codebook(jax.random.fold_in(key_of[8], 71), 0)
    value_weight = draw_value_weight(jax.random.fold_in(key_of[8], 71), 0)
    code_target = place_ends(jax.random.randint(key_of[5], (POSITIONS,), 0, CODES), jax.random.fold_in(key_of[5], 1), 0, CODES - 1).astype(jnp.int32)
    value_bin = place_ends(jax.random.randint(key_of[6], (POSITIONS,), 0, BINS - 1), jax.random.fold_in(key_of[6], 1), 0, (BINS - 1) - 1).astype(jnp.int32)
    value_frac = place_ends(jax.random.randint(key_of[7], (POSITIONS,), 0, 1025), jax.random.fold_in(key_of[7], 1), 0, 1024).astype(jnp.int32)
    return dict(trunk=trunk, pre_act=pre_act, proj_weight=proj_weight, codebook=codebook, value_weight=value_weight, code_target=code_target, value_bin=value_bin, value_frac=value_frac)


def reference(trunk, pre_act, proj_weight, codebook, value_weight, code_target, value_bin, value_frac):
    block_rows = ROWS_DEV * N_FSDP
    trunk_blocks = trunk.reshape(WIDTH, N_BATCH, block_rows).transpose(1, 0, 2)
    pre_blocks = pre_act.reshape(N_BATCH, block_rows, CODE_DIM)
    code_blocks = code_target.reshape(N_BATCH, block_rows)
    bin_blocks = value_bin.reshape(N_BATCH, block_rows)
    frac_blocks = value_frac.reshape(N_BATCH, block_rows)
    code_ids = jnp.arange(CODES, dtype=jnp.int32)[None, :]
    bin_ids = jnp.arange(BINS, dtype=jnp.int32)[None, :]

    def block_step(totals, inputs):
        proj_total, code_total, value_total = totals
        trunk_cols, pre_rows, code_rows, bin_rows, frac_rows = inputs
        pre_value = pre_rows.astype(jnp.float32)
        gate_sigma = jax.nn.sigmoid(pre_value)
        active = (pre_value * gate_sigma).astype(jnp.bfloat16)
        code_logits = jnp.dot(active, codebook.T, preferred_element_type=jnp.float32)
        code_probs = jax.nn.softmax(code_logits, axis=-1)
        one_hot = (code_rows[:, None] == code_ids).astype(jnp.float32)
        code_delta = (code_probs - one_hot).astype(jnp.bfloat16)
        value_logits = jnp.dot(active, value_weight, preferred_element_type=jnp.float32)
        value_probs = jax.nn.softmax(value_logits, axis=-1)
        fraction = frac_rows.astype(jnp.float32)[:, None] / 1024.0
        target = jnp.where(bin_ids == bin_rows[:, None], 1.0 - fraction, 0.0)
        target = target + jnp.where(bin_ids == bin_rows[:, None] + 1, fraction, 0.0)
        value_delta = (value_probs - target).astype(jnp.bfloat16)
        backward = jnp.dot(code_delta, codebook, preferred_element_type=jnp.float32)
        backward = backward + jnp.dot(value_delta, value_weight.T, preferred_element_type=jnp.float32)
        pre_grad = (backward * gate_sigma * (1.0 + pre_value * (1.0 - gate_sigma))).astype(jnp.bfloat16)
        code_total = code_total + jnp.dot(code_delta.T, active, preferred_element_type=jnp.float32)
        value_total = value_total + jnp.dot(active.T, value_delta, preferred_element_type=jnp.float32)
        proj_total = proj_total + jnp.dot(trunk_cols, pre_grad, preferred_element_type=jnp.float32)
        trunk_grad = jnp.dot(proj_weight, pre_grad.T, preferred_element_type=jnp.float32).astype(jnp.bfloat16)
        return (proj_total, code_total, value_total), trunk_grad

    initial = (jnp.zeros((WIDTH, CODE_DIM), jnp.float32), jnp.zeros((CODES, CODE_DIM), jnp.float32), jnp.zeros((CODE_DIM, BINS), jnp.float32))
    totals, trunk_grads = lax.scan(block_step, initial, (trunk_blocks, pre_blocks, code_blocks, bin_blocks, frac_blocks))
    return trunk_grads.transpose(1, 0, 2).reshape(WIDTH, POSITIONS), totals[0], totals[1], totals[2]
```

```python
import jax
import jax.numpy as jnp
from jax import lax
from jax.experimental import pallas as pl
from jax.experimental.pallas import tpu as pltpu
from jax.sharding import PartitionSpec as P

MESH = pl.DeviceIdType.MESH
BF16 = jnp.bfloat16
F32 = jnp.float32
CORES = 2
PLANES = 4


class Place:
    def __init__(self, nb, nf):
        self.nb, self.nz = nb, PLANES
        self.nx = nf // (PLANES * CORES)
        f = lax.axis_index("fsdp")
        self.b = lax.axis_index("batch")
        self.z = f // (self.nx * CORES)
        self.x = (f // CORES) % self.nx
        self.c = f % CORES

    def dev(self, b=None, z=None, x=None, c=None):
        b = self.b if b is None else b
        z = self.z if z is None else z
        x = self.x if x is None else x
        c = self.c if c is None else c
        return (b, (z * self.nx + x) * CORES + c)

    def zz(self, d):
        return lax.rem(self.z + d + self.nz, self.nz)

    def xx(self, d):
        return lax.rem(self.x + d + self.nx, self.nx)

    def bb(self, d):
        return lax.rem(self.b + d + self.nb, self.nb)

    def barrier(self):
        sem = pltpu.get_barrier_semaphore()
        peers = [self.dev(z=self.zz(d)) for d in range(1, self.nz)]
        peers += [self.dev(x=self.xx(d)) for d in range(1, self.nx)]
        peers += [self.dev(b=self.bb(d)) for d in range(1, self.nb)]
        peers += [self.dev(c=1 - self.c)]
        for peer in peers:
            pl.semaphore_signal(sem, inc=1, device_id=peer, device_id_type=MESH)
        pl.semaphore_wait(sem, len(peers))


def steps(nz):
    return [(way, far) for far in range(1, nz) for way in (1, -1)]


class Sends:
    def __init__(self, send_sem, recv_sem, keys, place):
        self.send_sem, self.recv_sem, self.place = send_sem, recv_sem, place
        self.at = {k: i for i, k in enumerate(keys)}
        self.like = {}
        self.started = []
        self.when = ()

    def make(self, key, src, dst, dev):
        i = self.at[key]
        return pltpu.make_async_remote_copy(
            src_ref=src,
            dst_ref=dst,
            send_sem=self.send_sem.at[i],
            recv_sem=self.recv_sem.at[i],
            device_id=dev,
            device_id_type=MESH,
        )

    def go(self, key, src, dst, dev, like=None):
        self.make(key, src, dst, dev).start()
        self.like[key] = dst if like is None else like
        self.started.append((key, self.when))

    def waiter(self, key):
        ref = self.like[key]
        ref = ref() if callable(ref) else ref
        return self.make(key, ref, ref, self.place.dev(c=1 - self.place.c))

    def arrived(self, key):
        self.waiter(key).wait_recv()

    def finish(self):
        for key, whens in self.started:

            def wait(key=key):
                self.waiter(key).wait_send()

            if whens:
                met = whens[0]()
                for when in whens[1:]:
                    met = jnp.logical_and(met, when())
                pl.when(met)(wait)
            else:
                wait()

    def only(self, when):
        def run(f):
            outer = self.when
            self.when = outer + (when,)

            @pl.when(when())
            def _():
                f()

            self.when = outer

        return run


def call(kernel, outs, scratch, cid, *args):
    return pl.pallas_call(
        kernel,
        out_shape=outs,
        in_specs=[pl.BlockSpec(memory_space=pltpu.VMEM)] * len(args),
        out_specs=[pl.BlockSpec(memory_space=pltpu.VMEM)] * len(outs),
        scratch_shapes=scratch,
        compiler_params=pltpu.CompilerParams(collective_id=cid, has_side_effects=True),
    )(*args)


def has(p, way, far):
    return p.z >= far if way == 1 else p.z + far < p.nz


def feeds(p, way):
    return p.z + 1 < p.nz if way == 1 else p.z >= 1


def gather_weights_keys(nb, nx, nz):
    keys = []
    for a in (0, 1):
        keys += [(a, "c", 0)]
        for hop in [(0, 0)] + steps(nz):
            if hop[1]:
                keys += [(a, "z", hop), (a, "cz", hop)]
                for dy in range(1, nb):
                    keys += [(a, "y", hop, dy), (a, "cy", hop, dy)]
            for dx in range(1, nx):
                keys += [(a, "x", hop, dx), (a, "cx", hop, dx)]
                for dy in range(1, nb):
                    keys += [(a, "d", hop, dx, dy), (a, "cd", hop, dx, dy)]
    return keys


def gather_weights(nb, nf, codebook, value_weight):
    nz, nx = PLANES, nf // (PLANES * CORES)
    keys = gather_weights_keys(nb, nx, nz)
    rows, width = codebook.shape
    vrows, bins = value_weight.shape

    def kernel(cb, vw, cb_out, vw_out, send_sem, recv_sem):
        p = Place(nb, nf)
        p.barrier()
        s = Sends(send_sem, recv_sem, keys, p)
        arrays = ((0, cb, cb_out), (1, vw, vw_out))

        def spot(out, z, x, h):
            return out.at[z, x, p.c, h]

        def relay(key, out, at_z, at_x, at_h, **to):
            ref = spot(out, at_z, at_x, at_h)
            s.go(key, ref, ref, p.dev(**to), lambda: out.at[0, 0, 0, 0])

        for a, own, out in arrays:
            here = spot(out, p.z, p.x, p.b)
            for way in (1, -1):

                @s.only(lambda way=way: feeds(p, way))
                def _(a=a, own=own, out=out, here=here, way=way):
                    s.go((a, "z", (way, 1)), own.at[p.b], here, p.dev(z=p.z + way), lambda: out.at[0, 0, 0, 0])

            for dx in range(1, nx):
                s.go((a, "x", (0, 0), dx), own.at[p.b], here, p.dev(x=p.xx(dx)))
            s.go((a, "c", 0), own, out.at[p.z, p.x, p.c], p.dev(c=1 - p.c))
        for a, own, out in arrays:
            out[p.z, p.x, p.c] = own[...]

        def from_z(hop):
            way, far = hop
            z = p.z - way * far
            for a, own, out in arrays:
                s.arrived((a, "z", hop))
                if far + 1 < nz:

                    @s.only(lambda way=way: feeds(p, way))
                    def _(a=a, out=out):
                        relay((a, "z", (way, far + 1)), out, z, p.x, p.b, z=p.z + way)

                for dx in range(1, nx):
                    relay((a, "x", hop, dx), out, z, p.x, p.b, x=p.xx(dx))
                for dy in range(1, nb):
                    relay((a, "y", hop, dy), out, z, p.x, p.b, b=p.bb(dy))
                relay((a, "cz", hop), out, z, p.x, p.b, c=1 - p.c)

        def from_plane(hop):
            way, far = hop
            z = p.z - way * far
            for a, own, out in arrays:
                for dx in range(1, nx):
                    x = p.xx(-dx)
                    s.arrived((a, "x", hop, dx))
                    if far % 2 == 0:
                        for dy in range(1, nb):
                            relay((a, "d", hop, dx, dy), out, z, x, p.b, b=p.bb(dy))
                    relay((a, "cx", hop, dx), out, z, x, p.b, c=1 - p.c)
                if far:
                    for dy in range(1, nb):
                        h = p.bb(-dy)
                        s.arrived((a, "y", hop, dy))
                        if far % 2:
                            for dx in range(1, nx):
                                relay((a, "d", hop, dx, dy), out, z, p.x, h, x=p.xx(dx))
                        relay((a, "cy", hop, dy), out, z, p.x, h, c=1 - p.c)

        def from_diagonal(hop):
            way, far = hop
            for a, own, out in arrays:
                for dx in range(1, nx):
                    for dy in range(1, nb):
                        s.arrived((a, "d", hop, dx, dy))
                        relay(
                            (a, "cd", hop, dx, dy),
                            out,
                            p.z - way * far,
                            p.xx(-dx),
                            p.bb(-dy),
                            c=1 - p.c,
                        )

        def from_core(hop):
            for key in keys:
                if key[1] in ("cz", "cx", "cy", "cd") and key[2] == hop:
                    s.arrived(key)

        def under(hop, f):
            if hop[1]:
                s.only(lambda: has(p, *hop))(lambda: f(hop))
            else:
                f(hop)

        hops = [(0, 0)] + steps(nz)
        by_far = [[h for h in hops if h[1] == far] for far in range(nz)]
        for far in range(nz + 2):
            if 1 <= far < nz:
                for hop in by_far[far]:
                    under(hop, from_z)
            if 1 <= far <= nz:
                for hop in by_far[far - 1]:
                    under(hop, from_plane)
            if far >= 2:
                for hop in by_far[far - 2]:
                    under(hop, from_diagonal)
        for a in (0, 1):
            s.arrived((a, "c", 0))
        for hop in hops:
            under(hop, from_core)
        s.finish()

    cb_out, vw_out = call(
        kernel,
        [
            jax.ShapeDtypeStruct((nz, nx, CORES, nb, rows // nb, width), BF16),
            jax.ShapeDtypeStruct((nz, nx, CORES, nb, vrows // nb, bins), BF16),
        ],
        [pltpu.SemaphoreType.DMA((len(keys),)), pltpu.SemaphoreType.DMA((len(keys),))],
        1,
        codebook.reshape(nb, rows // nb, width),
        value_weight.reshape(nb, vrows // nb, bins),
    )
    return cb_out.reshape(nf * rows, width), vw_out.reshape(nf * vrows, bins)


def gather_grads(nb, nf, pre_grad, active, delta_t, value_delta):
    nz, nx = PLANES, nf // (PLANES * CORES)
    rows, width = pre_grad.shape
    bins = value_delta.shape[1]
    half = delta_t.shape[1]
    hops = [(0, 0)] + steps(nz)
    keys = [("c", 0)]
    for hop in hops:
        if hop[1]:
            keys += [("z", hop), ("cz", hop)]
        for dx in range(1, nx):
            keys += [("x", hop, dx), ("cx", hop, dx)]
    keys += [(k, dy) for dy in range(1, nb) for k in ("act", "delta", "value")]

    def kernel(pg, act, dt, vd, pg_out, act_out, dt_out, vd_out, send_sem, recv_sem):
        p = Place(nb, nf)
        p.barrier()
        s = Sends(send_sem, recv_sem, keys, p)
        here, like = pg_out.at[p.z, p.x, p.c], pg_out.at[0, 0, 0]
        mine = pl.ds(pl.multiple_of(p.b * rows, rows), rows)
        for way in (1, -1):

            @s.only(lambda way=way: feeds(p, way))
            def _(way=way):
                s.go(("z", (way, 1)), pg, here, p.dev(z=p.z + way), like)

        for dx in range(1, nx):
            s.go(("x", (0, 0), dx), pg, here, p.dev(x=p.xx(dx)))
        for dy in range(1, nb):
            to = p.bb(dy)
            s.go(("act", dy), act, act_out.at[p.b], p.dev(b=to))
            s.go(("delta", dy), dt.at[to], dt_out.at[:, mine], p.dev(b=to))
            s.go(("value", dy), vd, vd_out.at[p.b], p.dev(b=to))
        s.go(("c", 0), pg, here, p.dev(c=1 - p.c))
        pg_out[p.z, p.x, p.c] = pg[...]
        act_out[p.b] = act[...]
        dt_out[:, mine] = dt[p.b]
        vd_out[p.b] = vd[...]

        def from_z(hop):
            way, far = hop
            ref = pg_out.at[p.z - way * far, p.x, p.c]
            s.arrived(("z", hop))
            if far + 1 < nz:

                @s.only(lambda way=way: feeds(p, way))
                def _():
                    s.go(("z", (way, far + 1)), ref, ref, p.dev(z=p.z + way), like)

            for dx in range(1, nx):
                s.go(("x", hop, dx), ref, ref, p.dev(x=p.xx(dx)), like)
            s.go(("cz", hop), ref, ref, p.dev(c=1 - p.c), like)

        def from_plane(hop):
            way, far = hop
            for dx in range(1, nx):
                s.arrived(("x", hop, dx))
                ref = pg_out.at[p.z - way * far, p.xx(-dx), p.c]
                s.go(("cx", hop, dx), ref, ref, p.dev(c=1 - p.c), like)

        def from_core(hop):
            for key in keys:
                if key[0] in ("cz", "cx") and key[1] == hop:
                    s.arrived(key)

        def under(hop, f):
            if hop[1]:
                s.only(lambda: has(p, *hop))(lambda: f(hop))
            else:
                f(hop)

        for far in range(nz + 1):
            for hop in hops:
                if far and hop[1] == far:
                    under(hop, from_z)
            for hop in hops:
                if hop[1] == far - 1:
                    under(hop, from_plane)
        for key in keys:
            if key[0] in ("act", "delta", "value", "c"):
                s.arrived(key)
        for hop in hops:
            under(hop, from_core)
        s.finish()

    pieces, act_all, dt_all, vd_all = call(
        kernel,
        [
            jax.ShapeDtypeStruct((nz, nx, CORES, rows, width), BF16),
            jax.ShapeDtypeStruct((nb, rows, width), BF16),
            jax.ShapeDtypeStruct((half, nb * rows), BF16),
            jax.ShapeDtypeStruct((nb, rows, bins), BF16),
        ],
        [pltpu.SemaphoreType.DMA((len(keys),)), pltpu.SemaphoreType.DMA((len(keys),))],
        2,
        pre_grad,
        active,
        delta_t,
        value_delta,
    )
    return (
        pieces.reshape(nf * rows, width),
        act_all.reshape(nb * rows, width),
        dt_all,
        vd_all.reshape(nb * rows, bins),
    )


def reduce_grads(nb, nf, trunk, proj_weight, pieces, code, value):
    nz, nx = PLANES, nf // (PLANES * CORES)
    depth = trunk.shape[0]
    width = pieces.shape[1]
    block = next(n for n in (192, 96, 64, 32, 16) if depth % n == 0)
    blocks = depth // block
    lanes = 256
    cuts = 2 if code.shape[3] % 32 == 0 else 1
    crows = code.shape[3] // cuts
    fused = len(value) == 2
    bins = value[-1].shape[-1]
    vrows = width // (nf * nb) if fused else value[0].shape[4]
    chunks = range(cuts + 1)
    keys = [("p", i, dy) for i in range(blocks) for dy in range(1, nb)]
    for a in chunks:
        keys += [(a, "c")] + [(a, "x", d) for d in range(1, nx)]
        keys += [(a, "z", d) for d in range(1, nz)] + [(a, "y", d) for d in range(1, nb)]

    def kernel(tr, pw, pg, cd, *rest):
        factors, rest = rest[: len(value)], rest[len(value) :]
        (tr_out, pj_out, cd_out, vl_out), rest = rest[:4], rest[4:]
        send_sem, recv_sem = rest[-2:]
        vl = rest[-3] if fused else factors[0]
        p = Place(nb, nf)
        p.barrier()
        s = Sends(send_sem, recv_sem, keys, p)
        arrays = []
        for a in chunks:
            if a < cuts:
                part = pl.ds(a * crows, crows)
                own, out = cd.at[:, :, :, part], cd_out.at[:, part]
            else:
                own, out = vl.at[:, :, :, p.b], vl_out
            arrays.append((a, own, out) + tuple(rest[6 * a : 6 * a + 6]))
        for a, own, out, core, *_ in arrays:
            if a == cuts and fused:
                product = lax.dot_general(
                    factors[0][...],
                    factors[1][...],
                    (((0,), (0,)), ((), ())),
                    preferred_element_type=F32,
                )
                vl[...] = product.astype(BF16).reshape(nz, nx, CORES, nb, vrows, bins)
            s.go((a, "c"), own.at[:, :, 1 - p.c], core, p.dev(c=1 - p.c))

        def multiply(i):
            rows = pl.ds(i * block, block)

            def tile(n, carry):
                cols = pl.ds(pl.multiple_of(n * lanes, lanes), lanes)
                pj_out[p.b, rows, cols] = jnp.dot(
                    tr[rows, :], pg[:, cols], preferred_element_type=F32
                ).astype(BF16)
                return carry

            lax.fori_loop(0, width // lanes, tile, 0)
            for dy in range(1, nb):
                ref = pj_out.at[p.b, rows]
                s.go(("p", i, dy), ref, ref, p.dev(b=p.bb(dy)))

        def columns(n, carry):
            cols = pl.ds(pl.multiple_of(n * lanes, lanes), lanes)
            tr_out[:, cols] = lax.dot_general(
                pw[...], pg[cols, :], (((1,), (1,)), ((), ())), preferred_element_type=F32
            ).astype(BF16)
            return carry

        multiply(0)
        for a, own, out, core, xin, xsend, acc, zin, zsend in arrays:
            s.arrived((a, "c"))
            for dx in range(1, nx):
                x = p.xx(dx)
                for z in range(nz):
                    both = own[z, x, p.c].astype(F32) + core[z, x].astype(F32)
                    xsend[dx - 1, z] = both.astype(BF16)
                s.go((a, "x", dx), xsend.at[dx - 1], xin.at[dx - 1], p.dev(x=x))
            for z in range(nz):
                acc[z] = own[z, p.x, p.c].astype(F32) + core[z, p.x].astype(F32)
        for i in range(1, blocks):
            multiply(i)
        for a, own, out, core, xin, xsend, acc, zin, zsend in arrays:
            for dx in range(1, nx):
                s.arrived((a, "x", dx))
                acc[...] += xin[dx - 1].astype(F32)
            for dz in [2, 1, 3]:
                z = p.zz(dz)
                zsend[dz - 1] = acc[z].astype(BF16)
                s.go((a, "z", dz), zsend.at[dz - 1], zin.at[dz - 1], p.dev(z=z))
        for a, own, out, core, xin, xsend, acc, zin, zsend in arrays:
            if a == 0:
                lax.fori_loop(0, pieces.shape[0] // lanes, columns, 0)
            total = acc[p.z]
            for dz in range(1, nz):
                s.arrived((a, "z", dz))
                total = total + zin[dz - 1].astype(F32)
            out[p.b] = total.astype(BF16)
            for dy in range(1, nb):
                s.go((a, "y", dy), out.at[p.b], out.at[p.b], p.dev(b=p.bb(dy)))
        for key in keys:
            if key[0] == "p" or key[1] == "y":
                s.arrived(key)
        s.finish()

    def buffers(r, k):
        return [
            pltpu.VMEM((nz, nx, r, k), BF16),
            pltpu.VMEM((max(nx - 1, 1), nz, r, k), BF16),
            pltpu.VMEM((max(nx - 1, 1), nz, r, k), BF16),
            pltpu.VMEM((nz, r, k), F32),
            pltpu.VMEM((nz - 1, r, k), BF16),
            pltpu.VMEM((nz - 1, r, k), BF16),
        ]

    return call(
        kernel,
        [
            jax.ShapeDtypeStruct((depth, pieces.shape[0]), BF16),
            jax.ShapeDtypeStruct((nb, depth, width), BF16),
            jax.ShapeDtypeStruct((nb, crows * cuts, width), BF16),
            jax.ShapeDtypeStruct((nb, vrows, bins), BF16),
        ],
        buffers(crows, width) * cuts
        + buffers(vrows, bins)
        + [pltpu.VMEM((nz, nx, CORES, nb, vrows, bins), BF16)] * fused
        + [pltpu.SemaphoreType.DMA((len(keys),)), pltpu.SemaphoreType.DMA((len(keys),))],
        3,
        trunk,
        proj_weight,
        pieces,
        code,
        *value,
    )


def dot(a, b, dims):
    return lax.dot_general(a, b, (dims, ((), ())), preferred_element_type=F32)


def fits(nb, nf, codebook, value_weight, depth):
    nx = nf // (PLANES * CORES)
    rows, width = codebook.shape
    vrows = value_weight.shape[0]
    half, vhalf = rows // nb, vrows // nb
    plane = nx * CORES
    return (
        half * nb == rows
        and vhalf * nb == vrows
        and half % 64 == 0
        and vhalf % 32 == 0
        and (plane * rows) % 256 == 0
        and (plane * vrows) % 256 == 0
        and width % 256 == 0
        and depth % 192 == 0
    )


def fused(nb, nf, trunk, pre_act, proj_weight, codebook, value_weight, target, low, frac):
    nz, nx = PLANES, nf // (PLANES * CORES)
    pos, width = pre_act.shape
    rows, vrows = codebook.shape[0], value_weight.shape[0]
    bins = value_weight.shape[1]
    depth, total_pos = trunk.shape
    codes = nf * rows
    half, vhalf = rows // nb, vrows // nb
    plane_codes, plane_rows = nx * CORES * rows, nx * CORES * vrows
    cw = 256
    pieces = width // cw
    cuts = 2
    ck = half // cuts
    hops = [(0, 0)] + steps(nz)
    by_far = [[h for h in hops if h[1] == far] for far in range(nz)]

    keys = []
    for a in range(3):
        keys += [("w", a, "c")]
        for hop in hops:
            if hop[1]:
                keys += [("w", a, "z", hop), ("w", a, "cz", hop)]
                for dy in range(1, nb):
                    keys += [("w", a, "y", hop, dy), ("w", a, "cy", hop, dy)]
            for dx in range(1, nx):
                keys += [("w", a, "x", hop, dx), ("w", a, "cx", hop, dx)]
                for dy in range(1, nb):
                    keys += [("w", a, "d", hop, dx, dy), ("w", a, "cd", hop, dx, dy)]
    for n in range(pieces):
        keys += [("g", n, "c")]
        for hop in hops:
            if hop[1]:
                keys += [("g", n, "z", hop), ("g", n, "cz", hop)]
            for dx in range(1, nx):
                keys += [("g", n, "x", hop, dx), ("g", n, "cx", hop, dx)]
    keys += [(k, dy) for dy in range(1, nb) for k in ("act", "delta", "value")]
    for a in range(cuts + 1):
        keys += [("r", a, "c")] + [("r", a, "x", d) for d in range(1, nx)]
        keys += [("r", a, "z", d) for d in range(1, nz)] + [("r", a, "y", d) for d in range(1, nb)]
    keys += [("p", n, dy) for n in range(pieces) for dy in range(1, nb)]

    def kernel(
        pre,
        cb,
        vw,
        tgt,
        lo,
        fr,
        tr_in,
        pw_in,
        tr_out,
        pj_out,
        cd_out,
        vl_out,
        tr,
        pw,
        cb_all,
        vw_all,
        gate,
        act_all,
        logit,
        top,
        vlog,
        delta,
        delta_t,
        vd_all,
        dt_all,
        pg,
        part,
        vpart,
        trg,
        pj_all,
        pj,
        cd_all,
        cd,
        vl_all,
        vl,
        *rest,
    ):
        local_sem, send_sem, recv_sem = rest[-3:]
        p = Place(nb, nf)
        loads = [
            pltpu.make_async_copy(tr_in, tr, local_sem.at[0]),
            pltpu.make_async_copy(pw_in, pw, local_sem.at[1]),
        ]
        for load in loads:
            load.start()
        p.barrier()
        s = Sends(send_sem, recv_sem, keys, p)

        def under(hop, f):
            if hop[1]:
                s.only(lambda: has(p, *hop))(lambda: f(hop))
            else:
                f(hop)

        def index(z, x, c):
            return (z * nx + x) * CORES + c

        sub = half // 2
        shards = (
            (0, vw, vw_all, vrows, vhalf, 0, vhalf),
            (1, cb, cb_all, rows, half, 0, sub),
            (2, cb, cb_all, rows, half, sub, sub),
        )

        def spot(shard, z, x, c, h):
            a, own, out, per, piece, skip, size = shard
            return out.at[pl.ds(pl.multiple_of(index(z, x, c) * per + h * piece + skip, size), size)]

        def mine(shard, h):
            a, own, out, per, piece, skip, size = shard
            return own.at[pl.ds(pl.multiple_of(h * piece + skip, size), size)]

        def whole(shard):
            a, own, out, per, piece, skip, size = shard
            return out.at[pl.ds(0, size)]

        def relay(key, shard, at_z, at_x, at_h, **to):
            ref = spot(shard, at_z, at_x, p.c, at_h)
            s.go(key, ref, ref, p.dev(**to), whole(shard))

        for shard in shards:
            a = shard[0]
            here = spot(shard, p.z, p.x, p.c, p.b)
            for way in (1, -1):

                @s.only(lambda way=way: feeds(p, way))
                def _(a=a, shard=shard, here=here, way=way):
                    s.go(
                        ("w", a, "z", (way, 1)), mine(shard, p.b), here, p.dev(z=p.z + way), whole(shard)
                    )

            for dx in range(1, nx):
                s.go(("w", a, "x", (0, 0), dx), mine(shard, p.b), here, p.dev(x=p.xx(dx)), whole(shard))
        own_rows = pl.ds(pl.multiple_of(index(p.z, p.x, p.c) * rows, rows), rows)
        own_vrows = pl.ds(pl.multiple_of(index(p.z, p.x, p.c) * vrows, vrows), vrows)
        s.go(("w", 0, "c"), vw, vw_all.at[own_vrows], p.dev(c=1 - p.c))
        s.go(("w", 1, "c"), cb, cb_all.at[own_rows], p.dev(c=1 - p.c))
        cb_all[own_rows, :] = cb[...]
        vw_all[own_vrows, :] = vw[...]

        def activate(i, carry):
            cols = pl.ds(pl.multiple_of(i * cw, cw), cw)
            v = pre[:, cols].astype(F32)
            sigma = jax.nn.sigmoid(v)
            act_all[p.b, :, cols] = (v * sigma).astype(BF16)
            gate[:, cols] = sigma * (1.0 + v * (1.0 - sigma))
            return carry

        lax.fori_loop(0, width // cw, activate, 0)
        top[...] = jnp.full(top.shape, -jnp.inf, F32)
        vlog[...] = jnp.zeros(vlog.shape, F32)

        def from_z(shard, hop):
            a = shard[0]
            way, far = hop
            z = p.z - way * far
            s.arrived(("w", a, "z", hop))
            if far + 1 < nz:

                @s.only(lambda way=way: feeds(p, way))
                def _():
                    relay(("w", a, "z", (way, far + 1)), shard, z, p.x, p.b, z=p.z + way)

            for dx in range(1, nx):
                relay(("w", a, "x", hop, dx), shard, z, p.x, p.b, x=p.xx(dx))
            for dy in range(1, nb):
                relay(("w", a, "y", hop, dy), shard, z, p.x, p.b, b=p.bb(dy))
            relay(("w", a, "cz", hop), shard, z, p.x, p.b, c=1 - p.c)

        def from_plane(shard, hop):
            a = shard[0]
            way, far = hop
            z = p.z - way * far
            for dx in range(1, nx):
                x = p.xx(-dx)
                s.arrived(("w", a, "x", hop, dx))
                if far % 2 == 0:
                    for dy in range(1, nb):
                        relay(("w", a, "d", hop, dx, dy), shard, z, x, p.b, b=p.bb(dy))
                relay(("w", a, "cx", hop, dx), shard, z, x, p.b, c=1 - p.c)
            if far:
                for dy in range(1, nb):
                    h = p.bb(-dy)
                    s.arrived(("w", a, "y", hop, dy))
                    if far % 2:
                        for dx in range(1, nx):
                            relay(("w", a, "d", hop, dx, dy), shard, z, p.x, h, x=p.xx(dx))
                    relay(("w", a, "cy", hop, dy), shard, z, p.x, h, c=1 - p.c)

        def from_diagonal(shard, hop):
            a = shard[0]
            way, far = hop
            for dx in range(1, nx):
                for dy in range(1, nb):
                    s.arrived(("w", a, "d", hop, dx, dy))
                    relay(
                        ("w", a, "cd", hop, dx, dy),
                        shard,
                        p.z - way * far,
                        p.xx(-dx),
                        p.bb(-dy),
                        c=1 - p.c,
                    )

        def from_core(hop):
            for key in keys:
                if key[0] == "w" and key[2] in ("cz", "cx", "cy", "cd") and key[3] == hop:
                    s.arrived(key)

        def near(j):
            up = (0, 1, 2, 3)[j], (1, 0, 2, 3)[j], (2, 3, 1, 0)[j], (3, 2, 1, 0)[j]
            z = jnp.where(p.z == 0, up[0], up[3])
            z = jnp.where(p.z == 1, up[1], z)
            return jnp.where(p.z == 2, up[2], z)

        def score(j):
            z = near(j)

            def tile(i, carry):
                at = pl.ds(pl.multiple_of(z * plane_codes + i * 256, 256), 256)
                block = dot(cb_all[at, :], act_all[p.b], ((1,), (1,)))
                logit[at, :] = block
                top[...] = jnp.maximum(top[...], jnp.max(block, axis=0, keepdims=True))
                return carry

            lax.fori_loop(0, plane_codes // 256, tile, 0)
            at = pl.ds(pl.multiple_of(z * plane_rows, plane_rows), plane_rows)
            vlog[...] += dot(act_all[p.b, :, at], vw_all[at, :], ((1,), (0,)))

        for far in range(nz + 2):
            for shard in shards:
                if 1 <= far < nz:
                    for hop in by_far[far]:
                        under(hop, lambda hop: from_z(shard, hop))
                if 1 <= far <= nz:
                    for hop in by_far[far - 1]:
                        under(hop, lambda hop: from_plane(shard, hop))
                if far >= 2:
                    for hop in by_far[far - 2]:
                        under(hop, lambda hop: from_diagonal(shard, hop))
            if far == nz:
                for dy in range(1, nb):
                    ref = act_all.at[p.b]
                    s.go(("act", dy), ref, ref, p.dev(b=p.bb(dy)))
            if far >= 2:
                if far == 2:
                    for a in (0, 1):
                        s.arrived(("w", a, "c"))
                for hop in by_far[far - 2]:
                    under(hop, from_core)
                score(far - 2)

        high = jnp.max(vlog[...], axis=1, keepdims=True)
        grown = jnp.exp(vlog[...] - high)
        probs = grown * (1.0 / jnp.sum(grown, axis=1, keepdims=True))
        ids = lax.broadcasted_iota(jnp.int32, (pos, bins), 1).astype(F32)
        column = jnp.broadcast_to(lo[...].astype(F32), (pos, pos)).T[:, :1]
        share = jnp.broadcast_to(fr[...].astype(F32) / 1024.0, (pos, pos)).T[:, :1]
        want = jnp.where(ids == column, 1.0 - share, 0.0)
        want = want + jnp.where(ids == column + 1.0, share, 0.0)
        vd_all[p.b] = (probs - want).astype(BF16)
        for dy in range(1, nb):
            ref = vd_all.at[p.b]
            s.go(("value", dy), ref, ref, p.dev(b=p.bb(dy)))

        blocks = codes // 256
        best = top[...]

        def grow(i, total):
            at = pl.ds(pl.multiple_of(i * 256, 256), 256)
            e = jnp.exp(logit[at, :] - best)
            logit[at, :] = e
            return total + jnp.sum(e, axis=0, keepdims=True)

        scale = 1.0 / lax.fori_loop(0, blocks, grow, jnp.zeros((1, pos), F32))
        group = 256 // rows
        code_ids = lax.broadcasted_iota(jnp.int32, (256, pos), 0)

        def differ(i, carry):
            at = pl.ds(pl.multiple_of(i * 256, 256), 256)
            hot = jnp.where(code_ids + i * 256 == tgt[...], 1.0, 0.0)
            d = logit[at, :] * scale - hot
            delta[:, at] = d.T.astype(BF16)
            delta_t[pl.ds(i * group, group)] = d.astype(BF16).reshape(group, nb, half, pos)
            return carry

        lax.fori_loop(0, blocks, differ, 0)
        lanes = pl.ds(pl.multiple_of(p.b * pos, pos), pos)
        for dy in range(1, nb):
            to = p.bb(dy)
            s.go(("delta", dy), delta_t.at[:, to], dt_all.at[:, :, lanes], p.dev(b=to))

        own_pos = pl.ds(pl.multiple_of(index(p.z, p.x, p.c) * pos, pos), pos)
        like = [pg.at[n, pl.ds(0, pos)] for n in range(pieces)]
        for n in range(pieces):
            cols = pl.ds(n * cw, cw)
            back = dot(delta[...], cb_all[:, cols], ((1,), (0,)))
            back = back + dot(vd_all[p.b], vw_all[cols, :], ((1,), (1,)))
            pg[n, own_pos, :] = (back * gate[:, cols]).astype(BF16)
            here = pg.at[n, own_pos]
            for way in (1, -1):

                @s.only(lambda way=way: feeds(p, way))
                def _(way=way):
                    s.go(("g", n, "z", (way, 1)), here, here, p.dev(z=p.z + way), like[n])

            for dx in range(1, nx):
                s.go(("g", n, "x", (0, 0), dx), here, here, p.dev(x=p.xx(dx)), like[n])
            s.go(("g", n, "c"), here, here, p.dev(c=1 - p.c), like[n])
        dt_all[:, :, lanes] = delta_t[:, p.b]

        def there(n, z, x):
            return pg.at[n, pl.ds(pl.multiple_of(index(z, x, p.c) * pos, pos), pos)]

        def grad_z(n, hop):
            way, far = hop
            ref = there(n, p.z - way * far, p.x)
            s.arrived(("g", n, "z", hop))
            if far + 1 < nz:

                @s.only(lambda way=way: feeds(p, way))
                def _():
                    s.go(("g", n, "z", (way, far + 1)), ref, ref, p.dev(z=p.z + way), like[n])

            for dx in range(1, nx):
                s.go(("g", n, "x", hop, dx), ref, ref, p.dev(x=p.xx(dx)), like[n])
            s.go(("g", n, "cz", hop), ref, ref, p.dev(c=1 - p.c), like[n])

        def grad_plane(n, hop):
            way, far = hop
            for dx in range(1, nx):
                s.arrived(("g", n, "x", hop, dx))
                ref = there(n, p.z - way * far, p.xx(-dx))
                s.go(("g", n, "cx", hop, dx), ref, ref, p.dev(c=1 - p.c), like[n])

        def grad_core(n, hop):
            for key in keys:
                if key[0] == "g" and key[1] == n and key[2] in ("cz", "cx") and key[3] == hop:
                    s.arrived(key)

        def stage_z(far):
            for n in range(pieces):
                for hop in by_far[far]:
                    under(hop, lambda hop: grad_z(n, hop))

        def stage_plane(far):
            for n in range(pieces):
                for hop in by_far[far]:
                    under(hop, lambda hop: grad_plane(n, hop))

        stage_z(1)

        arrays = []
        for a in range(cuts + 1):
            if a < cuts:
                own, out = part.at[:, :, :, pl.ds(a * ck, ck)], cd_all.at[:, pl.ds(a * ck, ck)]
            else:
                own, out = vpart.at[:, :, :, p.b], vl_all
            arrays.append((a, own, out) + tuple(rest[6 * a : 6 * a + 6]))
        for key in keys:
            if key[0] in ("act", "delta"):
                s.arrived(key)
        deep = nb * pos

        def share_codes(i, carry):
            z = i // (width // cw)
            cols = pl.ds(pl.multiple_of((i % (width // cw)) * cw, cw), cw)
            left = dt_all[pl.ds(z * nx * CORES, nx * CORES)].reshape(nx * CORES * half, deep)
            right = act_all[:, :, cols].reshape(deep, cw)
            block = dot(left, right, ((1,), (0,)))
            part[z, :, :, :, cols] = block.astype(BF16).reshape(nx, CORES, half, cw)
            return carry

        lax.fori_loop(0, nz * (width // cw), share_codes, 0)
        for a, own, out, core, *_ in arrays[:cuts]:
            s.go(("r", a, "c"), own.at[:, :, 1 - p.c], core, p.dev(c=1 - p.c))
        for key in keys:
            if key[0] == "value":
                s.arrived(key)

        def share_values(z, carry):
            cols = pl.ds(pl.multiple_of(z * plane_rows, plane_rows), plane_rows)
            left = act_all[:, :, cols].reshape(deep, plane_rows)
            block = dot(left, vd_all[...].reshape(deep, bins), ((0,), (0,)))
            vpart[z] = block.astype(BF16).reshape(nx, CORES, nb, vhalf, bins)
            return carry

        lax.fori_loop(0, nz, share_values, 0)
        for a, own, out, core, *_ in arrays[cuts:]:
            s.go(("r", a, "c"), own.at[:, :, 1 - p.c], core, p.dev(c=1 - p.c))

        stage_plane(0)
        stage_z(2)
        stage_plane(1)
        for a, own, out, core, xin, xsend, acc, zin, zsend in arrays:
            s.arrived(("r", a, "c"))
            for dx in range(1, nx):
                x = p.xx(dx)
                for z in range(nz):
                    both = own[z, x, p.c].astype(F32) + core[z, x].astype(F32)
                    xsend[dx - 1, z] = both.astype(BF16)
                s.go(("r", a, "x", dx), xsend.at[dx - 1], xin.at[dx - 1], p.dev(x=x))
            for z in range(nz):
                acc[z] = own[z, p.x, p.c].astype(F32) + core[z, p.x].astype(F32)
        stage_z(3)
        stage_plane(2)
        stage_plane(3)
        for load in loads:
            load.wait()
        for n in range(pieces):
            s.arrived(("g", n, "c"))
            for hop in hops:
                under(hop, lambda hop: grad_core(n, hop))

            def project(i, carry):
                at = pl.ds(pl.multiple_of(i * 192, 192), 192)
                pj_all[p.b, n, at, :] = jnp.dot(
                    tr[at, :], pg[n], preferred_element_type=F32
                ).astype(BF16)
                return carry

            lax.fori_loop(0, depth // 192, project, 0)
            for dy in range(1, nb):
                ref = pj_all.at[p.b, n]
                s.go(("p", n, dy), ref, ref, p.dev(b=p.bb(dy)))
        for a, own, out, core, xin, xsend, acc, zin, zsend in arrays:
            for dx in range(1, nx):
                s.arrived(("r", a, "x", dx))
                acc[...] += xin[dx - 1].astype(F32)
            for dz in [2, 1, 3]:
                z = p.zz(dz)
                zsend[dz - 1] = acc[z].astype(BF16)
                s.go(("r", a, "z", dz), zsend.at[dz - 1], zin.at[dz - 1], p.dev(z=z))

        def columns(i, carry):
            at = pl.ds(pl.multiple_of(i * 256, 256), 256)
            block = dot(pw[:, pl.ds(0, cw)], pg[0, at, :], ((1,), (1,)))
            for n in range(1, pieces):
                block = block + dot(pw[:, pl.ds(n * cw, cw)], pg[n, at, :], ((1,), (1,)))
            trg[:, at] = block.astype(BF16)
            return carry

        lax.fori_loop(0, total_pos // 256, columns, 0)
        stores = [pltpu.make_async_copy(trg, tr_out, local_sem.at[0])]
        stores[0].start()
        for a, own, out, core, xin, xsend, acc, zin, zsend in arrays:
            total = acc[p.z]
            for dz in range(1, nz):
                s.arrived(("r", a, "z", dz))
                total = total + zin[dz - 1].astype(F32)
            out[p.b] = total.astype(BF16)
            for dy in range(1, nb):
                s.go(("r", a, "y", dy), out.at[p.b], out.at[p.b], p.dev(b=p.bb(dy)))
        for n in range(pieces):
            for dy in range(1, nb):
                s.arrived(("p", n, dy))
            total = pj_all[0, n].astype(F32)
            for b in range(1, nb):
                total = total + pj_all[b, n].astype(F32)
            pj[:, pl.ds(n * cw, cw)] = total
        stores.append(pltpu.make_async_copy(pj, pj_out, local_sem.at[1]))
        stores[-1].start()
        for a in range(cuts + 1):
            for dy in range(1, nb):
                s.arrived(("r", a, "y", dy))
        for b in range(nb):
            cd[pl.ds(b * half, half), :] = cd_all[b].astype(F32)
            vl[pl.ds(b * vhalf, vhalf), :] = vl_all[b].astype(F32)
        stores.append(pltpu.make_async_copy(cd, cd_out, local_sem.at[2]))
        stores[-1].start()
        stores.append(pltpu.make_async_copy(vl, vl_out, local_sem.at[3]))
        stores[-1].start()
        s.finish()
        for store in stores:
            store.wait()

    def buffers(r, k):
        return [
            pltpu.VMEM((nz, nx, r, k), BF16),
            pltpu.VMEM((max(nx - 1, 1), nz, r, k), BF16),
            pltpu.VMEM((max(nx - 1, 1), nz, r, k), BF16),
            pltpu.VMEM((nz, r, k), F32),
            pltpu.VMEM((nz - 1, r, k), BF16),
            pltpu.VMEM((nz - 1, r, k), BF16),
        ]

    vmem = pl.BlockSpec(memory_space=pltpu.VMEM)
    anywhere = pl.BlockSpec(memory_space=pl.ANY)
    return pl.pallas_call(
        kernel,
        out_shape=[
            jax.ShapeDtypeStruct((depth, total_pos), BF16),
            jax.ShapeDtypeStruct((depth, width), F32),
            jax.ShapeDtypeStruct((rows, width), F32),
            jax.ShapeDtypeStruct((vrows, bins), F32),
        ],
        in_specs=[vmem] * 6 + [anywhere] * 2,
        out_specs=[anywhere] * 4,
        scratch_shapes=[
            pltpu.VMEM((depth, total_pos), BF16),
            pltpu.VMEM((depth, width), BF16),
            pltpu.VMEM((codes, width), BF16),
            pltpu.VMEM((width, bins), BF16),
            pltpu.VMEM((pos, width), F32),
            pltpu.VMEM((nb, pos, width), BF16),
            pltpu.VMEM((codes, pos), F32),
            pltpu.VMEM((1, pos), F32),
            pltpu.VMEM((pos, bins), F32),
            pltpu.VMEM((pos, codes), BF16),
            pltpu.VMEM((nf, nb, half, pos), BF16),
            pltpu.VMEM((nb, pos, bins), BF16),
            pltpu.VMEM((nf, half, nb * pos), BF16),
            pltpu.VMEM((pieces, nf * pos, cw), BF16),
            pltpu.VMEM((nz, nx, CORES, half, width), BF16),
            pltpu.VMEM((nz, nx, CORES, nb, vhalf, bins), BF16),
            pltpu.VMEM((depth, total_pos), BF16),
            pltpu.VMEM((nb, pieces, depth, cw), BF16),
            pltpu.VMEM((depth, width), F32),
            pltpu.VMEM((nb, half, width), BF16),
            pltpu.VMEM((rows, width), F32),
            pltpu.VMEM((nb, vhalf, bins), BF16),
            pltpu.VMEM((vrows, bins), F32),
        ]
        + buffers(ck, width) * cuts
        + buffers(vhalf, bins)
        + [
            pltpu.SemaphoreType.DMA((4,)),
            pltpu.SemaphoreType.DMA((len(keys),)),
            pltpu.SemaphoreType.DMA((len(keys),)),
        ],
        compiler_params=pltpu.CompilerParams(
            collective_id=4, has_side_effects=True, vmem_limit_bytes=48 << 20
        ),
    )(pre_act, codebook, value_weight, target, low, frac, trunk, proj_weight)


def make_body(nb, nf):
    nz, nx = PLANES, nf // (PLANES * CORES)

    def body(
        trunk, pre_act, proj_weight, codebook, value_weight, code_target, value_bin, value_frac
    ):
        if fits(nb, nf, codebook, value_weight, trunk.shape[0]):
            row = (1, pre_act.shape[0])
            return fused(
                nb,
                nf,
                trunk,
                pre_act,
                proj_weight,
                codebook,
                value_weight,
                code_target.reshape(row),
                value_bin.reshape(row),
                value_frac.reshape(row),
            )
        all_codes, bins_weight = gather_weights(nb, nf, codebook, value_weight)
        rows, width = pre_act.shape
        num_codes = all_codes.shape[0]
        num_bins = bins_weight.shape[1]
        pre_value = pre_act.astype(F32)
        gate_sigma = jax.nn.sigmoid(pre_value)
        active = (pre_value * gate_sigma).astype(BF16)
        code_logits = jnp.einsum("rk,ck->rc", active, all_codes, preferred_element_type=F32)
        code_probs = jax.nn.softmax(code_logits, axis=-1)
        code_ids = lax.broadcasted_iota(jnp.int32, (1, num_codes), 1)
        one_hot = (code_target[:, None] == code_ids).astype(F32)
        code_delta = (code_probs - one_hot).astype(BF16)
        value_logits = jnp.dot(active, bins_weight, preferred_element_type=F32)
        value_probs = jax.nn.softmax(value_logits, axis=-1)
        bin_ids = lax.broadcasted_iota(jnp.int32, (1, num_bins), 1)
        fraction = value_frac.astype(F32)[:, None] / 1024.0
        target = jnp.where(bin_ids == value_bin[:, None], 1.0 - fraction, 0.0)
        target = target + jnp.where(bin_ids == value_bin[:, None] + 1, fraction, 0.0)
        value_delta = (value_probs - target).astype(BF16)
        backward = jnp.dot(code_delta, all_codes, preferred_element_type=F32)
        backward = backward + jnp.einsum(
            "rb,kb->rk", value_delta, bins_weight, preferred_element_type=F32
        )
        pre_grad = (backward * gate_sigma * (1.0 + pre_value * (1.0 - gate_sigma))).astype(BF16)
        own = codebook.shape[0] // nb
        delta_t = code_delta.T.reshape(nf, nb, own, rows).swapaxes(0, 1)
        delta_t = delta_t.reshape(nb, nf * own, rows)
        pieces, act_all, dt_all, vd_all = gather_grads(
            nb, nf, pre_grad, active, delta_t, value_delta
        )
        code_part = jnp.dot(dt_all, act_all, preferred_element_type=F32)
        code_part = code_part.astype(BF16).reshape(nz, nx, CORES, own, width)
        vown = value_weight.shape[0] // nb
        if vown % 16 == 0:
            value_part = (act_all, vd_all)
        else:
            value_part = jnp.einsum("rk,rb->kb", act_all, vd_all, preferred_element_type=F32)
            value_part = value_part.astype(BF16)
            value_part = (value_part.reshape(nz, nx, CORES, nb, vown, num_bins),)
        out_cols, proj_all, code_all, value_all = reduce_grads(
            nb, nf, trunk, proj_weight, pieces, code_part, value_part
        )
        proj_grad = jnp.sum(proj_all.astype(F32), axis=0)
        code_grad = code_all.reshape(nb * own, width).astype(F32)
        value_grad = value_all.reshape(nb * vown, num_bins).astype(F32)
        return (out_cols, proj_grad, code_grad, value_grad)

    return body


def solution(mesh):
    in_specs = (
        P("fsdp", "batch"),
        P(("batch", "fsdp"), None),
        P("fsdp", None),
        P("fsdp", None),
        P("fsdp", None),
        P(("batch", "fsdp")),
        P(("batch", "fsdp")),
        P(("batch", "fsdp")),
    )
    out_specs = (P("fsdp", "batch"), P("fsdp", None), P("fsdp", None), P("fsdp", None))
    body = make_body(mesh.shape["batch"], mesh.shape["fsdp"])
    return jax.shard_map(body, mesh=mesh, in_specs=in_specs, out_specs=out_specs, check_vma=False)
```

```python
import jax
import jax.numpy as jnp
from jax import lax
from jax.experimental import pallas as pl
from jax.experimental.pallas import tpu as pltpu
from jax.sharding import PartitionSpec as P

MESH = pl.DeviceIdType.MESH
BF16 = jnp.bfloat16
F32 = jnp.float32
CORES = 2
PLANES = 4


class Place:
    def __init__(self, nb, nf):
        self.nb, self.nz = nb, PLANES
        self.nx = nf // (PLANES * CORES)
        f = lax.axis_index("fsdp")
        self.b = lax.axis_index("batch")
        self.z = f // (self.nx * CORES)
        self.x = (f // CORES) % self.nx
        self.c = f % CORES

    def dev(self, b=None, z=None, x=None, c=None):
        b = self.b if b is None else b
        z = self.z if z is None else z
        x = self.x if x is None else x
        c = self.c if c is None else c
        return (b, (z * self.nx + x) * CORES + c)

    def zz(self, d):
        return lax.rem(self.z + d + self.nz, self.nz)

    def xx(self, d):
        return lax.rem(self.x + d + self.nx, self.nx)

    def bb(self, d):
        return lax.rem(self.b + d + self.nb, self.nb)

    def barrier(self):
        sem = pltpu.get_barrier_semaphore()
        peers = [self.dev(z=self.zz(d)) for d in range(1, self.nz)]
        peers += [self.dev(x=self.xx(d)) for d in range(1, self.nx)]
        peers += [self.dev(b=self.bb(d)) for d in range(1, self.nb)]
        peers += [self.dev(c=1 - self.c)]
        for peer in peers:
            pl.semaphore_signal(sem, inc=1, device_id=peer, device_id_type=MESH)
        pl.semaphore_wait(sem, len(peers))


def steps(nz):
    return [(way, far) for far in range(1, nz) for way in (1, -1)]


class Sends:
    def __init__(self, send_sem, recv_sem, keys, place):
        self.send_sem, self.recv_sem, self.place = send_sem, recv_sem, place
        self.at = {k: i for i, k in enumerate(keys)}
        self.like = {}
        self.started = []
        self.when = ()

    def make(self, key, src, dst, dev):
        i = self.at[key]
        return pltpu.make_async_remote_copy(
            src_ref=src,
            dst_ref=dst,
            send_sem=self.send_sem.at[i],
            recv_sem=self.recv_sem.at[i],
            device_id=dev,
            device_id_type=MESH,
        )

    def go(self, key, src, dst, dev, like=None):
        self.make(key, src, dst, dev).start()
        self.like[key] = dst if like is None else like
        self.started.append((key, self.when))

    def waiter(self, key):
        ref = self.like[key]
        ref = ref() if callable(ref) else ref
        return self.make(key, ref, ref, self.place.dev(c=1 - self.place.c))

    def arrived(self, key):
        self.waiter(key).wait_recv()

    def finish(self):
        for key, whens in self.started:

            def wait(key=key):
                self.waiter(key).wait_send()

            if whens:
                met = whens[0]()
                for when in whens[1:]:
                    met = jnp.logical_and(met, when())
                pl.when(met)(wait)
            else:
                wait()

    def only(self, when):
        def run(f):
            outer = self.when
            self.when = outer + (when,)

            @pl.when(when())
            def _():
                f()

            self.when = outer

        return run


def call(kernel, outs, scratch, cid, *args):
    return pl.pallas_call(
        kernel,
        out_shape=outs,
        in_specs=[pl.BlockSpec(memory_space=pltpu.VMEM)] * len(args),
        out_specs=[pl.BlockSpec(memory_space=pltpu.VMEM)] * len(outs),
        scratch_shapes=scratch,
        compiler_params=pltpu.CompilerParams(collective_id=cid, has_side_effects=True),
    )(*args)


def has(p, way, far):
    return p.z >= far if way == 1 else p.z + far < p.nz


def feeds(p, way):
    return p.z + 1 < p.nz if way == 1 else p.z >= 1


def gather_weights_keys(nb, nx, nz):
    keys = []
    for a in (0, 1):
        keys += [(a, "c", 0)]
        for hop in [(0, 0)] + steps(nz):
            if hop[1]:
                keys += [(a, "z", hop), (a, "cz", hop)]
                for dy in range(1, nb):
                    keys += [(a, "y", hop, dy), (a, "cy", hop, dy)]
            for dx in range(1, nx):
                keys += [(a, "x", hop, dx), (a, "cx", hop, dx)]
                for dy in range(1, nb):
                    keys += [(a, "d", hop, dx, dy), (a, "cd", hop, dx, dy)]
    return keys


def gather_weights(nb, nf, codebook, value_weight):
    nz, nx = PLANES, nf // (PLANES * CORES)
    keys = gather_weights_keys(nb, nx, nz)
    rows, width = codebook.shape
    vrows, bins = value_weight.shape

    def kernel(cb, vw, cb_out, vw_out, send_sem, recv_sem):
        p = Place(nb, nf)
        p.barrier()
        s = Sends(send_sem, recv_sem, keys, p)
        arrays = ((0, cb, cb_out), (1, vw, vw_out))

        def spot(out, z, x, h):
            return out.at[z, x, p.c, h]

        def relay(key, out, at_z, at_x, at_h, **to):
            ref = spot(out, at_z, at_x, at_h)
            s.go(key, ref, ref, p.dev(**to), lambda: out.at[0, 0, 0, 0])

        for a, own, out in arrays:
            here = spot(out, p.z, p.x, p.b)
            for way in (1, -1):

                @s.only(lambda way=way: feeds(p, way))
                def _(a=a, own=own, out=out, here=here, way=way):
                    s.go((a, "z", (way, 1)), own.at[p.b], here, p.dev(z=p.z + way), lambda: out.at[0, 0, 0, 0])

            for dx in range(1, nx):
                s.go((a, "x", (0, 0), dx), own.at[p.b], here, p.dev(x=p.xx(dx)))
            s.go((a, "c", 0), own, out.at[p.z, p.x, p.c], p.dev(c=1 - p.c))
        for a, own, out in arrays:
            out[p.z, p.x, p.c] = own[...]

        def from_z(hop):
            way, far = hop
            z = p.z - way * far
            for a, own, out in arrays:
                s.arrived((a, "z", hop))
                if far + 1 < nz:

                    @s.only(lambda way=way: feeds(p, way))
                    def _(a=a, out=out):
                        relay((a, "z", (way, far + 1)), out, z, p.x, p.b, z=p.z + way)

                for dx in range(1, nx):
                    relay((a, "x", hop, dx), out, z, p.x, p.b, x=p.xx(dx))
                for dy in range(1, nb):
                    relay((a, "y", hop, dy), out, z, p.x, p.b, b=p.bb(dy))
                relay((a, "cz", hop), out, z, p.x, p.b, c=1 - p.c)

        def from_plane(hop):
            way, far = hop
            z = p.z - way * far
            for a, own, out in arrays:
                for dx in range(1, nx):
                    x = p.xx(-dx)
                    s.arrived((a, "x", hop, dx))
                    if far % 2 == 0:
                        for dy in range(1, nb):
                            relay((a, "d", hop, dx, dy), out, z, x, p.b, b=p.bb(dy))
                    relay((a, "cx", hop, dx), out, z, x, p.b, c=1 - p.c)
                if far:
                    for dy in range(1, nb):
                        h = p.bb(-dy)
                        s.arrived((a, "y", hop, dy))
                        if far % 2:
                            for dx in range(1, nx):
                                relay((a, "d", hop, dx, dy), out, z, p.x, h, x=p.xx(dx))
                        relay((a, "cy", hop, dy), out, z, p.x, h, c=1 - p.c)

        def from_diagonal(hop):
            way, far = hop
            for a, own, out in arrays:
                for dx in range(1, nx):
                    for dy in range(1, nb):
                        s.arrived((a, "d", hop, dx, dy))
                        relay(
                            (a, "cd", hop, dx, dy),
                            out,
                            p.z - way * far,
                            p.xx(-dx),
                            p.bb(-dy),
                            c=1 - p.c,
                        )

        def from_core(hop):
            for key in keys:
                if key[1] in ("cz", "cx", "cy", "cd") and key[2] == hop:
                    s.arrived(key)

        def under(hop, f):
            if hop[1]:
                s.only(lambda: has(p, *hop))(lambda: f(hop))
            else:
                f(hop)

        hops = [(0, 0)] + steps(nz)
        by_far = [[h for h in hops if h[1] == far] for far in range(nz)]
        for far in range(nz + 2):
            if 1 <= far < nz:
                for hop in by_far[far]:
                    under(hop, from_z)
            if 1 <= far <= nz:
                for hop in by_far[far - 1]:
                    under(hop, from_plane)
            if far >= 2:
                for hop in by_far[far - 2]:
                    under(hop, from_diagonal)
        for a in (0, 1):
            s.arrived((a, "c", 0))
        for hop in hops:
            under(hop, from_core)
        s.finish()

    cb_out, vw_out = call(
        kernel,
        [
            jax.ShapeDtypeStruct((nz, nx, CORES, nb, rows // nb, width), BF16),
            jax.ShapeDtypeStruct((nz, nx, CORES, nb, vrows // nb, bins), BF16),
        ],
        [pltpu.SemaphoreType.DMA((len(keys),)), pltpu.SemaphoreType.DMA((len(keys),))],
        1,
        codebook.reshape(nb, rows // nb, width),
        value_weight.reshape(nb, vrows // nb, bins),
    )
    return cb_out.reshape(nf * rows, width), vw_out.reshape(nf * vrows, bins)


def gather_grads(nb, nf, pre_grad, active, delta_t, value_delta):
    nz, nx = PLANES, nf // (PLANES * CORES)
    rows, width = pre_grad.shape
    bins = value_delta.shape[1]
    half = delta_t.shape[1]
    hops = [(0, 0)] + steps(nz)
    keys = [("c", 0)]
    for hop in hops:
        if hop[1]:
            keys += [("z", hop), ("cz", hop)]
        for dx in range(1, nx):
            keys += [("x", hop, dx), ("cx", hop, dx)]
    keys += [(k, dy) for dy in range(1, nb) for k in ("act", "delta", "value")]

    def kernel(pg, act, dt, vd, pg_out, act_out, dt_out, vd_out, send_sem, recv_sem):
        p = Place(nb, nf)
        p.barrier()
        s = Sends(send_sem, recv_sem, keys, p)
        here, like = pg_out.at[p.z, p.x, p.c], pg_out.at[0, 0, 0]
        mine = pl.ds(pl.multiple_of(p.b * rows, rows), rows)
        for way in (1, -1):

            @s.only(lambda way=way: feeds(p, way))
            def _(way=way):
                s.go(("z", (way, 1)), pg, here, p.dev(z=p.z + way), like)

        for dx in range(1, nx):
            s.go(("x", (0, 0), dx), pg, here, p.dev(x=p.xx(dx)))
        for dy in range(1, nb):
            to = p.bb(dy)
            s.go(("act", dy), act, act_out.at[p.b], p.dev(b=to))
            s.go(("delta", dy), dt.at[to], dt_out.at[:, mine], p.dev(b=to))
            s.go(("value", dy), vd, vd_out.at[p.b], p.dev(b=to))
        s.go(("c", 0), pg, here, p.dev(c=1 - p.c))
        pg_out[p.z, p.x, p.c] = pg[...]
        act_out[p.b] = act[...]
        dt_out[:, mine] = dt[p.b]
        vd_out[p.b] = vd[...]

        def from_z(hop):
            way, far = hop
            ref = pg_out.at[p.z - way * far, p.x, p.c]
            s.arrived(("z", hop))
            if far + 1 < nz:

                @s.only(lambda way=way: feeds(p, way))
                def _():
                    s.go(("z", (way, far + 1)), ref, ref, p.dev(z=p.z + way), like)

            for dx in range(1, nx):
                s.go(("x", hop, dx), ref, ref, p.dev(x=p.xx(dx)), like)
            s.go(("cz", hop), ref, ref, p.dev(c=1 - p.c), like)

        def from_plane(hop):
            way, far = hop
            for dx in range(1, nx):
                s.arrived(("x", hop, dx))
                ref = pg_out.at[p.z - way * far, p.xx(-dx), p.c]
                s.go(("cx", hop, dx), ref, ref, p.dev(c=1 - p.c), like)

        def from_core(hop):
            for key in keys:
                if key[0] in ("cz", "cx") and key[1] == hop:
                    s.arrived(key)

        def under(hop, f):
            if hop[1]:
                s.only(lambda: has(p, *hop))(lambda: f(hop))
            else:
                f(hop)

        for far in range(nz + 1):
            for hop in hops:
                if far and hop[1] == far:
                    under(hop, from_z)
            for hop in hops:
                if hop[1] == far - 1:
                    under(hop, from_plane)
        for key in keys:
            if key[0] in ("act", "delta", "value", "c"):
                s.arrived(key)
        for hop in hops:
            under(hop, from_core)
        s.finish()

    pieces, act_all, dt_all, vd_all = call(
        kernel,
        [
            jax.ShapeDtypeStruct((nz, nx, CORES, rows, width), BF16),
            jax.ShapeDtypeStruct((nb, rows, width), BF16),
            jax.ShapeDtypeStruct((half, nb * rows), BF16),
            jax.ShapeDtypeStruct((nb, rows, bins), BF16),
        ],
        [pltpu.SemaphoreType.DMA((len(keys),)), pltpu.SemaphoreType.DMA((len(keys),))],
        2,
        pre_grad,
        active,
        delta_t,
        value_delta,
    )
    return (
        pieces.reshape(nf * rows, width),
        act_all.reshape(nb * rows, width),
        dt_all,
        vd_all.reshape(nb * rows, bins),
    )


def reduce_grads(nb, nf, trunk, proj_weight, pieces, code, value):
    nz, nx = PLANES, nf // (PLANES * CORES)
    depth = trunk.shape[0]
    width = pieces.shape[1]
    block = next(n for n in (192, 96, 64, 32, 16) if depth % n == 0)
    blocks = depth // block
    lanes = 256
    cuts = 2 if code.shape[3] % 32 == 0 else 1
    crows = code.shape[3] // cuts
    fused = len(value) == 2
    bins = value[-1].shape[-1]
    vrows = width // (nf * nb) if fused else value[0].shape[4]
    chunks = range(cuts + 1)
    keys = [("p", i, dy) for i in range(blocks) for dy in range(1, nb)]
    for a in chunks:
        keys += [(a, "c")] + [(a, "x", d) for d in range(1, nx)]
        keys += [(a, "z", d) for d in range(1, nz)] + [(a, "y", d) for d in range(1, nb)]

    def kernel(tr, pw, pg, cd, *rest):
        factors, rest = rest[: len(value)], rest[len(value) :]
        (tr_out, pj_out, cd_out, vl_out), rest = rest[:4], rest[4:]
        send_sem, recv_sem = rest[-2:]
        vl = rest[-3] if fused else factors[0]
        p = Place(nb, nf)
        p.barrier()
        s = Sends(send_sem, recv_sem, keys, p)
        arrays = []
        for a in chunks:
            if a < cuts:
                part = pl.ds(a * crows, crows)
                own, out = cd.at[:, :, :, part], cd_out.at[:, part]
            else:
                own, out = vl.at[:, :, :, p.b], vl_out
            arrays.append((a, own, out) + tuple(rest[6 * a : 6 * a + 6]))
        for a, own, out, core, *_ in arrays:
            if a == cuts and fused:
                product = lax.dot_general(
                    factors[0][...],
                    factors[1][...],
                    (((0,), (0,)), ((), ())),
                    preferred_element_type=F32,
                )
                vl[...] = product.astype(BF16).reshape(nz, nx, CORES, nb, vrows, bins)
            s.go((a, "c"), own.at[:, :, 1 - p.c], core, p.dev(c=1 - p.c))

        def multiply(i):
            rows = pl.ds(i * block, block)

            def tile(n, carry):
                cols = pl.ds(pl.multiple_of(n * lanes, lanes), lanes)
                pj_out[p.b, rows, cols] = jnp.dot(
                    tr[rows, :], pg[:, cols], preferred_element_type=F32
                ).astype(BF16)
                return carry

            lax.fori_loop(0, width // lanes, tile, 0)
            for dy in range(1, nb):
                ref = pj_out.at[p.b, rows]
                s.go(("p", i, dy), ref, ref, p.dev(b=p.bb(dy)))

        def columns(n, carry):
            cols = pl.ds(pl.multiple_of(n * lanes, lanes), lanes)
            tr_out[:, cols] = lax.dot_general(
                pw[...], pg[cols, :], (((1,), (1,)), ((), ())), preferred_element_type=F32
            ).astype(BF16)
            return carry

        multiply(0)
        for a, own, out, core, xin, xsend, acc, zin, zsend in arrays:
            s.arrived((a, "c"))
            for dx in range(1, nx):
                x = p.xx(dx)
                for z in range(nz):
                    both = own[z, x, p.c].astype(F32) + core[z, x].astype(F32)
                    xsend[dx - 1, z] = both.astype(BF16)
                s.go((a, "x", dx), xsend.at[dx - 1], xin.at[dx - 1], p.dev(x=x))
            for z in range(nz):
                acc[z] = own[z, p.x, p.c].astype(F32) + core[z, p.x].astype(F32)
        for i in range(1, blocks):
            multiply(i)
        for a, own, out, core, xin, xsend, acc, zin, zsend in arrays:
            for dx in range(1, nx):
                s.arrived((a, "x", dx))
                acc[...] += xin[dx - 1].astype(F32)
            for dz in [2, 1, 3]:
                z = p.zz(dz)
                zsend[dz - 1] = acc[z].astype(BF16)
                s.go((a, "z", dz), zsend.at[dz - 1], zin.at[dz - 1], p.dev(z=z))
        for a, own, out, core, xin, xsend, acc, zin, zsend in arrays:
            if a == 0:
                lax.fori_loop(0, pieces.shape[0] // lanes, columns, 0)
            total = acc[p.z]
            for dz in range(1, nz):
                s.arrived((a, "z", dz))
                total = total + zin[dz - 1].astype(F32)
            out[p.b] = total.astype(BF16)
            for dy in range(1, nb):
                s.go((a, "y", dy), out.at[p.b], out.at[p.b], p.dev(b=p.bb(dy)))
        for key in keys:
            if key[0] == "p" or key[1] == "y":
                s.arrived(key)
        s.finish()

    def buffers(r, k):
        return [
            pltpu.VMEM((nz, nx, r, k), BF16),
            pltpu.VMEM((max(nx - 1, 1), nz, r, k), BF16),
            pltpu.VMEM((max(nx - 1, 1), nz, r, k), BF16),
            pltpu.VMEM((nz, r, k), F32),
            pltpu.VMEM((nz - 1, r, k), BF16),
            pltpu.VMEM((nz - 1, r, k), BF16),
        ]

    return call(
        kernel,
        [
            jax.ShapeDtypeStruct((depth, pieces.shape[0]), BF16),
            jax.ShapeDtypeStruct((nb, depth, width), BF16),
            jax.ShapeDtypeStruct((nb, crows * cuts, width), BF16),
            jax.ShapeDtypeStruct((nb, vrows, bins), BF16),
        ],
        buffers(crows, width) * cuts
        + buffers(vrows, bins)
        + [pltpu.VMEM((nz, nx, CORES, nb, vrows, bins), BF16)] * fused
        + [pltpu.SemaphoreType.DMA((len(keys),)), pltpu.SemaphoreType.DMA((len(keys),))],
        3,
        trunk,
        proj_weight,
        pieces,
        code,
        *value,
    )


def dot(a, b, dims):
    return lax.dot_general(a, b, (dims, ((), ())), preferred_element_type=F32)


class Slots(Sends):
    def __init__(self, send_sem, recv_sem, send_at, recv_at, place):
        super().__init__(send_sem, recv_sem, (), place)
        self.send_at, self.recv_at = send_at, recv_at

    def make(self, key, src, dst, dev):
        return pltpu.make_async_remote_copy(
            src_ref=src,
            dst_ref=dst,
            send_sem=self.send_sem.at[self.send_at[key]],
            recv_sem=self.recv_sem.at[self.recv_at[key]],
            device_id=dev,
            device_id_type=MESH,
        )


def number(keys, first, apart=()):
    at, names = {}, {}
    for key in keys:
        name = key
        if key[0] not in apart:
            name = tuple((0, k[1]) if isinstance(k, tuple) and k[1] > 1 else k for k in key)
        at[key] = first + names.setdefault(name, len(names))
    return at, first + len(names)


def fits(nb, nf, codebook, value_weight, depth, pos):
    nx = nf // (PLANES * CORES)
    rows, width = codebook.shape
    vrows = value_weight.shape[0]
    half, vhalf = rows // nb, vrows // nb
    return (
        nb * half == rows
        and nb * vhalf == vrows
        and half % 64 == 0
        and vhalf % 32 == 0
        and CORES * rows == 256
        and nx * CORES * vrows == 256
        and width == PLANES * 256
        and depth % 192 == 0
        and pos * CORES == 256
    )


ORDER = (
    ("pg", 0), ("pg", 1), ("pg", 2), ("pg", 3), ("z", 1, 1),
    ("z", 2, 1), ("z", 0, 1), ("z", 1, 2), ("z", 2, 2), ("z", 3, 1),
    ("z", 1, 3), ("x", 1, 1), ("x", 2, 1), ("x", 0, 0), ("code",),
    ("z", 2, 3), ("z", 0, 2), ("x", 1, 3), ("rsx", 0), ("zx", 0, 1),
    ("x", 2, 0), ("x", 2, 2), ("rsx", 1), ("x", 2, 3), ("z", 0, 3),
    ("x", 3, 0), ("x", 1, 0), ("proj", 2), ("x", 1, 2), ("val",),
    ("zx", 0, 2), ("zx", 0, 3), ("x", 3, 1), ("z", 3, 2), ("rsz", 0),
    ("proj", 1), ("proj", 0), ("z", 3, 3), ("rsx", 2), ("rsz", 1),
    ("x", 3, 2), ("x", 3, 3), ("proj", 3), ("rsz", 2), ("rsy", 0),
    ("fin", 2), ("rsy", 1), ("fin", 0), ("fin", 1), ("fin", 3),
    ("rsy", 2), ("col",),
)
CROSS_FIRST = (0,)


def fused(nb, nf, trunk, pre_act, proj_weight, codebook, value_weight, target, low, frac):
    nz, nx = PLANES, nf // (PLANES * CORES)
    pos, width = pre_act.shape
    rows, vrows = codebook.shape[0], value_weight.shape[0]
    bins = value_weight.shape[1]
    depth, total_pos = trunk.shape
    codes = nf * rows
    half, vhalf = rows // nb, vrows // nb
    cw = 256
    pieces = width // cw
    cuts = 2
    ck = half // cuts
    hops = [(0, 0)] + steps(nz)
    by_far = [[h for h in hops if h[1] == far] for far in range(nz)]

    early = []
    for hop in hops:
        early += [("core", k, hop) for k in range(2)]
        for a in range(3):
            if hop[1]:
                early += [("z", a, hop)] + [("y", a, hop, dy) for dy in range(1, nb)]
            for dx in range(1, nx):
                early += [("x", a, hop, dx)] + [("d", a, hop, dx, dy) for dy in range(1, nb)]
    swap = [(k, dy) for dy in range(1, nb) for k in ("act", "delta", "value")]
    late = []
    for n in range(pieces):
        for hop in hops:
            late += [("gc", n, hop)]
            if hop[1]:
                late += [("gz", n, hop)]
            if hop[1] == 0 or n not in CROSS_FIRST:
                late += [("gx", n, hop, dx) for dx in range(1, nx)]
            else:
                late += [("gzx", n, hop, dx) for dx in range(1, nx)]
        late += [("p", n, dy) for dy in range(1, nb)]
    for a in range(cuts + 1):
        late += [("rc", a)] + [("rx", a, d) for d in range(1, nx)]
        late += [("rz", a, d) for d in range(1, nz)] + [("ry", a, d) for d in range(1, nb)]
    swap_at, base = number(swap, 0)
    early_send, sends = number(early, base, ("z",))
    early_recv, recvs = number(early, base)
    late_send, last = number(late, base, ("gz", "gzx"))
    sends = max(sends, last)
    late_recv, recvs = number(late, recvs)
    early_send.update(swap_at)
    early_recv.update(swap_at)
    late_send.update(swap_at)
    late_recv.update(swap_at)

    def kernel(
        pre_in,
        cb_in,
        vw_in,
        tgt_in,
        lo_in,
        fr_in,
        tr_in,
        pw_in,
        tr_out,
        pj_out,
        cd_out,
        vl_out,
        cb,
        vw,
        pre,
        tgt,
        lo,
        fr,
        tr,
        pw,
        cb_all,
        vw_all,
        gate,
        act_all,
        logit,
        top,
        vlog,
        delta,
        delta_t,
        vd_all,
        dt_all,
        pg,
        part,
        vpart,
        trg,
        pj_all,
        pj,
        cd_all,
        cd,
        vl_all,
        vl,
        *rest,
    ):
        local_sem, send_sem, recv_sem = rest[-3:]
        p = Place(nb, nf)
        inputs = (cb_in, vw_in, pre_in, tgt_in, lo_in, fr_in, tr_in, pw_in)
        loads = [
            pltpu.make_async_copy(src, dst, local_sem.at[i])
            for i, (src, dst) in enumerate(zip(inputs, (cb, vw, pre, tgt, lo, fr, tr, pw)))
        ]
        for load in loads:
            load.start()
        p.barrier()
        for load in loads[:3]:
            load.wait()
        s = Slots(send_sem, recv_sem, early_send, early_recv, p)
        g = Slots(send_sem, recv_sem, late_send, late_recv, p)

        def under(s, far, f):
            for hop in by_far[far]:
                if far:
                    s.only(lambda hop=hop: has(p, *hop))(lambda: f(hop))
                else:
                    f(hop)

        sub = half // 2
        shards = (
            (0, vw, vw_all, vrows, vhalf, 0, vhalf),
            (1, cb, cb_all, rows, half, 0, sub),
            (2, cb, cb_all, rows, half, sub, sub),
        )

        def spot(shard, z, x, h):
            a, own, out, per, piece, skip, size = shard
            return out.at[z, x, p.c, pl.ds(pl.multiple_of(h * piece + skip, size), size)]

        def mine(shard, h):
            a, own, out, per, piece, skip, size = shard
            return own.at[pl.ds(pl.multiple_of(h * piece + skip, size), size)]

        def whole(shard):
            a, own, out, per, piece, skip, size = shard
            return lambda: out.at[0, 0, 0, pl.ds(0, size)]

        def relay(key, shard, at_z, at_x, at_h, **to):
            ref = spot(shard, at_z, at_x, at_h)
            s.go(key, ref, ref, p.dev(**to), whole(shard))

        for shard in shards:
            a = shard[0]
            here = spot(shard, p.z, p.x, p.b)
            for way in (1, -1):

                @s.only(lambda way=way: feeds(p, way))
                def _():
                    s.go(("z", a, (way, 1)), mine(shard, p.b), here, p.dev(z=p.z + way), whole(shard))

            for dx in range(1, nx):
                s.go(("x", a, (0, 0), dx), mine(shard, p.b), here, p.dev(x=p.xx(dx)), whole(shard))
        cb_all[p.z, p.x, p.c] = cb[...]
        vw_all[p.z, p.x, p.c] = vw[...]

        def activate(i, carry):
            cols = pl.ds(pl.multiple_of(i * cw, cw), cw)
            v = pre[:, cols].astype(F32)
            sigma = jax.nn.sigmoid(v)
            act_all[p.b, :, cols] = (v * sigma).astype(BF16)
            gate[:, cols] = sigma * (1.0 + v * (1.0 - sigma))
            return carry

        lax.fori_loop(0, width // cw, activate, 0)
        top[...] = jnp.full(top.shape, -jnp.inf, F32)
        vlog[...] = jnp.zeros(vlog.shape, F32)

        def from_z(shard, hop):
            a = shard[0]
            way, far = hop
            z = p.z - way * far
            s.arrived(("z", a, hop))
            if far + 1 < nz:

                @s.only(lambda way=way: feeds(p, way))
                def _():
                    relay(("z", a, (way, far + 1)), shard, z, p.x, p.b, z=p.z + way)

            for dx in range(1, nx):
                relay(("x", a, hop, dx), shard, z, p.x, p.b, x=p.xx(dx))
            for dy in range(1, nb):
                relay(("y", a, hop, dy), shard, z, p.x, p.b, b=p.bb(dy))

        def from_plane(shard, hop):
            a = shard[0]
            way, far = hop
            z = p.z - way * far
            for dx in range(1, nx):
                s.arrived(("x", a, hop, dx))
                if far % 2 == 0:
                    for dy in range(1, nb):
                        relay(("d", a, hop, dx, dy), shard, z, p.xx(-dx), p.b, b=p.bb(dy))
            if far:
                for dy in range(1, nb):
                    s.arrived(("y", a, hop, dy))
                    if far % 2:
                        for dx in range(1, nx):
                            relay(("d", a, hop, dx, dy), shard, z, p.x, p.bb(-dy), x=p.xx(dx))

        def from_diagonal(hop):
            way, far = hop
            for shard in shards:
                for dx in range(1, nx):
                    for dy in range(1, nb):
                        s.arrived(("d", shard[0], hop, dx, dy))
            for k, out in enumerate((cb_all, vw_all)):
                ref = out.at[p.z - way * far, :, p.c]
                s.go(("core", k, hop), ref, ref, p.dev(c=1 - p.c), lambda out=out: out.at[0, :, 0])

        def from_core(hop):
            for k in range(2):
                s.arrived(("core", k, hop))

        def near(j):
            up = (0, 1, 2, 3)[j], (1, 0, 2, 3)[j], (2, 3, 1, 0)[j], (3, 2, 1, 0)[j]
            z = jnp.where(p.z == 0, up[0], up[3])
            z = jnp.where(p.z == 1, up[1], z)
            return jnp.where(p.z == 2, up[2], z)

        def score(j):
            z = near(j)

            def tile(i, carry):
                at = pl.ds(pl.multiple_of((z * nx + i) * 256, 256), 256)
                block = dot(cb_all[z, i].reshape(256, width), act_all[p.b], ((1,), (1,)))
                logit[at, :] = block
                top[...] = jnp.maximum(top[...], jnp.max(block, axis=0, keepdims=True))
                return carry

            lax.fori_loop(0, nx, tile, 0)
            at = pl.ds(pl.multiple_of(z * 256, 256), 256)
            vlog[...] += dot(act_all[p.b, :, at], vw_all[z].reshape(256, bins), ((1,), (0,)))

        for far in range(nz + 3):
            for shard in shards:
                if 1 <= far < nz:
                    under(s, far, lambda hop: from_z(shard, hop))
                if 1 <= far <= nz:
                    under(s, far - 1, lambda hop: from_plane(shard, hop))
            if 2 <= far < nz + 2:
                under(s, far - 2, from_diagonal)
            if far == nz:
                for dy in range(1, nb):
                    ref = act_all.at[p.b]
                    g.go(("act", dy), ref, ref, p.dev(b=p.bb(dy)))
            if far >= 3:
                under(s, far - 3, from_core)
                score(far - 3)

        for load in loads[3:6]:
            load.wait()
        high = jnp.max(vlog[...], axis=1, keepdims=True)
        grown = jnp.exp(vlog[...] - high)
        probs = grown * (1.0 / jnp.sum(grown, axis=1, keepdims=True))
        ids = lax.broadcasted_iota(jnp.int32, (pos, bins), 1).astype(F32)
        column = jnp.broadcast_to(lo[...].astype(F32), (pos, pos)).T[:, :1]
        share = jnp.broadcast_to(fr[...].astype(F32) / 1024.0, (pos, pos)).T[:, :1]
        want = jnp.where(ids == column, 1.0 - share, 0.0)
        want = want + jnp.where(ids == column + 1.0, share, 0.0)
        vd_all[p.b] = (probs - want).astype(BF16)
        for dy in range(1, nb):
            ref = vd_all.at[p.b]
            g.go(("value", dy), ref, ref, p.dev(b=p.bb(dy)))

        blocks = codes // 256
        best = top[...]

        def grow(i, total):
            at = pl.ds(pl.multiple_of(i * 256, 256), 256)
            e = jnp.exp(logit[at, :] - best)
            logit[at, :] = e
            return total + jnp.sum(e, axis=0, keepdims=True)

        scale = 1.0 / lax.fori_loop(0, blocks, grow, jnp.zeros((1, pos), F32))
        group = 256 // rows
        code_ids = lax.broadcasted_iota(jnp.int32, (256, pos), 0)

        def differ(i, carry):
            at = pl.ds(pl.multiple_of(i * 256, 256), 256)
            hot = jnp.where(code_ids + i * 256 == tgt[...], 1.0, 0.0)
            d = logit[at, :] * scale - hot
            delta[:, at] = d.T.astype(BF16)
            delta_t[pl.ds(i * group, group)] = d.astype(BF16).reshape(group, nb, half, pos)
            return carry

        lax.fori_loop(0, blocks, differ, 0)
        lanes = pl.ds(pl.multiple_of(p.b * pos, pos), pos)
        for dy in range(1, nb):
            to = p.bb(dy)
            g.go(("delta", dy), delta_t.at[:, to], dt_all.at[:, :, lanes], p.dev(b=to))
        dt_all[:, :, lanes] = delta_t[:, p.b]
        s.finish()

        def pass_on(n, at_z, at_x, key, **to):
            ref = pg.at[n, at_z, at_x, p.c]
            g.go(key, ref, ref, p.dev(**to), lambda: pg.at[n, 0, 0, 0])

        def onward(n, kind, z, x, far, extra, ways):
            for way in ways:

                @g.only(lambda way=way: feeds(p, way))
                def _():
                    pass_on(n, z, x, (kind, n, (way, far)) + extra, z=p.z + way)

        def across(n, hop):
            for dx in range(1, nx):
                pass_on(n, p.z - hop[0] * hop[1], p.x, ("gx", n, hop, dx), x=p.xx(dx))

        def to_core(n, hop):
            ref = pg.at[n, p.z - hop[0] * hop[1], :, p.c]
            g.go(("gc", n, hop), ref, ref, p.dev(c=1 - p.c), lambda: pg.at[n, 0, :, 0])

        def head(n):
            cols = pl.ds(n * cw, cw)
            back = dot(delta[...], cb_all[:, :, :, :, cols].reshape(codes, cw), ((1,), (0,)))
            back = back + dot(vd_all[p.b], vw_all[n].reshape(cw, bins), ((1,), (1,)))
            pg[n, p.z, p.x, p.c] = (back * gate[:, cols]).astype(BF16)
            if n in CROSS_FIRST:
                across(n, (0, 0))
            onward(n, "gz", p.z, p.x, 1, (), (1, -1))
            if n not in CROSS_FIRST:
                across(n, (0, 0))

        def grad_z(n, far):
            def run(hop):
                z = p.z - hop[0] * far
                g.arrived(("gz", n, hop))
                if far + 1 < nz:
                    onward(n, "gz", z, p.x, far + 1, (), hop[:1])
                if n not in CROSS_FIRST:
                    across(n, hop)

            under(g, far, run)

        def grad_x(n, far):
            def run(hop):
                for dx in range(1, nx):
                    g.arrived(("gx", n, hop, dx))
                    if n in CROSS_FIRST:
                        onward(n, "gzx", p.z, p.xx(-dx), 1, (dx,), (1, -1))
                to_core(n, hop)

            under(g, far, run)

        def grad_zx(n, far):
            def run(hop):
                for dx in range(1, nx):
                    g.arrived(("gzx", n, hop, dx))
                    if far + 1 < nz:
                        onward(n, "gzx", p.z - hop[0] * far, p.xx(-dx), far + 1, (dx,), hop[:1])
                to_core(n, hop)

            under(g, far, run)

        arrays = []
        for a in range(cuts + 1):
            if a < cuts:
                own, out = part.at[:, :, :, pl.ds(a * ck, ck)], cd_all.at[:, pl.ds(a * ck, ck)]
            else:
                own, out = vpart.at[:, :, :, p.b], vl_all
            arrays.append((own, out) + tuple(rest[6 * a : 6 * a + 6]))
        deep = nb * pos

        def to_sum(a):
            own, out, core, *_ = arrays[a]
            g.go(("rc", a), own.at[:, :, 1 - p.c], core, p.dev(c=1 - p.c))

        def code():
            for dy in range(1, nb):
                g.arrived(("act", dy))
                g.arrived(("delta", dy))

            def block(i, carry):
                z = i // (width // cw)
                cols = pl.ds(pl.multiple_of((i % (width // cw)) * cw, cw), cw)
                left = dt_all[pl.ds(z * nx * CORES, nx * CORES)].reshape(nx * CORES * half, deep)
                right = act_all[:, :, cols].reshape(deep, cw)
                product = dot(left, right, ((1,), (0,)))
                part[z, :, :, :, cols] = product.astype(BF16).reshape(nx, CORES, half, cw)
                return carry

            lax.fori_loop(0, nz * (width // cw), block, 0)
            for a in range(cuts):
                to_sum(a)

        def val():
            for dy in range(1, nb):
                g.arrived(("value", dy))

            def block(z, carry):
                cols = pl.ds(pl.multiple_of(z * 256, 256), 256)
                left = act_all[:, :, cols].reshape(deep, 256)
                product = dot(left, vd_all[...].reshape(deep, bins), ((0,), (0,)))
                vpart[z] = product.astype(BF16).reshape(nx, CORES, nb, vhalf, bins)
                return carry

            lax.fori_loop(0, nz, block, 0)
            to_sum(cuts)

        def rsx(a):
            own, out, core, xin, xsend, acc, zin, zsend = arrays[a]
            g.arrived(("rc", a))
            for dx in range(1, nx):
                x = p.xx(dx)
                for z in range(nz):
                    both = own[z, x, p.c].astype(F32) + core[z, x].astype(F32)
                    xsend[dx - 1, z] = both.astype(BF16)
                g.go(("rx", a, dx), xsend.at[dx - 1], xin.at[dx - 1], p.dev(x=x))
            for z in range(nz):
                acc[z] = own[z, p.x, p.c].astype(F32) + core[z, p.x].astype(F32)

        def rsz(a):
            own, out, core, xin, xsend, acc, zin, zsend = arrays[a]
            for dx in range(1, nx):
                g.arrived(("rx", a, dx))
                acc[...] += xin[dx - 1].astype(F32)
            for dz in [2, 1, 3]:
                z = p.zz(dz)
                zsend[dz - 1] = acc[z].astype(BF16)
                g.go(("rz", a, dz), zsend.at[dz - 1], zin.at[dz - 1], p.dev(z=z))

        def rsy(a):
            own, out, core, xin, xsend, acc, zin, zsend = arrays[a]
            total = acc[p.z]
            for dz in range(1, nz):
                g.arrived(("rz", a, dz))
                total = total + zin[dz - 1].astype(F32)
            out[p.b] = total.astype(BF16)
            for dy in range(1, nb):
                g.go(("ry", a, dy), out.at[p.b], out.at[p.b], p.dev(b=p.bb(dy)))

        def proj(n):
            for far in range(nz):
                under(g, far, lambda hop: g.arrived(("gc", n, hop)))

            def block(i, carry):
                at = pl.ds(pl.multiple_of(i * 192, 192), 192)
                pj_all[p.b, n, at, :] = jnp.dot(
                    tr[at, :], pg[n].reshape(total_pos, cw), preferred_element_type=F32
                ).astype(BF16)
                return carry

            lax.fori_loop(0, depth // 192, block, 0)
            for dy in range(1, nb):
                ref = pj_all.at[p.b, n]
                g.go(("p", n, dy), ref, ref, p.dev(b=p.bb(dy)))

        stores = [
            pltpu.make_async_copy(src, dst, local_sem.at[i])
            for i, (src, dst) in enumerate(((trg, tr_out), (pj, pj_out), (cd, cd_out), (vl, vl_out)))
        ]

        def col():
            def block(i, carry):
                at = pl.ds(pl.multiple_of(i * 256, 256), 256)
                z, x = i // nx, i % nx
                total = 0.0
                for n in range(pieces):
                    there = pg[n, z, x].reshape(256, cw)
                    total = total + dot(pw[:, pl.ds(n * cw, cw)], there, ((1,), (1,)))
                trg[:, at] = total.astype(BF16)
                return carry

            lax.fori_loop(0, nz * nx, block, 0)
            stores[0].start()

        def fin(n):
            for dy in range(1, nb):
                g.arrived(("p", n, dy))
            total = pj_all[0, n].astype(F32)
            for b in range(1, nb):
                total = total + pj_all[b, n].astype(F32)
            pj[:, pl.ds(n * cw, cw)] = total

        for load in loads[6:]:
            load.wait()
        acts = dict(
            pg=head, z=grad_z, x=grad_x, zx=grad_zx, code=code, val=val, rsx=rsx, rsz=rsz, rsy=rsy,
            proj=proj, col=col, fin=fin,
        )
        for name, *where in ORDER:
            acts[name](*where)
        stores[1].start()
        for a in range(cuts + 1):
            for dy in range(1, nb):
                g.arrived(("ry", a, dy))
        for b in range(nb):
            cd[pl.ds(b * half, half), :] = cd_all[b].astype(F32)
            vl[pl.ds(b * vhalf, vhalf), :] = vl_all[b].astype(F32)
        for store in stores[2:]:
            store.start()
        g.finish()
        for store in stores:
            store.wait()

    def buffers(r, k):
        return [
            pltpu.VMEM((nz, nx, r, k), BF16),
            pltpu.VMEM((max(nx - 1, 1), nz, r, k), BF16),
            pltpu.VMEM((max(nx - 1, 1), nz, r, k), BF16),
            pltpu.VMEM((nz, r, k), F32),
            pltpu.VMEM((nz - 1, r, k), BF16),
            pltpu.VMEM((nz - 1, r, k), BF16),
        ]

    anywhere = pl.BlockSpec(memory_space=pl.ANY)
    results = pl.pallas_call(
        kernel,
        out_shape=[
            jax.ShapeDtypeStruct((depth, total_pos), BF16),
            jax.ShapeDtypeStruct((depth, width), F32),
            jax.ShapeDtypeStruct((rows, width), F32),
            jax.ShapeDtypeStruct((vrows, bins), F32),
        ],
        in_specs=[anywhere] * 8,
        out_specs=[anywhere] * 4,
        scratch_shapes=[
            pltpu.VMEM((rows, width), BF16),
            pltpu.VMEM((vrows, bins), BF16),
            pltpu.VMEM((pos, width), BF16),
            pltpu.VMEM((1, pos), jnp.int32),
            pltpu.VMEM((1, pos), jnp.int32),
            pltpu.VMEM((1, pos), jnp.int32),
            pltpu.VMEM((depth, total_pos), BF16),
            pltpu.VMEM((depth, width), BF16),
            pltpu.VMEM((nz, nx, CORES, rows, width), BF16),
            pltpu.VMEM((nz, nx, CORES, vrows, bins), BF16),
            pltpu.VMEM((pos, width), F32),
            pltpu.VMEM((nb, pos, width), BF16),
            pltpu.VMEM((codes, pos), F32),
            pltpu.VMEM((1, pos), F32),
            pltpu.VMEM((pos, bins), F32),
            pltpu.VMEM((pos, codes), BF16),
            pltpu.VMEM((nf, nb, half, pos), BF16),
            pltpu.VMEM((nb, pos, bins), BF16),
            pltpu.VMEM((nf, half, nb * pos), BF16),
            pltpu.VMEM((pieces, nz, nx, CORES, pos, cw), BF16),
            pltpu.VMEM((nz, nx, CORES, half, width), BF16),
            pltpu.VMEM((nz, nx, CORES, nb, vhalf, bins), BF16),
            pltpu.VMEM((depth, total_pos), BF16),
            pltpu.VMEM((nb, pieces, depth, cw), BF16),
            pltpu.VMEM((depth, width), F32),
            pltpu.VMEM((nb, half, width), BF16),
            pltpu.VMEM((rows, width), F32),
            pltpu.VMEM((nb, vhalf, bins), BF16),
            pltpu.VMEM((vrows, bins), F32),
        ]
        + buffers(ck, width) * cuts
        + buffers(vhalf, bins)
        + [
            pltpu.SemaphoreType.DMA((8,)),
            pltpu.SemaphoreType.DMA((sends,)),
            pltpu.SemaphoreType.DMA((recvs,)),
        ],
        compiler_params=pltpu.CompilerParams(
            collective_id=4, has_side_effects=True, vmem_limit_bytes=60 << 20
        ),
    )(pre_act, codebook, value_weight, target, low, frac, trunk, proj_weight)

    def hand_over(*refs):
        count = len(results)
        sources, sinks, held = refs[:count], refs[count : 2 * count], refs[2 * count : 3 * count]
        sem = refs[-1]
        incoming, outgoing = [], []
        for i in range(count):
            cut = 2 if results[i].shape[0] % 128 == 0 else 1
            size = results[i].shape[0] // cut
            for k in range(cut):
                at, n = pl.ds(k * size, size), 2 * i + k
                incoming.append(
                    pltpu.make_async_copy(sources[i].at[at], held[i].at[at], sem.at[0, n])
                )
                outgoing.append(
                    pltpu.make_async_copy(held[i].at[at], sinks[i].at[at], sem.at[1, n])
                )
        for copy in incoming:
            copy.start()
        for first, second in zip(incoming, outgoing):
            first.wait()
            second.start()
        for copy in outgoing:
            copy.wait()

    return pl.pallas_call(
        hand_over,
        out_shape=[jax.ShapeDtypeStruct(r.shape, r.dtype) for r in results],
        in_specs=[anywhere] * 4,
        out_specs=[anywhere] * 4,
        scratch_shapes=[pltpu.VMEM(r.shape, r.dtype) for r in results]
        + [pltpu.SemaphoreType.DMA((2, 8))],
        compiler_params=pltpu.CompilerParams(vmem_limit_bytes=60 << 20),
    )(*results)


def make_body(nb, nf):
    nz, nx = PLANES, nf // (PLANES * CORES)

    def body(
        trunk, pre_act, proj_weight, codebook, value_weight, code_target, value_bin, value_frac
    ):
        if fits(nb, nf, codebook, value_weight, trunk.shape[0], pre_act.shape[0]):
            row = (1, pre_act.shape[0])
            return fused(
                nb,
                nf,
                trunk,
                pre_act,
                proj_weight,
                codebook,
                value_weight,
                code_target.reshape(row),
                value_bin.reshape(row),
                value_frac.reshape(row),
            )
        all_codes, bins_weight = gather_weights(nb, nf, codebook, value_weight)
        rows, width = pre_act.shape
        num_codes = all_codes.shape[0]
        num_bins = bins_weight.shape[1]
        pre_value = pre_act.astype(F32)
        gate_sigma = jax.nn.sigmoid(pre_value)
        active = (pre_value * gate_sigma).astype(BF16)
        code_logits = jnp.einsum("rk,ck->rc", active, all_codes, preferred_element_type=F32)
        code_probs = jax.nn.softmax(code_logits, axis=-1)
        code_ids = lax.broadcasted_iota(jnp.int32, (1, num_codes), 1)
        one_hot = (code_target[:, None] == code_ids).astype(F32)
        code_delta = (code_probs - one_hot).astype(BF16)
        value_logits = jnp.dot(active, bins_weight, preferred_element_type=F32)
        value_probs = jax.nn.softmax(value_logits, axis=-1)
        bin_ids = lax.broadcasted_iota(jnp.int32, (1, num_bins), 1)
        fraction = value_frac.astype(F32)[:, None] / 1024.0
        target = jnp.where(bin_ids == value_bin[:, None], 1.0 - fraction, 0.0)
        target = target + jnp.where(bin_ids == value_bin[:, None] + 1, fraction, 0.0)
        value_delta = (value_probs - target).astype(BF16)
        backward = jnp.dot(code_delta, all_codes, preferred_element_type=F32)
        backward = backward + jnp.einsum(
            "rb,kb->rk", value_delta, bins_weight, preferred_element_type=F32
        )
        pre_grad = (backward * gate_sigma * (1.0 + pre_value * (1.0 - gate_sigma))).astype(BF16)
        own = codebook.shape[0] // nb
        delta_t = code_delta.T.reshape(nf, nb, own, rows).swapaxes(0, 1)
        delta_t = delta_t.reshape(nb, nf * own, rows)
        pieces, act_all, dt_all, vd_all = gather_grads(
            nb, nf, pre_grad, active, delta_t, value_delta
        )
        code_part = jnp.dot(dt_all, act_all, preferred_element_type=F32)
        code_part = code_part.astype(BF16).reshape(nz, nx, CORES, own, width)
        vown = value_weight.shape[0] // nb
        if vown % 16 == 0:
            value_part = (act_all, vd_all)
        else:
            value_part = jnp.einsum("rk,rb->kb", act_all, vd_all, preferred_element_type=F32)
            value_part = value_part.astype(BF16)
            value_part = (value_part.reshape(nz, nx, CORES, nb, vown, num_bins),)
        out_cols, proj_all, code_all, value_all = reduce_grads(
            nb, nf, trunk, proj_weight, pieces, code_part, value_part
        )
        proj_grad = jnp.sum(proj_all.astype(F32), axis=0)
        code_grad = code_all.reshape(nb * own, width).astype(F32)
        value_grad = value_all.reshape(nb * vown, num_bins).astype(F32)
        return (out_cols, proj_grad, code_grad, value_grad)

    return body


def solution(mesh):
    in_specs = (
        P("fsdp", "batch"),
        P(("batch", "fsdp"), None),
        P("fsdp", None),
        P("fsdp", None),
        P("fsdp", None),
        P(("batch", "fsdp")),
        P(("batch", "fsdp")),
        P(("batch", "fsdp")),
    )
    out_specs = (P("fsdp", "batch"), P("fsdp", None), P("fsdp", None), P("fsdp", None))
    body = make_body(mesh.shape["batch"], mesh.shape["fsdp"])
    return jax.shard_map(body, mesh=mesh, in_specs=in_specs, out_specs=out_specs, check_vma=False)
```

```python
import jax
import jax.numpy as jnp
from jax import lax
from jax.experimental import pallas as pl
from jax.experimental.pallas import tpu as pltpu
from jax.sharding import PartitionSpec as P

MESH = pl.DeviceIdType.MESH
BF16 = jnp.bfloat16
F32 = jnp.float32
CORES = 2
PLANES = 4


class Place:
    def __init__(self, nb, nf):
        self.nb, self.nz = nb, PLANES
        self.nx = nf // (PLANES * CORES)
        f = lax.axis_index("fsdp")
        self.b = lax.axis_index("batch")
        self.z = f // (self.nx * CORES)
        self.x = (f // CORES) % self.nx
        self.c = f % CORES

    def dev(self, b=None, z=None, x=None, c=None):
        b = self.b if b is None else b
        z = self.z if z is None else z
        x = self.x if x is None else x
        c = self.c if c is None else c
        return (b, (z * self.nx + x) * CORES + c)

    def zz(self, d):
        return lax.rem(self.z + d + self.nz, self.nz)

    def xx(self, d):
        return lax.rem(self.x + d + self.nx, self.nx)

    def bb(self, d):
        return lax.rem(self.b + d + self.nb, self.nb)

    def barrier(self):
        sem = pltpu.get_barrier_semaphore()
        peers = [self.dev(z=self.zz(d)) for d in range(1, self.nz)]
        peers += [self.dev(x=self.xx(d)) for d in range(1, self.nx)]
        peers += [self.dev(b=self.bb(d)) for d in range(1, self.nb)]
        peers += [self.dev(c=1 - self.c)]
        for peer in peers:
            pl.semaphore_signal(sem, inc=1, device_id=peer, device_id_type=MESH)
        pl.semaphore_wait(sem, len(peers))


def steps(nz):
    return [(way, far) for far in range(1, nz) for way in (1, -1)]


class Sends:
    def __init__(self, send_sem, recv_sem, keys, place):
        self.send_sem, self.recv_sem, self.place = send_sem, recv_sem, place
        self.at = {k: i for i, k in enumerate(keys)}
        self.like = {}
        self.started = []
        self.when = ()

    def make(self, key, src, dst, dev):
        i = self.at[key]
        return pltpu.make_async_remote_copy(
            src_ref=src,
            dst_ref=dst,
            send_sem=self.send_sem.at[i],
            recv_sem=self.recv_sem.at[i],
            device_id=dev,
            device_id_type=MESH,
        )

    def go(self, key, src, dst, dev, like=None):
        self.make(key, src, dst, dev).start()
        self.like[key] = dst if like is None else like
        self.started.append((key, self.when))

    def waiter(self, key):
        ref = self.like[key]
        ref = ref() if callable(ref) else ref
        return self.make(key, ref, ref, self.place.dev(c=1 - self.place.c))

    def arrived(self, key):
        self.waiter(key).wait_recv()

    def finish(self):
        for key, whens in self.started:

            def wait(key=key):
                self.waiter(key).wait_send()

            if whens:
                met = whens[0]()
                for when in whens[1:]:
                    met = jnp.logical_and(met, when())
                pl.when(met)(wait)
            else:
                wait()

    def only(self, when):
        def run(f):
            outer = self.when
            self.when = outer + (when,)

            @pl.when(when())
            def _():
                f()

            self.when = outer

        return run


def call(kernel, outs, scratch, cid, *args):
    return pl.pallas_call(
        kernel,
        out_shape=outs,
        in_specs=[pl.BlockSpec(memory_space=pltpu.VMEM)] * len(args),
        out_specs=[pl.BlockSpec(memory_space=pltpu.VMEM)] * len(outs),
        scratch_shapes=scratch,
        compiler_params=pltpu.CompilerParams(collective_id=cid, has_side_effects=True),
    )(*args)


def has(p, way, far):
    return p.z >= far if way == 1 else p.z + far < p.nz


def feeds(p, way):
    return p.z + 1 < p.nz if way == 1 else p.z >= 1


def gather_weights_keys(nb, nx, nz):
    keys = []
    for a in (0, 1):
        keys += [(a, "c", 0)]
        for hop in [(0, 0)] + steps(nz):
            if hop[1]:
                keys += [(a, "z", hop), (a, "cz", hop)]
                for dy in range(1, nb):
                    keys += [(a, "y", hop, dy), (a, "cy", hop, dy)]
            for dx in range(1, nx):
                keys += [(a, "x", hop, dx), (a, "cx", hop, dx)]
                for dy in range(1, nb):
                    keys += [(a, "d", hop, dx, dy), (a, "cd", hop, dx, dy)]
    return keys


def gather_weights(nb, nf, codebook, value_weight):
    nz, nx = PLANES, nf // (PLANES * CORES)
    keys = gather_weights_keys(nb, nx, nz)
    rows, width = codebook.shape
    vrows, bins = value_weight.shape

    def kernel(cb, vw, cb_out, vw_out, send_sem, recv_sem):
        p = Place(nb, nf)
        p.barrier()
        s = Sends(send_sem, recv_sem, keys, p)
        arrays = ((0, cb, cb_out), (1, vw, vw_out))

        def spot(out, z, x, h):
            return out.at[z, x, p.c, h]

        def relay(key, out, at_z, at_x, at_h, **to):
            ref = spot(out, at_z, at_x, at_h)
            s.go(key, ref, ref, p.dev(**to), lambda: out.at[0, 0, 0, 0])

        for a, own, out in arrays:
            here = spot(out, p.z, p.x, p.b)
            for way in (1, -1):

                @s.only(lambda way=way: feeds(p, way))
                def _(a=a, own=own, out=out, here=here, way=way):
                    s.go((a, "z", (way, 1)), own.at[p.b], here, p.dev(z=p.z + way), lambda: out.at[0, 0, 0, 0])

            for dx in range(1, nx):
                s.go((a, "x", (0, 0), dx), own.at[p.b], here, p.dev(x=p.xx(dx)))
            s.go((a, "c", 0), own, out.at[p.z, p.x, p.c], p.dev(c=1 - p.c))
        for a, own, out in arrays:
            out[p.z, p.x, p.c] = own[...]

        def from_z(hop):
            way, far = hop
            z = p.z - way * far
            for a, own, out in arrays:
                s.arrived((a, "z", hop))
                if far + 1 < nz:

                    @s.only(lambda way=way: feeds(p, way))
                    def _(a=a, out=out):
                        relay((a, "z", (way, far + 1)), out, z, p.x, p.b, z=p.z + way)

                for dx in range(1, nx):
                    relay((a, "x", hop, dx), out, z, p.x, p.b, x=p.xx(dx))
                for dy in range(1, nb):
                    relay((a, "y", hop, dy), out, z, p.x, p.b, b=p.bb(dy))
                relay((a, "cz", hop), out, z, p.x, p.b, c=1 - p.c)

        def from_plane(hop):
            way, far = hop
            z = p.z - way * far
            for a, own, out in arrays:
                for dx in range(1, nx):
                    x = p.xx(-dx)
                    s.arrived((a, "x", hop, dx))
                    if far % 2 == 0:
                        for dy in range(1, nb):
                            relay((a, "d", hop, dx, dy), out, z, x, p.b, b=p.bb(dy))
                    relay((a, "cx", hop, dx), out, z, x, p.b, c=1 - p.c)
                if far:
                    for dy in range(1, nb):
                        h = p.bb(-dy)
                        s.arrived((a, "y", hop, dy))
                        if far % 2:
                            for dx in range(1, nx):
                                relay((a, "d", hop, dx, dy), out, z, p.x, h, x=p.xx(dx))
                        relay((a, "cy", hop, dy), out, z, p.x, h, c=1 - p.c)

        def from_diagonal(hop):
            way, far = hop
            for a, own, out in arrays:
                for dx in range(1, nx):
                    for dy in range(1, nb):
                        s.arrived((a, "d", hop, dx, dy))
                        relay(
                            (a, "cd", hop, dx, dy),
                            out,
                            p.z - way * far,
                            p.xx(-dx),
                            p.bb(-dy),
                            c=1 - p.c,
                        )

        def from_core(hop):
            for key in keys:
                if key[1] in ("cz", "cx", "cy", "cd") and key[2] == hop:
                    s.arrived(key)

        def under(hop, f):
            if hop[1]:
                s.only(lambda: has(p, *hop))(lambda: f(hop))
            else:
                f(hop)

        hops = [(0, 0)] + steps(nz)
        by_far = [[h for h in hops if h[1] == far] for far in range(nz)]
        for far in range(nz + 2):
            if 1 <= far < nz:
                for hop in by_far[far]:
                    under(hop, from_z)
            if 1 <= far <= nz:
                for hop in by_far[far - 1]:
                    under(hop, from_plane)
            if far >= 2:
                for hop in by_far[far - 2]:
                    under(hop, from_diagonal)
        for a in (0, 1):
            s.arrived((a, "c", 0))
        for hop in hops:
            under(hop, from_core)
        s.finish()

    cb_out, vw_out = call(
        kernel,
        [
            jax.ShapeDtypeStruct((nz, nx, CORES, nb, rows // nb, width), BF16),
            jax.ShapeDtypeStruct((nz, nx, CORES, nb, vrows // nb, bins), BF16),
        ],
        [pltpu.SemaphoreType.DMA((len(keys),)), pltpu.SemaphoreType.DMA((len(keys),))],
        1,
        codebook.reshape(nb, rows // nb, width),
        value_weight.reshape(nb, vrows // nb, bins),
    )
    return cb_out.reshape(nf * rows, width), vw_out.reshape(nf * vrows, bins)


def gather_grads(nb, nf, pre_grad, active, delta_t, value_delta):
    nz, nx = PLANES, nf // (PLANES * CORES)
    rows, width = pre_grad.shape
    bins = value_delta.shape[1]
    half = delta_t.shape[1]
    hops = [(0, 0)] + steps(nz)
    keys = [("c", 0)]
    for hop in hops:
        if hop[1]:
            keys += [("z", hop), ("cz", hop)]
        for dx in range(1, nx):
            keys += [("x", hop, dx), ("cx", hop, dx)]
    keys += [(k, dy) for dy in range(1, nb) for k in ("act", "delta", "value")]

    def kernel(pg, act, dt, vd, pg_out, act_out, dt_out, vd_out, send_sem, recv_sem):
        p = Place(nb, nf)
        p.barrier()
        s = Sends(send_sem, recv_sem, keys, p)
        here, like = pg_out.at[p.z, p.x, p.c], pg_out.at[0, 0, 0]
        mine = pl.ds(pl.multiple_of(p.b * rows, rows), rows)
        for way in (1, -1):

            @s.only(lambda way=way: feeds(p, way))
            def _(way=way):
                s.go(("z", (way, 1)), pg, here, p.dev(z=p.z + way), like)

        for dx in range(1, nx):
            s.go(("x", (0, 0), dx), pg, here, p.dev(x=p.xx(dx)))
        for dy in range(1, nb):
            to = p.bb(dy)
            s.go(("act", dy), act, act_out.at[p.b], p.dev(b=to))
            s.go(("delta", dy), dt.at[to], dt_out.at[:, mine], p.dev(b=to))
            s.go(("value", dy), vd, vd_out.at[p.b], p.dev(b=to))
        s.go(("c", 0), pg, here, p.dev(c=1 - p.c))
        pg_out[p.z, p.x, p.c] = pg[...]
        act_out[p.b] = act[...]
        dt_out[:, mine] = dt[p.b]
        vd_out[p.b] = vd[...]

        def from_z(hop):
            way, far = hop
            ref = pg_out.at[p.z - way * far, p.x, p.c]
            s.arrived(("z", hop))
            if far + 1 < nz:

                @s.only(lambda way=way: feeds(p, way))
                def _():
                    s.go(("z", (way, far + 1)), ref, ref, p.dev(z=p.z + way), like)

            for dx in range(1, nx):
                s.go(("x", hop, dx), ref, ref, p.dev(x=p.xx(dx)), like)
            s.go(("cz", hop), ref, ref, p.dev(c=1 - p.c), like)

        def from_plane(hop):
            way, far = hop
            for dx in range(1, nx):
                s.arrived(("x", hop, dx))
                ref = pg_out.at[p.z - way * far, p.xx(-dx), p.c]
                s.go(("cx", hop, dx), ref, ref, p.dev(c=1 - p.c), like)

        def from_core(hop):
            for key in keys:
                if key[0] in ("cz", "cx") and key[1] == hop:
                    s.arrived(key)

        def under(hop, f):
            if hop[1]:
                s.only(lambda: has(p, *hop))(lambda: f(hop))
            else:
                f(hop)

        for far in range(nz + 1):
            for hop in hops:
                if far and hop[1] == far:
                    under(hop, from_z)
            for hop in hops:
                if hop[1] == far - 1:
                    under(hop, from_plane)
        for key in keys:
            if key[0] in ("act", "delta", "value", "c"):
                s.arrived(key)
        for hop in hops:
            under(hop, from_core)
        s.finish()

    pieces, act_all, dt_all, vd_all = call(
        kernel,
        [
            jax.ShapeDtypeStruct((nz, nx, CORES, rows, width), BF16),
            jax.ShapeDtypeStruct((nb, rows, width), BF16),
            jax.ShapeDtypeStruct((half, nb * rows), BF16),
            jax.ShapeDtypeStruct((nb, rows, bins), BF16),
        ],
        [pltpu.SemaphoreType.DMA((len(keys),)), pltpu.SemaphoreType.DMA((len(keys),))],
        2,
        pre_grad,
        active,
        delta_t,
        value_delta,
    )
    return (
        pieces.reshape(nf * rows, width),
        act_all.reshape(nb * rows, width),
        dt_all,
        vd_all.reshape(nb * rows, bins),
    )


def reduce_grads(nb, nf, trunk, proj_weight, pieces, code, value):
    nz, nx = PLANES, nf // (PLANES * CORES)
    depth = trunk.shape[0]
    width = pieces.shape[1]
    block = next(n for n in (192, 96, 64, 32, 16) if depth % n == 0)
    blocks = depth // block
    lanes = 256
    cuts = 2 if code.shape[3] % 32 == 0 else 1
    crows = code.shape[3] // cuts
    fused = len(value) == 2
    bins = value[-1].shape[-1]
    vrows = width // (nf * nb) if fused else value[0].shape[4]
    chunks = range(cuts + 1)
    keys = [("p", i, dy) for i in range(blocks) for dy in range(1, nb)]
    for a in chunks:
        keys += [(a, "c")] + [(a, "x", d) for d in range(1, nx)]
        keys += [(a, "z", d) for d in range(1, nz)] + [(a, "y", d) for d in range(1, nb)]

    def kernel(tr, pw, pg, cd, *rest):
        factors, rest = rest[: len(value)], rest[len(value) :]
        (tr_out, pj_out, cd_out, vl_out), rest = rest[:4], rest[4:]
        send_sem, recv_sem = rest[-2:]
        vl = rest[-3] if fused else factors[0]
        p = Place(nb, nf)
        p.barrier()
        s = Sends(send_sem, recv_sem, keys, p)
        arrays = []
        for a in chunks:
            if a < cuts:
                part = pl.ds(a * crows, crows)
                own, out = cd.at[:, :, :, part], cd_out.at[:, part]
            else:
                own, out = vl.at[:, :, :, p.b], vl_out
            arrays.append((a, own, out) + tuple(rest[6 * a : 6 * a + 6]))
        for a, own, out, core, *_ in arrays:
            if a == cuts and fused:
                product = lax.dot_general(
                    factors[0][...],
                    factors[1][...],
                    (((0,), (0,)), ((), ())),
                    preferred_element_type=F32,
                )
                vl[...] = product.astype(BF16).reshape(nz, nx, CORES, nb, vrows, bins)
            s.go((a, "c"), own.at[:, :, 1 - p.c], core, p.dev(c=1 - p.c))

        def multiply(i):
            rows = pl.ds(i * block, block)

            def tile(n, carry):
                cols = pl.ds(pl.multiple_of(n * lanes, lanes), lanes)
                pj_out[p.b, rows, cols] = jnp.dot(
                    tr[rows, :], pg[:, cols], preferred_element_type=F32
                ).astype(BF16)
                return carry

            lax.fori_loop(0, width // lanes, tile, 0)
            for dy in range(1, nb):
                ref = pj_out.at[p.b, rows]
                s.go(("p", i, dy), ref, ref, p.dev(b=p.bb(dy)))

        def columns(n, carry):
            cols = pl.ds(pl.multiple_of(n * lanes, lanes), lanes)
            tr_out[:, cols] = lax.dot_general(
                pw[...], pg[cols, :], (((1,), (1,)), ((), ())), preferred_element_type=F32
            ).astype(BF16)
            return carry

        multiply(0)
        for a, own, out, core, xin, xsend, acc, zin, zsend in arrays:
            s.arrived((a, "c"))
            for dx in range(1, nx):
                x = p.xx(dx)
                for z in range(nz):
                    both = own[z, x, p.c].astype(F32) + core[z, x].astype(F32)
                    xsend[dx - 1, z] = both.astype(BF16)
                s.go((a, "x", dx), xsend.at[dx - 1], xin.at[dx - 1], p.dev(x=x))
            for z in range(nz):
                acc[z] = own[z, p.x, p.c].astype(F32) + core[z, p.x].astype(F32)
        for i in range(1, blocks):
            multiply(i)
        for a, own, out, core, xin, xsend, acc, zin, zsend in arrays:
            for dx in range(1, nx):
                s.arrived((a, "x", dx))
                acc[...] += xin[dx - 1].astype(F32)
            for dz in [2, 1, 3]:
                z = p.zz(dz)
                zsend[dz - 1] = acc[z].astype(BF16)
                s.go((a, "z", dz), zsend.at[dz - 1], zin.at[dz - 1], p.dev(z=z))
        for a, own, out, core, xin, xsend, acc, zin, zsend in arrays:
            if a == 0:
                lax.fori_loop(0, pieces.shape[0] // lanes, columns, 0)
            total = acc[p.z]
            for dz in range(1, nz):
                s.arrived((a, "z", dz))
                total = total + zin[dz - 1].astype(F32)
            out[p.b] = total.astype(BF16)
            for dy in range(1, nb):
                s.go((a, "y", dy), out.at[p.b], out.at[p.b], p.dev(b=p.bb(dy)))
        for key in keys:
            if key[0] == "p" or key[1] == "y":
                s.arrived(key)
        s.finish()

    def buffers(r, k):
        return [
            pltpu.VMEM((nz, nx, r, k), BF16),
            pltpu.VMEM((max(nx - 1, 1), nz, r, k), BF16),
            pltpu.VMEM((max(nx - 1, 1), nz, r, k), BF16),
            pltpu.VMEM((nz, r, k), F32),
            pltpu.VMEM((nz - 1, r, k), BF16),
            pltpu.VMEM((nz - 1, r, k), BF16),
        ]

    return call(
        kernel,
        [
            jax.ShapeDtypeStruct((depth, pieces.shape[0]), BF16),
            jax.ShapeDtypeStruct((nb, depth, width), BF16),
            jax.ShapeDtypeStruct((nb, crows * cuts, width), BF16),
            jax.ShapeDtypeStruct((nb, vrows, bins), BF16),
        ],
        buffers(crows, width) * cuts
        + buffers(vrows, bins)
        + [pltpu.VMEM((nz, nx, CORES, nb, vrows, bins), BF16)] * fused
        + [pltpu.SemaphoreType.DMA((len(keys),)), pltpu.SemaphoreType.DMA((len(keys),))],
        3,
        trunk,
        proj_weight,
        pieces,
        code,
        *value,
    )


def dot(a, b, dims):
    return lax.dot_general(a, b, (dims, ((), ())), preferred_element_type=F32)


class Slots(Sends):
    def __init__(self, send_sem, recv_sem, send_at, recv_at, place):
        super().__init__(send_sem, recv_sem, (), place)
        self.send_at, self.recv_at = send_at, recv_at

    def make(self, key, src, dst, dev):
        return pltpu.make_async_remote_copy(
            src_ref=src,
            dst_ref=dst,
            send_sem=self.send_sem.at[self.send_at[key]],
            recv_sem=self.recv_sem.at[self.recv_at[key]],
            device_id=dev,
            device_id_type=MESH,
        )


def number(keys, first, apart=()):
    at, names = {}, {}
    for key in keys:
        name = key
        if key[0] not in apart:
            name = tuple((0, k[1]) if isinstance(k, tuple) and k[1] > 1 else k for k in key)
        at[key] = first + names.setdefault(name, len(names))
    return at, first + len(names)


def fits(nb, nf, codebook, value_weight, depth, pos):
    nx = nf // (PLANES * CORES)
    rows, width = codebook.shape
    vrows = value_weight.shape[0]
    half, vhalf = rows // nb, vrows // nb
    return (
        nb * half == rows
        and nb * vhalf == vrows
        and half % 64 == 0
        and vhalf % 32 == 0
        and CORES * rows == 256
        and nx * CORES * vrows == 256
        and width == PLANES * 256
        and depth % 192 == 0
        and pos * CORES == 256
    )


ORDER = (
    ("pg", 0), ("pg", 1), ("pg", 2), ("pg", 3), ("z", 1, 1),
    ("z", 2, 1), ("z", 0, 1), ("z", 1, 2), ("z", 2, 2), ("z", 3, 1),
    ("z", 1, 3), ("x", 1, 1), ("x", 2, 1), ("x", 0, 0), ("code",),
    ("z", 2, 3), ("z", 0, 2), ("x", 1, 3), ("rsx", 0), ("zx", 0, 1),
    ("x", 2, 0), ("x", 2, 2), ("rsx", 1), ("x", 2, 3), ("z", 0, 3),
    ("x", 3, 0), ("x", 1, 0), ("proj", 2), ("x", 1, 2), ("val",),
    ("zx", 0, 2), ("zx", 0, 3), ("x", 3, 1), ("z", 3, 2), ("rsz", 0),
    ("proj", 1), ("proj", 0), ("z", 3, 3), ("rsx", 2), ("rsz", 1),
    ("x", 3, 2), ("x", 3, 3), ("proj", 3), ("rsz", 2), ("rsy", 0),
    ("fin", 2), ("rsy", 1), ("fin", 0), ("fin", 1), ("fin", 3),
    ("rsy", 2), ("col",),
)
CROSS_FIRST = (0,)


def fused(nb, nf, trunk, pre_act, proj_weight, codebook, value_weight, target, low, frac):
    nz, nx = PLANES, nf // (PLANES * CORES)
    pos, width = pre_act.shape
    rows, vrows = codebook.shape[0], value_weight.shape[0]
    bins = value_weight.shape[1]
    depth, total_pos = trunk.shape
    codes = nf * rows
    half, vhalf = rows // nb, vrows // nb
    cw = 256
    pieces = width // cw
    cuts = 2
    ck = half // cuts
    hops = [(0, 0)] + steps(nz)
    by_far = [[h for h in hops if h[1] == far] for far in range(nz)]

    early = []
    for hop in hops:
        early += [("core", k, hop) for k in range(2)]
        for a in range(3):
            if hop[1]:
                early += [("z", a, hop)] + [("y", a, hop, dy) for dy in range(1, nb)]
            for dx in range(1, nx):
                early += [("x", a, hop, dx)] + [("d", a, hop, dx, dy) for dy in range(1, nb)]
    swap = [(k, dy) for dy in range(1, nb) for k in ("act", "delta", "value")]
    late = []
    for n in range(pieces):
        for hop in hops:
            late += [("gc", n, hop)]
            if hop[1]:
                late += [("gz", n, hop)]
            if hop[1] == 0 or n not in CROSS_FIRST:
                late += [("gx", n, hop, dx) for dx in range(1, nx)]
            else:
                late += [("gzx", n, hop, dx) for dx in range(1, nx)]
        late += [("p", n, dy) for dy in range(1, nb)]
    for a in range(cuts + 1):
        late += [("rc", a)] + [("rx", a, d) for d in range(1, nx)]
        late += [("rz", a, d) for d in range(1, nz)] + [("ry", a, d) for d in range(1, nb)]
    swap_at, base = number(swap, 0)
    early_send, sends = number(early, base, ("z",))
    early_recv, recvs = number(early, base)
    late_send, last = number(late, base, ("gz", "gzx"))
    sends = max(sends, last)
    late_recv, recvs = number(late, recvs)
    early_send.update(swap_at)
    early_recv.update(swap_at)
    late_send.update(swap_at)
    late_recv.update(swap_at)

    def kernel(
        pre_in,
        cb_in,
        vw_in,
        tgt_in,
        lo_in,
        fr_in,
        tr_in,
        pw_in,
        trg,
        pj,
        cd,
        vl,
        cb,
        vw,
        pre,
        tgt,
        lo,
        fr,
        tr,
        pw,
        cb_all,
        vw_all,
        gate,
        act_all,
        logit,
        top,
        vlog,
        delta,
        delta_t,
        vd_all,
        dt_all,
        pg,
        part,
        vpart,
        pj_all,
        cd_all,
        vl_all,
        *rest,
    ):
        local_sem, send_sem, recv_sem = rest[-3:]
        p = Place(nb, nf)
        inputs = (cb_in, vw_in, pre_in, tgt_in, lo_in, fr_in, tr_in, pw_in)
        loads = [
            pltpu.make_async_copy(src, dst, local_sem.at[i])
            for i, (src, dst) in enumerate(zip(inputs, (cb, vw, pre, tgt, lo, fr, tr, pw)))
        ]
        for load in loads:
            load.start()
        p.barrier()
        for load in loads[:3]:
            load.wait()
        s = Slots(send_sem, recv_sem, early_send, early_recv, p)
        g = Slots(send_sem, recv_sem, late_send, late_recv, p)

        def under(s, far, f):
            for hop in by_far[far]:
                if far:
                    s.only(lambda hop=hop: has(p, *hop))(lambda: f(hop))
                else:
                    f(hop)

        sub = half // 2
        shards = (
            (0, vw, vw_all, vrows, vhalf, 0, vhalf),
            (1, cb, cb_all, rows, half, 0, sub),
            (2, cb, cb_all, rows, half, sub, sub),
        )

        def spot(shard, z, x, h):
            a, own, out, per, piece, skip, size = shard
            return out.at[z, x, p.c, pl.ds(pl.multiple_of(h * piece + skip, size), size)]

        def mine(shard, h):
            a, own, out, per, piece, skip, size = shard
            return own.at[pl.ds(pl.multiple_of(h * piece + skip, size), size)]

        def whole(shard):
            a, own, out, per, piece, skip, size = shard
            return lambda: out.at[0, 0, 0, pl.ds(0, size)]

        def relay(key, shard, at_z, at_x, at_h, **to):
            ref = spot(shard, at_z, at_x, at_h)
            s.go(key, ref, ref, p.dev(**to), whole(shard))

        for shard in shards:
            a = shard[0]
            here = spot(shard, p.z, p.x, p.b)
            for way in (1, -1):

                @s.only(lambda way=way: feeds(p, way))
                def _():
                    s.go(("z", a, (way, 1)), mine(shard, p.b), here, p.dev(z=p.z + way), whole(shard))

            for dx in range(1, nx):
                s.go(("x", a, (0, 0), dx), mine(shard, p.b), here, p.dev(x=p.xx(dx)), whole(shard))
        cb_all[p.z, p.x, p.c] = cb[...]
        vw_all[p.z, p.x, p.c] = vw[...]

        def activate(i, carry):
            cols = pl.ds(pl.multiple_of(i * cw, cw), cw)
            v = pre[:, cols].astype(F32)
            sigma = jax.nn.sigmoid(v)
            act_all[p.b, :, cols] = (v * sigma).astype(BF16)
            gate[:, cols] = sigma * (1.0 + v * (1.0 - sigma))
            return carry

        lax.fori_loop(0, width // cw, activate, 0)
        top[...] = jnp.full(top.shape, -jnp.inf, F32)
        vlog[...] = jnp.zeros(vlog.shape, F32)

        def from_z(shard, hop):
            a = shard[0]
            way, far = hop
            z = p.z - way * far
            s.arrived(("z", a, hop))
            if far + 1 < nz:

                @s.only(lambda way=way: feeds(p, way))
                def _():
                    relay(("z", a, (way, far + 1)), shard, z, p.x, p.b, z=p.z + way)

            for dx in range(1, nx):
                relay(("x", a, hop, dx), shard, z, p.x, p.b, x=p.xx(dx))
            for dy in range(1, nb):
                relay(("y", a, hop, dy), shard, z, p.x, p.b, b=p.bb(dy))

        def from_plane(shard, hop):
            a = shard[0]
            way, far = hop
            z = p.z - way * far
            for dx in range(1, nx):
                s.arrived(("x", a, hop, dx))
                if far % 2 == 0:
                    for dy in range(1, nb):
                        relay(("d", a, hop, dx, dy), shard, z, p.xx(-dx), p.b, b=p.bb(dy))
            if far:
                for dy in range(1, nb):
                    s.arrived(("y", a, hop, dy))
                    if far % 2:
                        for dx in range(1, nx):
                            relay(("d", a, hop, dx, dy), shard, z, p.x, p.bb(-dy), x=p.xx(dx))

        def from_diagonal(hop):
            way, far = hop
            for shard in shards:
                for dx in range(1, nx):
                    for dy in range(1, nb):
                        s.arrived(("d", shard[0], hop, dx, dy))
            for k, out in enumerate((cb_all, vw_all)):
                ref = out.at[p.z - way * far, :, p.c]
                s.go(("core", k, hop), ref, ref, p.dev(c=1 - p.c), lambda out=out: out.at[0, :, 0])

        def from_core(hop):
            for k in range(2):
                s.arrived(("core", k, hop))

        def near(j):
            up = (0, 1, 2, 3)[j], (1, 0, 2, 3)[j], (2, 3, 1, 0)[j], (3, 2, 1, 0)[j]
            z = jnp.where(p.z == 0, up[0], up[3])
            z = jnp.where(p.z == 1, up[1], z)
            return jnp.where(p.z == 2, up[2], z)

        def score(j):
            z = near(j)

            def tile(i, carry):
                at = pl.ds(pl.multiple_of((z * nx + i) * 256, 256), 256)
                block = dot(cb_all[z, i].reshape(256, width), act_all[p.b], ((1,), (1,)))
                logit[at, :] = block
                top[...] = jnp.maximum(top[...], jnp.max(block, axis=0, keepdims=True))
                return carry

            lax.fori_loop(0, nx, tile, 0)
            at = pl.ds(pl.multiple_of(z * 256, 256), 256)
            vlog[...] += dot(act_all[p.b, :, at], vw_all[z].reshape(256, bins), ((1,), (0,)))

        for far in range(nz + 3):
            for shard in shards:
                if 1 <= far < nz:
                    under(s, far, lambda hop: from_z(shard, hop))
                if 1 <= far <= nz:
                    under(s, far - 1, lambda hop: from_plane(shard, hop))
            if 2 <= far < nz + 2:
                under(s, far - 2, from_diagonal)
            if far == nz:
                for dy in range(1, nb):
                    ref = act_all.at[p.b]
                    g.go(("act", dy), ref, ref, p.dev(b=p.bb(dy)))
            if far >= 3:
                under(s, far - 3, from_core)
                score(far - 3)

        for load in loads[3:6]:
            load.wait()
        high = jnp.max(vlog[...], axis=1, keepdims=True)
        grown = jnp.exp(vlog[...] - high)
        probs = grown * (1.0 / jnp.sum(grown, axis=1, keepdims=True))
        ids = lax.broadcasted_iota(jnp.int32, (pos, bins), 1).astype(F32)
        column = jnp.broadcast_to(lo[...].astype(F32), (pos, pos)).T[:, :1]
        share = jnp.broadcast_to(fr[...].astype(F32) / 1024.0, (pos, pos)).T[:, :1]
        want = jnp.where(ids == column, 1.0 - share, 0.0)
        want = want + jnp.where(ids == column + 1.0, share, 0.0)
        vd_all[p.b] = (probs - want).astype(BF16)
        for dy in range(1, nb):
            ref = vd_all.at[p.b]
            g.go(("value", dy), ref, ref, p.dev(b=p.bb(dy)))

        blocks = codes // 256
        best = top[...]

        def grow(i, total):
            at = pl.ds(pl.multiple_of(i * 256, 256), 256)
            e = jnp.exp(logit[at, :] - best)
            logit[at, :] = e
            return total + jnp.sum(e, axis=0, keepdims=True)

        scale = 1.0 / lax.fori_loop(0, blocks, grow, jnp.zeros((1, pos), F32))
        group = 256 // rows
        code_ids = lax.broadcasted_iota(jnp.int32, (256, pos), 0)

        def differ(i, carry):
            at = pl.ds(pl.multiple_of(i * 256, 256), 256)
            hot = jnp.where(code_ids + i * 256 == tgt[...], 1.0, 0.0)
            d = logit[at, :] * scale - hot
            delta[:, at] = d.T.astype(BF16)
            delta_t[pl.ds(i * group, group)] = d.astype(BF16).reshape(group, nb, half, pos)
            return carry

        lax.fori_loop(0, blocks, differ, 0)
        lanes = pl.ds(pl.multiple_of(p.b * pos, pos), pos)
        for dy in range(1, nb):
            to = p.bb(dy)
            g.go(("delta", dy), delta_t.at[:, to], dt_all.at[:, :, lanes], p.dev(b=to))
        dt_all[:, :, lanes] = delta_t[:, p.b]
        s.finish()

        def pass_on(n, at_z, at_x, key, **to):
            ref = pg.at[n, at_z, at_x, p.c]
            g.go(key, ref, ref, p.dev(**to), lambda: pg.at[n, 0, 0, 0])

        def onward(n, kind, z, x, far, extra, ways):
            for way in ways:

                @g.only(lambda way=way: feeds(p, way))
                def _():
                    pass_on(n, z, x, (kind, n, (way, far)) + extra, z=p.z + way)

        def across(n, hop):
            for dx in range(1, nx):
                pass_on(n, p.z - hop[0] * hop[1], p.x, ("gx", n, hop, dx), x=p.xx(dx))

        def to_core(n, hop):
            ref = pg.at[n, p.z - hop[0] * hop[1], :, p.c]
            g.go(("gc", n, hop), ref, ref, p.dev(c=1 - p.c), lambda: pg.at[n, 0, :, 0])

        def head(n):
            cols = pl.ds(n * cw, cw)
            back = dot(delta[...], cb_all[:, :, :, :, cols].reshape(codes, cw), ((1,), (0,)))
            back = back + dot(vd_all[p.b], vw_all[n].reshape(cw, bins), ((1,), (1,)))
            pg[n, p.z, p.x, p.c] = (back * gate[:, cols]).astype(BF16)
            if n in CROSS_FIRST:
                across(n, (0, 0))
            onward(n, "gz", p.z, p.x, 1, (), (1, -1))
            if n not in CROSS_FIRST:
                across(n, (0, 0))

        def grad_z(n, far):
            def run(hop):
                z = p.z - hop[0] * far
                g.arrived(("gz", n, hop))
                if far + 1 < nz:
                    onward(n, "gz", z, p.x, far + 1, (), hop[:1])
                if n not in CROSS_FIRST:
                    across(n, hop)

            under(g, far, run)

        def grad_x(n, far):
            def run(hop):
                for dx in range(1, nx):
                    g.arrived(("gx", n, hop, dx))
                    if n in CROSS_FIRST:
                        onward(n, "gzx", p.z, p.xx(-dx), 1, (dx,), (1, -1))
                to_core(n, hop)

            under(g, far, run)

        def grad_zx(n, far):
            def run(hop):
                for dx in range(1, nx):
                    g.arrived(("gzx", n, hop, dx))
                    if far + 1 < nz:
                        onward(n, "gzx", p.z - hop[0] * far, p.xx(-dx), far + 1, (dx,), hop[:1])
                to_core(n, hop)

            under(g, far, run)

        arrays = []
        for a in range(cuts + 1):
            if a < cuts:
                own, out = part.at[:, :, :, pl.ds(a * ck, ck)], cd_all.at[:, pl.ds(a * ck, ck)]
            else:
                own, out = vpart.at[:, :, :, p.b], vl_all
            arrays.append((own, out) + tuple(rest[6 * a : 6 * a + 6]))
        deep = nb * pos

        def to_sum(a):
            own, out, core, *_ = arrays[a]
            g.go(("rc", a), own.at[:, :, 1 - p.c], core, p.dev(c=1 - p.c))

        def code():
            for dy in range(1, nb):
                g.arrived(("act", dy))
                g.arrived(("delta", dy))

            def block(i, carry):
                z = i // (width // cw)
                cols = pl.ds(pl.multiple_of((i % (width // cw)) * cw, cw), cw)
                left = dt_all[pl.ds(z * nx * CORES, nx * CORES)].reshape(nx * CORES * half, deep)
                right = act_all[:, :, cols].reshape(deep, cw)
                product = dot(left, right, ((1,), (0,)))
                part[z, :, :, :, cols] = product.astype(BF16).reshape(nx, CORES, half, cw)
                return carry

            lax.fori_loop(0, nz * (width // cw), block, 0)
            for a in range(cuts):
                to_sum(a)

        def val():
            for dy in range(1, nb):
                g.arrived(("value", dy))

            def block(z, carry):
                cols = pl.ds(pl.multiple_of(z * 256, 256), 256)
                left = act_all[:, :, cols].reshape(deep, 256)
                product = dot(left, vd_all[...].reshape(deep, bins), ((0,), (0,)))
                vpart[z] = product.astype(BF16).reshape(nx, CORES, nb, vhalf, bins)
                return carry

            lax.fori_loop(0, nz, block, 0)
            to_sum(cuts)

        def rsx(a):
            own, out, core, xin, xsend, acc, zin, zsend = arrays[a]
            g.arrived(("rc", a))
            for dx in range(1, nx):
                x = p.xx(dx)
                for z in range(nz):
                    both = own[z, x, p.c].astype(F32) + core[z, x].astype(F32)
                    xsend[dx - 1, z] = both.astype(BF16)
                g.go(("rx", a, dx), xsend.at[dx - 1], xin.at[dx - 1], p.dev(x=x))
            for z in range(nz):
                acc[z] = own[z, p.x, p.c].astype(F32) + core[z, p.x].astype(F32)

        def rsz(a):
            own, out, core, xin, xsend, acc, zin, zsend = arrays[a]
            for dx in range(1, nx):
                g.arrived(("rx", a, dx))
                acc[...] += xin[dx - 1].astype(F32)
            for dz in [2, 1, 3]:
                z = p.zz(dz)
                zsend[dz - 1] = acc[z].astype(BF16)
                g.go(("rz", a, dz), zsend.at[dz - 1], zin.at[dz - 1], p.dev(z=z))

        def rsy(a):
            own, out, core, xin, xsend, acc, zin, zsend = arrays[a]
            total = acc[p.z]
            for dz in range(1, nz):
                g.arrived(("rz", a, dz))
                total = total + zin[dz - 1].astype(F32)
            out[p.b] = total.astype(BF16)
            for dy in range(1, nb):
                g.go(("ry", a, dy), out.at[p.b], out.at[p.b], p.dev(b=p.bb(dy)))

        def proj(n):
            for far in range(nz):
                under(g, far, lambda hop: g.arrived(("gc", n, hop)))

            def block(i, carry):
                at = pl.ds(pl.multiple_of(i * 192, 192), 192)
                pj_all[p.b, n, at, :] = jnp.dot(
                    tr[at, :], pg[n].reshape(total_pos, cw), preferred_element_type=F32
                ).astype(BF16)
                return carry

            lax.fori_loop(0, depth // 192, block, 0)
            for dy in range(1, nb):
                ref = pj_all.at[p.b, n]
                g.go(("p", n, dy), ref, ref, p.dev(b=p.bb(dy)))

        def col():
            def block(i, carry):
                at = pl.ds(pl.multiple_of(i * 256, 256), 256)
                z, x = i // nx, i % nx
                total = 0.0
                for n in range(pieces):
                    there = pg[n, z, x].reshape(256, cw)
                    total = total + dot(pw[:, pl.ds(n * cw, cw)], there, ((1,), (1,)))
                trg[:, at] = total.astype(BF16)
                return carry

            lax.fori_loop(0, nz * nx, block, 0)

        def fin(n):
            for dy in range(1, nb):
                g.arrived(("p", n, dy))
            total = pj_all[0, n].astype(F32)
            for b in range(1, nb):
                total = total + pj_all[b, n].astype(F32)
            pj[:, pl.ds(n * cw, cw)] = total

        for load in loads[6:]:
            load.wait()
        acts = dict(
            pg=head, z=grad_z, x=grad_x, zx=grad_zx, code=code, val=val, rsx=rsx, rsz=rsz, rsy=rsy,
            proj=proj, col=col, fin=fin,
        )
        for name, *where in ORDER:
            acts[name](*where)
        for a in range(cuts + 1):
            for dy in range(1, nb):
                g.arrived(("ry", a, dy))
        for b in range(nb):
            cd[pl.ds(b * half, half), :] = cd_all[b].astype(F32)
            vl[pl.ds(b * vhalf, vhalf), :] = vl_all[b].astype(F32)
        g.finish()

    def buffers(r, k):
        return [
            pltpu.VMEM((nz, nx, r, k), BF16),
            pltpu.VMEM((max(nx - 1, 1), nz, r, k), BF16),
            pltpu.VMEM((max(nx - 1, 1), nz, r, k), BF16),
            pltpu.VMEM((nz, r, k), F32),
            pltpu.VMEM((nz - 1, r, k), BF16),
            pltpu.VMEM((nz - 1, r, k), BF16),
        ]

    anywhere = pl.BlockSpec(memory_space=pl.ANY)
    stay = pl.BlockSpec(memory_space=pltpu.HBM)
    results = pl.pallas_call(
        kernel,
        out_shape=[
            jax.ShapeDtypeStruct((depth, total_pos), BF16),
            jax.ShapeDtypeStruct((depth, width), F32),
            jax.ShapeDtypeStruct((rows, width), F32),
            jax.ShapeDtypeStruct((vrows, bins), F32),
        ],
        in_specs=[stay] * 8,
        out_specs=[pl.BlockSpec(memory_space=pltpu.VMEM)] * 4,
        scratch_shapes=[
            pltpu.VMEM((rows, width), BF16),
            pltpu.VMEM((vrows, bins), BF16),
            pltpu.VMEM((pos, width), BF16),
            pltpu.VMEM((1, pos), jnp.int32),
            pltpu.VMEM((1, pos), jnp.int32),
            pltpu.VMEM((1, pos), jnp.int32),
            pltpu.VMEM((depth, total_pos), BF16),
            pltpu.VMEM((depth, width), BF16),
            pltpu.VMEM((nz, nx, CORES, rows, width), BF16),
            pltpu.VMEM((nz, nx, CORES, vrows, bins), BF16),
            pltpu.VMEM((pos, width), F32),
            pltpu.VMEM((nb, pos, width), BF16),
            pltpu.VMEM((codes, pos), F32),
            pltpu.VMEM((1, pos), F32),
            pltpu.VMEM((pos, bins), F32),
            pltpu.VMEM((pos, codes), BF16),
            pltpu.VMEM((nf, nb, half, pos), BF16),
            pltpu.VMEM((nb, pos, bins), BF16),
            pltpu.VMEM((nf, half, nb * pos), BF16),
            pltpu.VMEM((pieces, nz, nx, CORES, pos, cw), BF16),
            pltpu.VMEM((nz, nx, CORES, half, width), BF16),
            pltpu.VMEM((nz, nx, CORES, nb, vhalf, bins), BF16),
            pltpu.VMEM((nb, pieces, depth, cw), BF16),
            pltpu.VMEM((nb, half, width), BF16),
            pltpu.VMEM((nb, vhalf, bins), BF16),
        ]
        + buffers(ck, width) * cuts
        + buffers(vhalf, bins)
        + [
            pltpu.SemaphoreType.DMA((8,)),
            pltpu.SemaphoreType.DMA((sends,)),
            pltpu.SemaphoreType.DMA((recvs,)),
        ],
        compiler_params=pltpu.CompilerParams(
            collective_id=4, has_side_effects=True, vmem_limit_bytes=44 << 20
        ),
    )(
        *(
            pltpu.with_memory_space_constraint(x, pltpu.HBM)
            for x in (
                pre_act, codebook, value_weight, target, low, frac, trunk, proj_weight,
            )
        )
    )

    def hand_over(*refs):
        copies = [
            pltpu.make_async_copy(refs[i], refs[4 + i], refs[8].at[i]) for i in range(4)
        ]
        for copy in copies:
            copy.start()
        for copy in copies:
            copy.wait()

    return pl.pallas_call(
        hand_over,
        out_shape=[jax.ShapeDtypeStruct(r.shape, r.dtype) for r in results],
        in_specs=[anywhere] * 4,
        out_specs=[stay] * 4,
        scratch_shapes=[pltpu.SemaphoreType.DMA((4,))],
        compiler_params=pltpu.CompilerParams(vmem_limit_bytes=1 << 20),
    )(*results)


def make_body(nb, nf):
    nz, nx = PLANES, nf // (PLANES * CORES)

    def body(
        trunk, pre_act, proj_weight, codebook, value_weight, code_target, value_bin, value_frac
    ):
        if fits(nb, nf, codebook, value_weight, trunk.shape[0], pre_act.shape[0]):
            row = (1, pre_act.shape[0])
            return fused(
                nb,
                nf,
                trunk,
                pre_act,
                proj_weight,
                codebook,
                value_weight,
                code_target.reshape(row),
                value_bin.reshape(row),
                value_frac.reshape(row),
            )
        all_codes, bins_weight = gather_weights(nb, nf, codebook, value_weight)
        rows, width = pre_act.shape
        num_codes = all_codes.shape[0]
        num_bins = bins_weight.shape[1]
        pre_value = pre_act.astype(F32)
        gate_sigma = jax.nn.sigmoid(pre_value)
        active = (pre_value * gate_sigma).astype(BF16)
        code_logits = jnp.einsum("rk,ck->rc", active, all_codes, preferred_element_type=F32)
        code_probs = jax.nn.softmax(code_logits, axis=-1)
        code_ids = lax.broadcasted_iota(jnp.int32, (1, num_codes), 1)
        one_hot = (code_target[:, None] == code_ids).astype(F32)
        code_delta = (code_probs - one_hot).astype(BF16)
        value_logits = jnp.dot(active, bins_weight, preferred_element_type=F32)
        value_probs = jax.nn.softmax(value_logits, axis=-1)
        bin_ids = lax.broadcasted_iota(jnp.int32, (1, num_bins), 1)
        fraction = value_frac.astype(F32)[:, None] / 1024.0
        target = jnp.where(bin_ids == value_bin[:, None], 1.0 - fraction, 0.0)
        target = target + jnp.where(bin_ids == value_bin[:, None] + 1, fraction, 0.0)
        value_delta = (value_probs - target).astype(BF16)
        backward = jnp.dot(code_delta, all_codes, preferred_element_type=F32)
        backward = backward + jnp.einsum(
            "rb,kb->rk", value_delta, bins_weight, preferred_element_type=F32
        )
        pre_grad = (backward * gate_sigma * (1.0 + pre_value * (1.0 - gate_sigma))).astype(BF16)
        own = codebook.shape[0] // nb
        delta_t = code_delta.T.reshape(nf, nb, own, rows).swapaxes(0, 1)
        delta_t = delta_t.reshape(nb, nf * own, rows)
        pieces, act_all, dt_all, vd_all = gather_grads(
            nb, nf, pre_grad, active, delta_t, value_delta
        )
        code_part = jnp.dot(dt_all, act_all, preferred_element_type=F32)
        code_part = code_part.astype(BF16).reshape(nz, nx, CORES, own, width)
        vown = value_weight.shape[0] // nb
        if vown % 16 == 0:
            value_part = (act_all, vd_all)
        else:
            value_part = jnp.einsum("rk,rb->kb", act_all, vd_all, preferred_element_type=F32)
            value_part = value_part.astype(BF16)
            value_part = (value_part.reshape(nz, nx, CORES, nb, vown, num_bins),)
        out_cols, proj_all, code_all, value_all = reduce_grads(
            nb, nf, trunk, proj_weight, pieces, code_part, value_part
        )
        proj_grad = jnp.sum(proj_all.astype(F32), axis=0)
        code_grad = code_all.reshape(nb * own, width).astype(F32)
        value_grad = value_all.reshape(nb * vown, num_bins).astype(F32)
        return (out_cols, proj_grad, code_grad, value_grad)

    return body


def solution(mesh):
    in_specs = (
        P("fsdp", "batch"),
        P(("batch", "fsdp"), None),
        P("fsdp", None),
        P("fsdp", None),
        P("fsdp", None),
        P(("batch", "fsdp")),
        P(("batch", "fsdp")),
        P(("batch", "fsdp")),
    )
    out_specs = (P("fsdp", "batch"), P("fsdp", None), P("fsdp", None), P("fsdp", None))
    body = make_body(mesh.shape["batch"], mesh.shape["fsdp"])
    return jax.shard_map(body, mesh=mesh, in_specs=in_specs, out_specs=out_specs, check_vma=False)
```

```python
import jax
import jax.numpy as jnp
from jax import lax
from jax.experimental import pallas as pl
from jax.experimental.pallas import tpu as pltpu
from jax.sharding import PartitionSpec as P

MESH = pl.DeviceIdType.MESH
BF16 = jnp.bfloat16
F32 = jnp.float32
CORES = 2
PLANES = 4


class Place:
    def __init__(self, nb, nf):
        self.nb, self.nz = nb, PLANES
        self.nx = nf // (PLANES * CORES)
        f = lax.axis_index("fsdp")
        self.b = lax.axis_index("batch")
        self.z = f // (self.nx * CORES)
        self.x = (f // CORES) % self.nx
        self.c = f % CORES

    def dev(self, b=None, z=None, x=None, c=None):
        b = self.b if b is None else b
        z = self.z if z is None else z
        x = self.x if x is None else x
        c = self.c if c is None else c
        return (b, (z * self.nx + x) * CORES + c)

    def zz(self, d):
        return lax.rem(self.z + d + self.nz, self.nz)

    def xx(self, d):
        return lax.rem(self.x + d + self.nx, self.nx)

    def bb(self, d):
        return lax.rem(self.b + d + self.nb, self.nb)

    def barrier(self):
        sem = pltpu.get_barrier_semaphore()
        peers = [self.dev(z=self.zz(d)) for d in range(1, self.nz)]
        peers += [self.dev(x=self.xx(d)) for d in range(1, self.nx)]
        peers += [self.dev(b=self.bb(d)) for d in range(1, self.nb)]
        peers += [self.dev(c=1 - self.c)]
        for peer in peers:
            pl.semaphore_signal(sem, inc=1, device_id=peer, device_id_type=MESH)
        pl.semaphore_wait(sem, len(peers))


def steps(nz):
    return [(way, far) for far in range(1, nz) for way in (1, -1)]


class Sends:
    def __init__(self, send_sem, recv_sem, keys, place):
        self.send_sem, self.recv_sem, self.place = send_sem, recv_sem, place
        self.at = {k: i for i, k in enumerate(keys)}
        self.like = {}
        self.started = []
        self.when = ()

    def make(self, key, src, dst, dev):
        i = self.at[key]
        return pltpu.make_async_remote_copy(
            src_ref=src,
            dst_ref=dst,
            send_sem=self.send_sem.at[i],
            recv_sem=self.recv_sem.at[i],
            device_id=dev,
            device_id_type=MESH,
        )

    def go(self, key, src, dst, dev, like=None):
        self.make(key, src, dst, dev).start()
        self.like[key] = dst if like is None else like
        self.started.append((key, self.when))

    def waiter(self, key):
        ref = self.like[key]
        ref = ref() if callable(ref) else ref
        return self.make(key, ref, ref, self.place.dev(c=1 - self.place.c))

    def arrived(self, key):
        self.waiter(key).wait_recv()

    def finish(self):
        for key, whens in self.started:

            def wait(key=key):
                self.waiter(key).wait_send()

            if whens:
                met = whens[0]()
                for when in whens[1:]:
                    met = jnp.logical_and(met, when())
                pl.when(met)(wait)
            else:
                wait()

    def only(self, when):
        def run(f):
            outer = self.when
            self.when = outer + (when,)

            @pl.when(when())
            def _():
                f()

            self.when = outer

        return run


def call(kernel, outs, scratch, cid, *args):
    return pl.pallas_call(
        kernel,
        out_shape=outs,
        in_specs=[pl.BlockSpec(memory_space=pltpu.VMEM)] * len(args),
        out_specs=[pl.BlockSpec(memory_space=pltpu.VMEM)] * len(outs),
        scratch_shapes=scratch,
        compiler_params=pltpu.CompilerParams(collective_id=cid, has_side_effects=True),
    )(*args)


def has(p, way, far):
    return p.z >= far if way == 1 else p.z + far < p.nz


def feeds(p, way):
    return p.z + 1 < p.nz if way == 1 else p.z >= 1


def gather_weights_keys(nb, nx, nz):
    keys = []
    for a in (0, 1):
        keys += [(a, "c", 0)]
        for hop in [(0, 0)] + steps(nz):
            if hop[1]:
                keys += [(a, "z", hop), (a, "cz", hop)]
                for dy in range(1, nb):
                    keys += [(a, "y", hop, dy), (a, "cy", hop, dy)]
            for dx in range(1, nx):
                keys += [(a, "x", hop, dx), (a, "cx", hop, dx)]
                for dy in range(1, nb):
                    keys += [(a, "d", hop, dx, dy), (a, "cd", hop, dx, dy)]
    return keys


def gather_weights(nb, nf, codebook, value_weight):
    nz, nx = PLANES, nf // (PLANES * CORES)
    keys = gather_weights_keys(nb, nx, nz)
    rows, width = codebook.shape
    vrows, bins = value_weight.shape

    def kernel(cb, vw, cb_out, vw_out, send_sem, recv_sem):
        p = Place(nb, nf)
        p.barrier()
        s = Sends(send_sem, recv_sem, keys, p)
        arrays = ((0, cb, cb_out), (1, vw, vw_out))

        def spot(out, z, x, h):
            return out.at[z, x, p.c, h]

        def relay(key, out, at_z, at_x, at_h, **to):
            ref = spot(out, at_z, at_x, at_h)
            s.go(key, ref, ref, p.dev(**to), lambda: out.at[0, 0, 0, 0])

        for a, own, out in arrays:
            here = spot(out, p.z, p.x, p.b)
            for way in (1, -1):

                @s.only(lambda way=way: feeds(p, way))
                def _(a=a, own=own, out=out, here=here, way=way):
                    s.go((a, "z", (way, 1)), own.at[p.b], here, p.dev(z=p.z + way), lambda: out.at[0, 0, 0, 0])

            for dx in range(1, nx):
                s.go((a, "x", (0, 0), dx), own.at[p.b], here, p.dev(x=p.xx(dx)))
            s.go((a, "c", 0), own, out.at[p.z, p.x, p.c], p.dev(c=1 - p.c))
        for a, own, out in arrays:
            out[p.z, p.x, p.c] = own[...]

        def from_z(hop):
            way, far = hop
            z = p.z - way * far
            for a, own, out in arrays:
                s.arrived((a, "z", hop))
                if far + 1 < nz:

                    @s.only(lambda way=way: feeds(p, way))
                    def _(a=a, out=out):
                        relay((a, "z", (way, far + 1)), out, z, p.x, p.b, z=p.z + way)

                for dx in range(1, nx):
                    relay((a, "x", hop, dx), out, z, p.x, p.b, x=p.xx(dx))
                for dy in range(1, nb):
                    relay((a, "y", hop, dy), out, z, p.x, p.b, b=p.bb(dy))
                relay((a, "cz", hop), out, z, p.x, p.b, c=1 - p.c)

        def from_plane(hop):
            way, far = hop
            z = p.z - way * far
            for a, own, out in arrays:
                for dx in range(1, nx):
                    x = p.xx(-dx)
                    s.arrived((a, "x", hop, dx))
                    if far % 2 == 0:
                        for dy in range(1, nb):
                            relay((a, "d", hop, dx, dy), out, z, x, p.b, b=p.bb(dy))
                    relay((a, "cx", hop, dx), out, z, x, p.b, c=1 - p.c)
                if far:
                    for dy in range(1, nb):
                        h = p.bb(-dy)
                        s.arrived((a, "y", hop, dy))
                        if far % 2:
                            for dx in range(1, nx):
                                relay((a, "d", hop, dx, dy), out, z, p.x, h, x=p.xx(dx))
                        relay((a, "cy", hop, dy), out, z, p.x, h, c=1 - p.c)

        def from_diagonal(hop):
            way, far = hop
            for a, own, out in arrays:
                for dx in range(1, nx):
                    for dy in range(1, nb):
                        s.arrived((a, "d", hop, dx, dy))
                        relay(
                            (a, "cd", hop, dx, dy),
                            out,
                            p.z - way * far,
                            p.xx(-dx),
                            p.bb(-dy),
                            c=1 - p.c,
                        )

        def from_core(hop):
            for key in keys:
                if key[1] in ("cz", "cx", "cy", "cd") and key[2] == hop:
                    s.arrived(key)

        def under(hop, f):
            if hop[1]:
                s.only(lambda: has(p, *hop))(lambda: f(hop))
            else:
                f(hop)

        hops = [(0, 0)] + steps(nz)
        by_far = [[h for h in hops if h[1] == far] for far in range(nz)]
        for far in range(nz + 2):
            if 1 <= far < nz:
                for hop in by_far[far]:
                    under(hop, from_z)
            if 1 <= far <= nz:
                for hop in by_far[far - 1]:
                    under(hop, from_plane)
            if far >= 2:
                for hop in by_far[far - 2]:
                    under(hop, from_diagonal)
        for a in (0, 1):
            s.arrived((a, "c", 0))
        for hop in hops:
            under(hop, from_core)
        s.finish()

    cb_out, vw_out = call(
        kernel,
        [
            jax.ShapeDtypeStruct((nz, nx, CORES, nb, rows // nb, width), BF16),
            jax.ShapeDtypeStruct((nz, nx, CORES, nb, vrows // nb, bins), BF16),
        ],
        [pltpu.SemaphoreType.DMA((len(keys),)), pltpu.SemaphoreType.DMA((len(keys),))],
        1,
        codebook.reshape(nb, rows // nb, width),
        value_weight.reshape(nb, vrows // nb, bins),
    )
    return cb_out.reshape(nf * rows, width), vw_out.reshape(nf * vrows, bins)


def gather_grads(nb, nf, pre_grad, active, delta_t, value_delta):
    nz, nx = PLANES, nf // (PLANES * CORES)
    rows, width = pre_grad.shape
    bins = value_delta.shape[1]
    half = delta_t.shape[1]
    hops = [(0, 0)] + steps(nz)
    keys = [("c", 0)]
    for hop in hops:
        if hop[1]:
            keys += [("z", hop), ("cz", hop)]
        for dx in range(1, nx):
            keys += [("x", hop, dx), ("cx", hop, dx)]
    keys += [(k, dy) for dy in range(1, nb) for k in ("act", "delta", "value")]

    def kernel(pg, act, dt, vd, pg_out, act_out, dt_out, vd_out, send_sem, recv_sem):
        p = Place(nb, nf)
        p.barrier()
        s = Sends(send_sem, recv_sem, keys, p)
        here, like = pg_out.at[p.z, p.x, p.c], pg_out.at[0, 0, 0]
        mine = pl.ds(pl.multiple_of(p.b * rows, rows), rows)
        for way in (1, -1):

            @s.only(lambda way=way: feeds(p, way))
            def _(way=way):
                s.go(("z", (way, 1)), pg, here, p.dev(z=p.z + way), like)

        for dx in range(1, nx):
            s.go(("x", (0, 0), dx), pg, here, p.dev(x=p.xx(dx)))
        for dy in range(1, nb):
            to = p.bb(dy)
            s.go(("act", dy), act, act_out.at[p.b], p.dev(b=to))
            s.go(("delta", dy), dt.at[to], dt_out.at[:, mine], p.dev(b=to))
            s.go(("value", dy), vd, vd_out.at[p.b], p.dev(b=to))
        s.go(("c", 0), pg, here, p.dev(c=1 - p.c))
        pg_out[p.z, p.x, p.c] = pg[...]
        act_out[p.b] = act[...]
        dt_out[:, mine] = dt[p.b]
        vd_out[p.b] = vd[...]

        def from_z(hop):
            way, far = hop
            ref = pg_out.at[p.z - way * far, p.x, p.c]
            s.arrived(("z", hop))
            if far + 1 < nz:

                @s.only(lambda way=way: feeds(p, way))
                def _():
                    s.go(("z", (way, far + 1)), ref, ref, p.dev(z=p.z + way), like)

            for dx in range(1, nx):
                s.go(("x", hop, dx), ref, ref, p.dev(x=p.xx(dx)), like)
            s.go(("cz", hop), ref, ref, p.dev(c=1 - p.c), like)

        def from_plane(hop):
            way, far = hop
            for dx in range(1, nx):
                s.arrived(("x", hop, dx))
                ref = pg_out.at[p.z - way * far, p.xx(-dx), p.c]
                s.go(("cx", hop, dx), ref, ref, p.dev(c=1 - p.c), like)

        def from_core(hop):
            for key in keys:
                if key[0] in ("cz", "cx") and key[1] == hop:
                    s.arrived(key)

        def under(hop, f):
            if hop[1]:
                s.only(lambda: has(p, *hop))(lambda: f(hop))
            else:
                f(hop)

        for far in range(nz + 1):
            for hop in hops:
                if far and hop[1] == far:
                    under(hop, from_z)
            for hop in hops:
                if hop[1] == far - 1:
                    under(hop, from_plane)
        for key in keys:
            if key[0] in ("act", "delta", "value", "c"):
                s.arrived(key)
        for hop in hops:
            under(hop, from_core)
        s.finish()

    pieces, act_all, dt_all, vd_all = call(
        kernel,
        [
            jax.ShapeDtypeStruct((nz, nx, CORES, rows, width), BF16),
            jax.ShapeDtypeStruct((nb, rows, width), BF16),
            jax.ShapeDtypeStruct((half, nb * rows), BF16),
            jax.ShapeDtypeStruct((nb, rows, bins), BF16),
        ],
        [pltpu.SemaphoreType.DMA((len(keys),)), pltpu.SemaphoreType.DMA((len(keys),))],
        2,
        pre_grad,
        active,
        delta_t,
        value_delta,
    )
    return (
        pieces.reshape(nf * rows, width),
        act_all.reshape(nb * rows, width),
        dt_all,
        vd_all.reshape(nb * rows, bins),
    )


def reduce_grads(nb, nf, trunk, proj_weight, pieces, code, value):
    nz, nx = PLANES, nf // (PLANES * CORES)
    depth = trunk.shape[0]
    width = pieces.shape[1]
    block = next(n for n in (192, 96, 64, 32, 16) if depth % n == 0)
    blocks = depth // block
    lanes = 256
    cuts = 2 if code.shape[3] % 32 == 0 else 1
    crows = code.shape[3] // cuts
    fused = len(value) == 2
    bins = value[-1].shape[-1]
    vrows = width // (nf * nb) if fused else value[0].shape[4]
    chunks = range(cuts + 1)
    keys = [("p", i, dy) for i in range(blocks) for dy in range(1, nb)]
    for a in chunks:
        keys += [(a, "c")] + [(a, "x", d) for d in range(1, nx)]
        keys += [(a, "z", d) for d in range(1, nz)] + [(a, "y", d) for d in range(1, nb)]

    def kernel(tr, pw, pg, cd, *rest):
        factors, rest = rest[: len(value)], rest[len(value) :]
        (tr_out, pj_out, cd_out, vl_out), rest = rest[:4], rest[4:]
        send_sem, recv_sem = rest[-2:]
        vl = rest[-3] if fused else factors[0]
        p = Place(nb, nf)
        p.barrier()
        s = Sends(send_sem, recv_sem, keys, p)
        arrays = []
        for a in chunks:
            if a < cuts:
                part = pl.ds(a * crows, crows)
                own, out = cd.at[:, :, :, part], cd_out.at[:, part]
            else:
                own, out = vl.at[:, :, :, p.b], vl_out
            arrays.append((a, own, out) + tuple(rest[6 * a : 6 * a + 6]))
        for a, own, out, core, *_ in arrays:
            if a == cuts and fused:
                product = lax.dot_general(
                    factors[0][...],
                    factors[1][...],
                    (((0,), (0,)), ((), ())),
                    preferred_element_type=F32,
                )
                vl[...] = product.astype(BF16).reshape(nz, nx, CORES, nb, vrows, bins)
            s.go((a, "c"), own.at[:, :, 1 - p.c], core, p.dev(c=1 - p.c))

        def multiply(i):
            rows = pl.ds(i * block, block)

            def tile(n, carry):
                cols = pl.ds(pl.multiple_of(n * lanes, lanes), lanes)
                pj_out[p.b, rows, cols] = jnp.dot(
                    tr[rows, :], pg[:, cols], preferred_element_type=F32
                ).astype(BF16)
                return carry

            lax.fori_loop(0, width // lanes, tile, 0)
            for dy in range(1, nb):
                ref = pj_out.at[p.b, rows]
                s.go(("p", i, dy), ref, ref, p.dev(b=p.bb(dy)))

        def columns(n, carry):
            cols = pl.ds(pl.multiple_of(n * lanes, lanes), lanes)
            tr_out[:, cols] = lax.dot_general(
                pw[...], pg[cols, :], (((1,), (1,)), ((), ())), preferred_element_type=F32
            ).astype(BF16)
            return carry

        multiply(0)
        for a, own, out, core, xin, xsend, acc, zin, zsend in arrays:
            s.arrived((a, "c"))
            for dx in range(1, nx):
                x = p.xx(dx)
                for z in range(nz):
                    both = own[z, x, p.c].astype(F32) + core[z, x].astype(F32)
                    xsend[dx - 1, z] = both.astype(BF16)
                s.go((a, "x", dx), xsend.at[dx - 1], xin.at[dx - 1], p.dev(x=x))
            for z in range(nz):
                acc[z] = own[z, p.x, p.c].astype(F32) + core[z, p.x].astype(F32)
        for i in range(1, blocks):
            multiply(i)
        for a, own, out, core, xin, xsend, acc, zin, zsend in arrays:
            for dx in range(1, nx):
                s.arrived((a, "x", dx))
                acc[...] += xin[dx - 1].astype(F32)
            for dz in [2, 1, 3]:
                z = p.zz(dz)
                zsend[dz - 1] = acc[z].astype(BF16)
                s.go((a, "z", dz), zsend.at[dz - 1], zin.at[dz - 1], p.dev(z=z))
        for a, own, out, core, xin, xsend, acc, zin, zsend in arrays:
            if a == 0:
                lax.fori_loop(0, pieces.shape[0] // lanes, columns, 0)
            total = acc[p.z]
            for dz in range(1, nz):
                s.arrived((a, "z", dz))
                total = total + zin[dz - 1].astype(F32)
            out[p.b] = total.astype(BF16)
            for dy in range(1, nb):
                s.go((a, "y", dy), out.at[p.b], out.at[p.b], p.dev(b=p.bb(dy)))
        for key in keys:
            if key[0] == "p" or key[1] == "y":
                s.arrived(key)
        s.finish()

    def buffers(r, k):
        return [
            pltpu.VMEM((nz, nx, r, k), BF16),
            pltpu.VMEM((max(nx - 1, 1), nz, r, k), BF16),
            pltpu.VMEM((max(nx - 1, 1), nz, r, k), BF16),
            pltpu.VMEM((nz, r, k), F32),
            pltpu.VMEM((nz - 1, r, k), BF16),
            pltpu.VMEM((nz - 1, r, k), BF16),
        ]

    return call(
        kernel,
        [
            jax.ShapeDtypeStruct((depth, pieces.shape[0]), BF16),
            jax.ShapeDtypeStruct((nb, depth, width), BF16),
            jax.ShapeDtypeStruct((nb, crows * cuts, width), BF16),
            jax.ShapeDtypeStruct((nb, vrows, bins), BF16),
        ],
        buffers(crows, width) * cuts
        + buffers(vrows, bins)
        + [pltpu.VMEM((nz, nx, CORES, nb, vrows, bins), BF16)] * fused
        + [pltpu.SemaphoreType.DMA((len(keys),)), pltpu.SemaphoreType.DMA((len(keys),))],
        3,
        trunk,
        proj_weight,
        pieces,
        code,
        *value,
    )


def dot(a, b, dims):
    return lax.dot_general(a, b, (dims, ((), ())), preferred_element_type=F32)


class Slots(Sends):
    def __init__(self, send_sem, recv_sem, send_at, recv_at, place):
        super().__init__(send_sem, recv_sem, (), place)
        self.send_at, self.recv_at = send_at, recv_at

    def make(self, key, src, dst, dev):
        return pltpu.make_async_remote_copy(
            src_ref=src,
            dst_ref=dst,
            send_sem=self.send_sem.at[self.send_at[key]],
            recv_sem=self.recv_sem.at[self.recv_at[key]],
            device_id=dev,
            device_id_type=MESH,
        )


def number(keys, first, apart=()):
    at, names = {}, {}
    for key in keys:
        name = key
        if key[0] not in apart:
            name = tuple((0, k[1]) if isinstance(k, tuple) and k[1] > 1 else k for k in key)
        at[key] = first + names.setdefault(name, len(names))
    return at, first + len(names)


def fits(nb, nf, codebook, value_weight, depth, pos):
    nx = nf // (PLANES * CORES)
    rows, width = codebook.shape
    vrows = value_weight.shape[0]
    half, vhalf = rows // nb, vrows // nb
    return (
        nb * half == rows
        and nb * vhalf == vrows
        and half % 64 == 0
        and vhalf % 32 == 0
        and CORES * rows == 256
        and nx * CORES * vrows == 256
        and width == PLANES * 256
        and depth % 192 == 0
        and pos * CORES == 256
    )


EARLY = (
    ("sx", 0), ("sz", 1), ("sz", 2), ("sx", 1), ("sz", 0),
    ("sx", 2), ("x0", 0), ("z", 1, 1), ("z", 2, 1), ("x0", 1),
    ("y", 1, 1), ("z", 1, 2), ("z", 2, 2), ("x", 1, 1), ("z", 0, 1),
    ("x0", 2), ("zx", 0, 1), ("y", 2, 1), ("y", 1, 2), ("d", 1, 1),
    ("core", 1, 1), ("d", 1, 0), ("z", 1, 3), ("x", 2, 1), ("y", 2, 2),
    ("z", 2, 3), ("zx", 0, 2), ("z", 0, 2), ("x", 1, 2), ("core", 0, 1),
    ("d", 2, 0), ("core", 0, 2), ("d", 2, 1), ("d", 0, 0), ("core", 0, 0),
    ("zx", 0, 3), ("core", 1, 2), ("y", 1, 3), ("z", 0, 3), ("send",),
    ("d", 1, 2), ("core", 2, 1), ("zxy", 0, 1), ("y", 2, 3), ("zy", 0, 1),
    ("zxy", 0, 2), ("x", 2, 2), ("core", 1, 0), ("score", 0), ("zy", 0, 2),
    ("x", 2, 3), ("core", 2, 0), ("x", 1, 3), ("d", 2, 2), ("zxy", 0, 3),
    ("d", 1, 3), ("core", 3, 1), ("core", 2, 2), ("zy", 0, 3), ("core", 3, 0),
    ("score", 1), ("d", 2, 3), ("core", 3, 2), ("score", 2), ("score", 3),
)
SPREAD = (0,)
LATE = (
    ("pg", 0), ("pg", 1), ("pg", 2), ("pg", 3), ("z", 1, 1),
    ("z", 2, 1), ("z", 1, 2), ("x", 1, 0), ("z", 2, 2), ("z", 3, 1),
    ("z", 1, 3), ("x", 0, 0), ("z", 0, 1), ("x", 2, 0), ("code",),
    ("x", 2, 2), ("z", 2, 3), ("x", 1, 1), ("z", 3, 2), ("val",),
    ("x", 1, 2), ("rsx", 2), ("rsx", 0), ("x", 2, 1), ("zx", 0, 1),
    ("x", 1, 3), ("x", 2, 3), ("rsx", 1), ("proj", 2), ("x", 3, 2),
    ("z", 3, 3), ("z", 0, 2), ("proj", 1), ("rsx", 4), ("x", 3, 0),
    ("rsx", 3), ("zx", 0, 2), ("rsz", 2), ("rsz", 0), ("x", 3, 1),
    ("z", 0, 3), ("zx", 0, 3), ("proj", 0), ("rsz", 1), ("fin", 2),
    ("fin", 1), ("rsy", 2), ("x", 3, 3), ("rsz", 4), ("proj", 3),
    ("rsz", 3), ("col",), ("rsy", 0), ("rsy", 1), ("rsy", 4),
    ("rsy", 3), ("fin", 0), ("fin", 3),
)
CROSS_FIRST = (0,)


def fused(nb, nf, trunk, pre_act, proj_weight, codebook, value_weight, target, low, frac):
    nz, nx = PLANES, nf // (PLANES * CORES)
    pos, width = pre_act.shape
    rows, vrows = codebook.shape[0], value_weight.shape[0]
    bins = value_weight.shape[1]
    depth, total_pos = trunk.shape
    codes = nf * rows
    half, vhalf = rows // nb, vrows // nb
    cw = 256
    pieces = width // cw
    cuts = 4
    ck = half // cuts
    hops = [(0, 0)] + steps(nz)
    by_far = [[h for h in hops if h[1] == far] for far in range(nz)]

    early = []
    for a in range(3):
        for hop in hops:
            early += [("core", a, hop)]
            if hop[1]:
                early += [("z", a, hop)]
            if hop[1] and a in SPREAD:
                early += [("zy", a, hop, dy) for dy in range(1, nb)]
                for dx in range(1, nx):
                    early += [("zx", a, hop, dx)]
                    early += [("zxy", a, hop, dx, dy) for dy in range(1, nb)]
            else:
                if hop[1]:
                    early += [("y", a, hop, dy) for dy in range(1, nb)]
                for dx in range(1, nx):
                    early += [("x", a, hop, dx)]
                    early += [("d", a, hop, dx, dy) for dy in range(1, nb)]
    swap = [(k, dy) for dy in range(1, nb) for k in ("act", "delta", "value")]
    late = []
    for n in range(pieces):
        for hop in hops:
            late += [("gc", n, hop)]
            if hop[1]:
                late += [("gz", n, hop)]
            if hop[1] == 0 or n not in CROSS_FIRST:
                late += [("gx", n, hop, dx) for dx in range(1, nx)]
            else:
                late += [("gzx", n, hop, dx) for dx in range(1, nx)]
        late += [("p", n, dy) for dy in range(1, nb)]
    for a in range(cuts + 1):
        late += [("rc", a)] + [("rx", a, d) for d in range(1, nx)]
        late += [("rz", a, d) for d in range(1, nz)] + [("ry", a, d) for d in range(1, nb)]
    swap_at, base = number(swap, 0)
    early_send, sends = number(early, base, ("z", "zx"))
    early_recv, recvs = number(early, base)
    late_send, last = number(late, base, ("gz", "gzx"))
    sends = max(sends, last)
    late_recv, recvs = number(late, recvs)
    early_send.update(swap_at)
    early_recv.update(swap_at)
    late_send.update(swap_at)
    late_recv.update(swap_at)

    def kernel(
        pre_in,
        cb_in,
        vw_in,
        tgt_in,
        lo_in,
        fr_in,
        tr_in,
        pw_in,
        trg,
        pj,
        cd,
        vl,
        cb,
        vw,
        pre,
        tgt,
        lo,
        fr,
        tr,
        pw,
        cb_all,
        vw_all,
        gate,
        act_all,
        logit,
        top,
        vlog,
        delta,
        delta_t,
        vd_all,
        dt_all,
        pg,
        part,
        vpart,
        pj_all,
        cd_all,
        vl_all,
        *rest,
    ):
        local_sem, send_sem, recv_sem = rest[-3:]
        p = Place(nb, nf)
        inputs = (cb_in, vw_in, pre_in, tgt_in, lo_in, fr_in, tr_in, pw_in)
        loads = [
            pltpu.make_async_copy(src, dst, local_sem.at[i])
            for i, (src, dst) in enumerate(zip(inputs, (cb, vw, pre, tgt, lo, fr, tr, pw)))
        ]
        for load in loads:
            load.start()
        p.barrier()
        for load in loads[:3]:
            load.wait()
        s = Slots(send_sem, recv_sem, early_send, early_recv, p)
        g = Slots(send_sem, recv_sem, late_send, late_recv, p)

        def under(s, far, f):
            for hop in by_far[far]:
                if far:
                    s.only(lambda hop=hop: has(p, *hop))(lambda: f(hop))
                else:
                    f(hop)

        sub = half // 2
        shards = (
            (vw, vw_all, vhalf, 0, vhalf),
            (cb, cb_all, half, 0, sub),
            (cb, cb_all, half, sub, sub),
        )

        def relay(key, at_z, at_x, at_h, **to):
            own, out, piece, skip, size = shards[key[1]]
            ref = out.at[at_z, at_x, p.c, at_h, pl.ds(skip, size)]
            s.go(key, ref, ref, p.dev(**to), lambda: out.at[0, 0, 0, 0, pl.ds(skip, size)])

        def publish(key, **to):
            own, out, piece, skip, size = shards[key[1]]
            src = own.at[pl.ds(pl.multiple_of(p.b * piece + skip, size), size)]
            dst = out.at[p.z, p.x, p.c, p.b, pl.ds(skip, size)]
            s.go(key, src, dst, p.dev(**to), lambda: out.at[0, 0, 0, 0, pl.ds(skip, size)])

        def farther(kind, a, z, x, far, extra, ways):
            for way in ways:

                @s.only(lambda way=way: feeds(p, way))
                def _():
                    relay((kind, a, (way, far)) + extra, z, x, p.b, z=p.z + way)

        def send_x(a):
            for dx in range(1, nx):
                publish(("x", a, (0, 0), dx), x=p.xx(dx))

        def send_z(a):
            for way in (1, -1):

                @s.only(lambda way=way: feeds(p, way))
                def _():
                    publish(("z", a, (way, 1)), z=p.z + way)

        for name, a in EARLY[:6]:
            (send_x if name == "sx" else send_z)(a)
        cb_all[p.z, p.x, p.c] = cb[...].reshape(nb, half, width)
        vw_all[p.z, p.x, p.c] = vw[...].reshape(nb, vhalf, bins)

        def activate(i, carry):
            cols = pl.ds(pl.multiple_of(i * cw, cw), cw)
            v = pre[:, cols].astype(F32)
            sigma = jax.nn.sigmoid(v)
            act_all[p.b, :, cols] = (v * sigma).astype(BF16)
            gate[:, cols] = sigma * (1.0 + v * (1.0 - sigma))
            return carry

        lax.fori_loop(0, width // cw, activate, 0)
        top[...] = jnp.full(top.shape, -jnp.inf, F32)
        vlog[...] = jnp.zeros(vlog.shape, F32)

        def from_x0(a):
            for dx in range(1, nx):
                s.arrived(("x", a, (0, 0), dx))
                x = p.xx(-dx)
                if a in SPREAD:
                    farther("zx", a, p.z, x, 1, (dx,), (1, -1))
                for dy in range(1, nb):
                    relay(("d", a, (0, 0), dx, dy), p.z, x, p.b, b=p.bb(dy))

        def from_z(a, far):
            def run(hop):
                z = p.z - hop[0] * far
                s.arrived(("z", a, hop))
                if far + 1 < nz:
                    farther("z", a, z, p.x, far + 1, (), hop[:1])
                if a not in SPREAD:
                    for dx in range(1, nx):
                        relay(("x", a, hop, dx), z, p.x, p.b, x=p.xx(dx))
                for dy in range(1, nb):
                    relay(("zy" if a in SPREAD else "y", a, hop, dy), z, p.x, p.b, b=p.bb(dy))

            under(s, far, run)

        def from_zx(a, far):
            def run(hop):
                z = p.z - hop[0] * far
                for dx in range(1, nx):
                    s.arrived(("zx", a, hop, dx))
                    x = p.xx(-dx)
                    if far + 1 < nz:
                        farther("zx", a, z, x, far + 1, (dx,), hop[:1])
                    for dy in range(1, nb):
                        relay(("zxy", a, hop, dx, dy), z, x, p.b, b=p.bb(dy))

            under(s, far, run)

        def from_x(a, far):
            under(s, far, lambda hop: [s.arrived(("x", a, hop, dx)) for dx in range(1, nx)])

        def from_y(a, far):
            def run(hop):
                for dy in range(1, nb):
                    s.arrived(("y", a, hop, dy))
                    for dx in range(1, nx):
                        z, h = p.z - hop[0] * far, p.bb(-dy)
                        relay(("d", a, hop, dx, dy), z, p.x, h, x=p.xx(dx))

            under(s, far, run)

        def landed(kind):
            def wait(a, far):
                def run(hop):
                    for key in early:
                        if key[:3] == (kind, a, hop):
                            s.arrived(key)

                under(s, far, run)

            return wait

        def to_other(far, a):
            own, out, piece, skip, size = shards[a]
            part = pl.ds(skip, size)

            def run(hop):
                ref = out.at[p.z - hop[0] * far, :, p.c, :, part]
                like = lambda: out.at[0, :, 0, :, part]
                s.go(("core", a, hop), ref, ref, p.dev(c=1 - p.c), like)

            under(s, far, run)

        def near(j):
            up = (0, 1, 2, 3)[j], (1, 0, 2, 3)[j], (2, 3, 1, 0)[j], (3, 2, 1, 0)[j]
            z = jnp.where(p.z == 0, up[0], up[3])
            z = jnp.where(p.z == 1, up[1], z)
            return jnp.where(p.z == 2, up[2], z)

        def score(j):
            z = near(j)
            for a in range(3):
                landed("core")(a, j)

            def tile(i, carry):
                at = pl.ds(pl.multiple_of((z * nx + i) * 256, 256), 256)
                block = dot(cb_all[z, i].reshape(256, width), act_all[p.b], ((1,), (1,)))
                logit[at, :] = block
                top[...] = jnp.maximum(top[...], jnp.max(block, axis=0, keepdims=True))
                return carry

            lax.fori_loop(0, nx, tile, 0)
            at = pl.ds(pl.multiple_of(z * 256, 256), 256)
            vlog[...] += dot(act_all[p.b, :, at], vw_all[z].reshape(256, bins), ((1,), (0,)))

        def send_active():
            for dy in range(1, nb):
                ref = act_all.at[p.b]
                g.go(("act", dy), ref, ref, p.dev(b=p.bb(dy)))

        acts = dict(
            x0=from_x0, z=from_z, zx=from_zx, x=from_x, y=from_y, d=landed("d"), zy=landed("zy"),
            zxy=landed("zxy"), core=to_other, score=score, send=send_active,
        )
        for name, *where in EARLY[6:]:
            acts[name](*where)
        for load in loads[3:6]:
            load.wait()
        high = jnp.max(vlog[...], axis=1, keepdims=True)
        grown = jnp.exp(vlog[...] - high)
        probs = grown * (1.0 / jnp.sum(grown, axis=1, keepdims=True))
        ids = lax.broadcasted_iota(jnp.int32, (pos, bins), 1).astype(F32)
        column = jnp.broadcast_to(lo[...].astype(F32), (pos, pos)).T[:, :1]
        share = jnp.broadcast_to(fr[...].astype(F32) / 1024.0, (pos, pos)).T[:, :1]
        want = jnp.where(ids == column, 1.0 - share, 0.0)
        want = want + jnp.where(ids == column + 1.0, share, 0.0)
        vd_all[p.b] = (probs - want).astype(BF16)
        for dy in range(1, nb):
            ref = vd_all.at[p.b]
            g.go(("value", dy), ref, ref, p.dev(b=p.bb(dy)))

        blocks = codes // 256
        best = top[...]

        def grow(i, total):
            at = pl.ds(pl.multiple_of(i * 256, 256), 256)
            e = jnp.exp(logit[at, :] - best)
            logit[at, :] = e
            return total + jnp.sum(e, axis=0, keepdims=True)

        scale = 1.0 / lax.fori_loop(0, blocks, grow, jnp.zeros((1, pos), F32))
        group = 256 // rows
        code_ids = lax.broadcasted_iota(jnp.int32, (256, pos), 0)

        def differ(i, carry):
            at = pl.ds(pl.multiple_of(i * 256, 256), 256)
            hot = jnp.where(code_ids + i * 256 == tgt[...], 1.0, 0.0)
            d = logit[at, :] * scale - hot
            delta[:, at] = d.T.astype(BF16)
            delta_t[pl.ds(i * group, group)] = d.astype(BF16).reshape(group, nb, half, pos)
            return carry

        lax.fori_loop(0, blocks, differ, 0)
        lanes = pl.ds(pl.multiple_of(p.b * pos, pos), pos)
        for dy in range(1, nb):
            to = p.bb(dy)
            g.go(("delta", dy), delta_t.at[:, to], dt_all.at[:, :, lanes], p.dev(b=to))
        dt_all[:, :, lanes] = delta_t[:, p.b]
        s.finish()

        def pass_on(n, at_z, at_x, key, **to):
            ref = pg.at[n, at_z, at_x, p.c]
            g.go(key, ref, ref, p.dev(**to), lambda: pg.at[n, 0, 0, 0])

        def onward(n, kind, z, x, far, extra, ways):
            for way in ways:

                @g.only(lambda way=way: feeds(p, way))
                def _():
                    pass_on(n, z, x, (kind, n, (way, far)) + extra, z=p.z + way)

        def across(n, hop):
            for dx in range(1, nx):
                pass_on(n, p.z - hop[0] * hop[1], p.x, ("gx", n, hop, dx), x=p.xx(dx))

        def to_core(n, hop):
            ref = pg.at[n, p.z - hop[0] * hop[1], :, p.c]
            g.go(("gc", n, hop), ref, ref, p.dev(c=1 - p.c), lambda: pg.at[n, 0, :, 0])

        def head(n):
            cols = pl.ds(n * cw, cw)
            back = dot(delta[...], cb_all[:, :, :, :, :, cols].reshape(codes, cw), ((1,), (0,)))
            back = back + dot(vd_all[p.b], vw_all[n].reshape(cw, bins), ((1,), (1,)))
            pg[n, p.z, p.x, p.c] = (back * gate[:, cols]).astype(BF16)
            if n in CROSS_FIRST:
                across(n, (0, 0))
            onward(n, "gz", p.z, p.x, 1, (), (1, -1))
            if n not in CROSS_FIRST:
                across(n, (0, 0))

        def grad_z(n, far):
            def run(hop):
                z = p.z - hop[0] * far
                g.arrived(("gz", n, hop))
                if far + 1 < nz:
                    onward(n, "gz", z, p.x, far + 1, (), hop[:1])
                if n not in CROSS_FIRST:
                    across(n, hop)

            under(g, far, run)

        def grad_x(n, far):
            def run(hop):
                for dx in range(1, nx):
                    g.arrived(("gx", n, hop, dx))
                    if n in CROSS_FIRST:
                        onward(n, "gzx", p.z, p.xx(-dx), 1, (dx,), (1, -1))
                to_core(n, hop)

            under(g, far, run)

        def grad_zx(n, far):
            def run(hop):
                for dx in range(1, nx):
                    g.arrived(("gzx", n, hop, dx))
                    if far + 1 < nz:
                        onward(n, "gzx", p.z - hop[0] * far, p.xx(-dx), far + 1, (dx,), hop[:1])
                to_core(n, hop)

            under(g, far, run)

        arrays = []
        for a in range(cuts + 1):
            if a < cuts:
                own, out = part.at[:, :, :, pl.ds(a * ck, ck)], cd_all.at[:, pl.ds(a * ck, ck)]
            else:
                own, out = vpart.at[:, :, :, p.b], vl_all
            arrays.append((own, out) + tuple(rest[6 * a : 6 * a + 6]))
        deep = nb * pos

        def to_sum(a):
            own, out, core, *_ = arrays[a]
            g.go(("rc", a), own.at[:, :, 1 - p.c], core, p.dev(c=1 - p.c))

        def code():
            for dy in range(1, nb):
                g.arrived(("act", dy))
                g.arrived(("delta", dy))

            def block(i, carry):
                z = i // (width // cw)
                cols = pl.ds(pl.multiple_of((i % (width // cw)) * cw, cw), cw)
                left = dt_all[pl.ds(z * nx * CORES, nx * CORES)].reshape(nx * CORES * half, deep)
                right = act_all[:, :, cols].reshape(deep, cw)
                product = dot(left, right, ((1,), (0,)))
                part[z, :, :, :, cols] = product.astype(BF16).reshape(nx, CORES, half, cw)
                return carry

            lax.fori_loop(0, nz * (width // cw), block, 0)
            for a in range(cuts):
                to_sum(a)

        def val():
            for dy in range(1, nb):
                g.arrived(("value", dy))

            def block(z, carry):
                cols = pl.ds(pl.multiple_of(z * 256, 256), 256)
                left = act_all[:, :, cols].reshape(deep, 256)
                product = dot(left, vd_all[...].reshape(deep, bins), ((0,), (0,)))
                vpart[z] = product.astype(BF16).reshape(nx, CORES, nb, vhalf, bins)
                return carry

            lax.fori_loop(0, nz, block, 0)
            to_sum(cuts)

        def rsx(a):
            own, out, core, xin, xsend, acc, zin, zsend = arrays[a]
            g.arrived(("rc", a))
            for dx in range(1, nx):
                x = p.xx(dx)
                for z in range(nz):
                    both = own[z, x, p.c].astype(F32) + core[z, x].astype(F32)
                    xsend[dx - 1, z] = both.astype(BF16)
                g.go(("rx", a, dx), xsend.at[dx - 1], xin.at[dx - 1], p.dev(x=x))
            for z in range(nz):
                acc[z] = own[z, p.x, p.c].astype(F32) + core[z, p.x].astype(F32)

        def rsz(a):
            own, out, core, xin, xsend, acc, zin, zsend = arrays[a]
            for dx in range(1, nx):
                g.arrived(("rx", a, dx))
                acc[...] += xin[dx - 1].astype(F32)
            for dz in [2, 1, 3]:
                z = p.zz(dz)
                zsend[dz - 1] = acc[z].astype(BF16)
                g.go(("rz", a, dz), zsend.at[dz - 1], zin.at[dz - 1], p.dev(z=z))

        def rsy(a):
            own, out, core, xin, xsend, acc, zin, zsend = arrays[a]
            total = acc[p.z]
            for dz in range(1, nz):
                g.arrived(("rz", a, dz))
                total = total + zin[dz - 1].astype(F32)
            out[p.b] = total.astype(BF16)
            for dy in range(1, nb):
                g.go(("ry", a, dy), out.at[p.b], out.at[p.b], p.dev(b=p.bb(dy)))

        def proj(n):
            for far in range(nz):
                under(g, far, lambda hop: g.arrived(("gc", n, hop)))

            def block(i, carry):
                at = pl.ds(pl.multiple_of(i * 192, 192), 192)
                pj_all[p.b, n, at, :] = jnp.dot(
                    tr[at, :], pg[n].reshape(total_pos, cw), preferred_element_type=F32
                ).astype(BF16)
                return carry

            lax.fori_loop(0, depth // 192, block, 0)
            for dy in range(1, nb):
                ref = pj_all.at[p.b, n]
                g.go(("p", n, dy), ref, ref, p.dev(b=p.bb(dy)))

        def col():
            def block(i, carry):
                at = pl.ds(pl.multiple_of(i * 256, 256), 256)
                z, x = i // nx, i % nx
                total = 0.0
                for n in range(pieces):
                    there = pg[n, z, x].reshape(256, cw)
                    total = total + dot(pw[:, pl.ds(n * cw, cw)], there, ((1,), (1,)))
                trg[:, at] = total.astype(BF16)
                return carry

            lax.fori_loop(0, nz * nx, block, 0)

        def fin(n):
            for dy in range(1, nb):
                g.arrived(("p", n, dy))
            total = pj_all[0, n].astype(F32)
            for b in range(1, nb):
                total = total + pj_all[b, n].astype(F32)
            pj[:, pl.ds(n * cw, cw)] = total

        for load in loads[6:]:
            load.wait()
        acts = dict(
            pg=head, z=grad_z, x=grad_x, zx=grad_zx, code=code, val=val, rsx=rsx, rsz=rsz, rsy=rsy,
            proj=proj, col=col, fin=fin,
        )
        for name, *where in LATE:
            acts[name](*where)
        for a in range(cuts + 1):
            for dy in range(1, nb):
                g.arrived(("ry", a, dy))
        for b in range(nb):
            cd[pl.ds(b * half, half), :] = cd_all[b].astype(F32)
            vl[pl.ds(b * vhalf, vhalf), :] = vl_all[b].astype(F32)
        g.finish()

    def buffers(r, k):
        return [
            pltpu.VMEM((nz, nx, r, k), BF16),
            pltpu.VMEM((max(nx - 1, 1), nz, r, k), BF16),
            pltpu.VMEM((max(nx - 1, 1), nz, r, k), BF16),
            pltpu.VMEM((nz, r, k), F32),
            pltpu.VMEM((nz - 1, r, k), BF16),
            pltpu.VMEM((nz - 1, r, k), BF16),
        ]

    anywhere = pl.BlockSpec(memory_space=pl.ANY)
    stay = pl.BlockSpec(memory_space=pltpu.HBM)
    results = pl.pallas_call(
        kernel,
        out_shape=[
            jax.ShapeDtypeStruct((depth, total_pos), BF16),
            jax.ShapeDtypeStruct((depth, width), F32),
            jax.ShapeDtypeStruct((rows, width), F32),
            jax.ShapeDtypeStruct((vrows, bins), F32),
        ],
        in_specs=[stay] * 8,
        out_specs=[pl.BlockSpec(memory_space=pltpu.VMEM)] * 4,
        scratch_shapes=[
            pltpu.VMEM((rows, width), BF16),
            pltpu.VMEM((vrows, bins), BF16),
            pltpu.VMEM((pos, width), BF16),
            pltpu.VMEM((1, pos), jnp.int32),
            pltpu.VMEM((1, pos), jnp.int32),
            pltpu.VMEM((1, pos), jnp.int32),
            pltpu.VMEM((depth, total_pos), BF16),
            pltpu.VMEM((depth, width), BF16),
            pltpu.VMEM((nz, nx, CORES, nb, half, width), BF16),
            pltpu.VMEM((nz, nx, CORES, nb, vhalf, bins), BF16),
            pltpu.VMEM((pos, width), F32),
            pltpu.VMEM((nb, pos, width), BF16),
            pltpu.VMEM((codes, pos), F32),
            pltpu.VMEM((1, pos), F32),
            pltpu.VMEM((pos, bins), F32),
            pltpu.VMEM((pos, codes), BF16),
            pltpu.VMEM((nf, nb, half, pos), BF16),
            pltpu.VMEM((nb, pos, bins), BF16),
            pltpu.VMEM((nf, half, nb * pos), BF16),
            pltpu.VMEM((pieces, nz, nx, CORES, pos, cw), BF16),
            pltpu.VMEM((nz, nx, CORES, half, width), BF16),
            pltpu.VMEM((nz, nx, CORES, nb, vhalf, bins), BF16),
            pltpu.VMEM((nb, pieces, depth, cw), BF16),
            pltpu.VMEM((nb, half, width), BF16),
            pltpu.VMEM((nb, vhalf, bins), BF16),
        ]
        + buffers(ck, width) * cuts
        + buffers(vhalf, bins)
        + [
            pltpu.SemaphoreType.DMA((8,)),
            pltpu.SemaphoreType.DMA((sends,)),
            pltpu.SemaphoreType.DMA((recvs,)),
        ],
        compiler_params=pltpu.CompilerParams(
            collective_id=4, has_side_effects=True, vmem_limit_bytes=44 << 20
        ),
    )(
        *(
            pltpu.with_memory_space_constraint(x, pltpu.HBM)
            for x in (
                pre_act, codebook, value_weight, target, low, frac, trunk, proj_weight,
            )
        )
    )

    def hand_over(*refs):
        copies = [
            pltpu.make_async_copy(refs[i], refs[4 + i], refs[8].at[i]) for i in range(4)
        ]
        for copy in copies:
            copy.start()
        for copy in copies:
            copy.wait()

    return pl.pallas_call(
        hand_over,
        out_shape=[jax.ShapeDtypeStruct(r.shape, r.dtype) for r in results],
        in_specs=[anywhere] * 4,
        out_specs=[stay] * 4,
        scratch_shapes=[pltpu.SemaphoreType.DMA((4,))],
        compiler_params=pltpu.CompilerParams(vmem_limit_bytes=1 << 20),
    )(*results)


def make_body(nb, nf):
    nz, nx = PLANES, nf // (PLANES * CORES)

    def body(
        trunk, pre_act, proj_weight, codebook, value_weight, code_target, value_bin, value_frac
    ):
        if fits(nb, nf, codebook, value_weight, trunk.shape[0], pre_act.shape[0]):
            row = (1, pre_act.shape[0])
            return fused(
                nb,
                nf,
                trunk,
                pre_act,
                proj_weight,
                codebook,
                value_weight,
                code_target.reshape(row),
                value_bin.reshape(row),
                value_frac.reshape(row),
            )
        all_codes, bins_weight = gather_weights(nb, nf, codebook, value_weight)
        rows, width = pre_act.shape
        num_codes = all_codes.shape[0]
        num_bins = bins_weight.shape[1]
        pre_value = pre_act.astype(F32)
        gate_sigma = jax.nn.sigmoid(pre_value)
        active = (pre_value * gate_sigma).astype(BF16)
        code_logits = jnp.einsum("rk,ck->rc", active, all_codes, preferred_element_type=F32)
        code_probs = jax.nn.softmax(code_logits, axis=-1)
        code_ids = lax.broadcasted_iota(jnp.int32, (1, num_codes), 1)
        one_hot = (code_target[:, None] == code_ids).astype(F32)
        code_delta = (code_probs - one_hot).astype(BF16)
        value_logits = jnp.dot(active, bins_weight, preferred_element_type=F32)
        value_probs = jax.nn.softmax(value_logits, axis=-1)
        bin_ids = lax.broadcasted_iota(jnp.int32, (1, num_bins), 1)
        fraction = value_frac.astype(F32)[:, None] / 1024.0
        target = jnp.where(bin_ids == value_bin[:, None], 1.0 - fraction, 0.0)
        target = target + jnp.where(bin_ids == value_bin[:, None] + 1, fraction, 0.0)
        value_delta = (value_probs - target).astype(BF16)
        backward = jnp.dot(code_delta, all_codes, preferred_element_type=F32)
        backward = backward + jnp.einsum(
            "rb,kb->rk", value_delta, bins_weight, preferred_element_type=F32
        )
        pre_grad = (backward * gate_sigma * (1.0 + pre_value * (1.0 - gate_sigma))).astype(BF16)
        own = codebook.shape[0] // nb
        delta_t = code_delta.T.reshape(nf, nb, own, rows).swapaxes(0, 1)
        delta_t = delta_t.reshape(nb, nf * own, rows)
        pieces, act_all, dt_all, vd_all = gather_grads(
            nb, nf, pre_grad, active, delta_t, value_delta
        )
        code_part = jnp.dot(dt_all, act_all, preferred_element_type=F32)
        code_part = code_part.astype(BF16).reshape(nz, nx, CORES, own, width)
        vown = value_weight.shape[0] // nb
        if vown % 16 == 0:
            value_part = (act_all, vd_all)
        else:
            value_part = jnp.einsum("rk,rb->kb", act_all, vd_all, preferred_element_type=F32)
            value_part = value_part.astype(BF16)
            value_part = (value_part.reshape(nz, nx, CORES, nb, vown, num_bins),)
        out_cols, proj_all, code_all, value_all = reduce_grads(
            nb, nf, trunk, proj_weight, pieces, code_part, value_part
        )
        proj_grad = jnp.sum(proj_all.astype(F32), axis=0)
        code_grad = code_all.reshape(nb * own, width).astype(F32)
        value_grad = value_all.reshape(nb * vown, num_bins).astype(F32)
        return (out_cols, proj_grad, code_grad, value_grad)

    return body


def solution(mesh):
    in_specs = (
        P("fsdp", "batch"),
        P(("batch", "fsdp"), None),
        P("fsdp", None),
        P("fsdp", None),
        P("fsdp", None),
        P(("batch", "fsdp")),
        P(("batch", "fsdp")),
        P(("batch", "fsdp")),
    )
    out_specs = (P("fsdp", "batch"), P("fsdp", None), P("fsdp", None), P("fsdp", None))
    body = make_body(mesh.shape["batch"], mesh.shape["fsdp"])
    return jax.shard_map(body, mesh=mesh, in_specs=in_specs, out_specs=out_specs, check_vma=False)
```

```python
import jax
import jax.numpy as jnp
from jax import lax
from jax.experimental import pallas as pl
from jax.experimental.pallas import tpu as pltpu
from jax.sharding import PartitionSpec as P

MESH = pl.DeviceIdType.MESH
BF16 = jnp.bfloat16
F32 = jnp.float32
CORES = 2
PLANES = 4


class Place:
    def __init__(self, nb, nf):
        self.nb, self.nz = nb, PLANES
        self.nx = nf // (PLANES * CORES)
        f = lax.axis_index("fsdp")
        self.b = lax.axis_index("batch")
        self.z = f // (self.nx * CORES)
        self.x = (f // CORES) % self.nx
        self.c = f % CORES

    def dev(self, b=None, z=None, x=None, c=None):
        b = self.b if b is None else b
        z = self.z if z is None else z
        x = self.x if x is None else x
        c = self.c if c is None else c
        return (b, (z * self.nx + x) * CORES + c)

    def zz(self, d):
        return lax.rem(self.z + d + self.nz, self.nz)

    def xx(self, d):
        return lax.rem(self.x + d + self.nx, self.nx)

    def bb(self, d):
        return lax.rem(self.b + d + self.nb, self.nb)

    def barrier(self):
        sem = pltpu.get_barrier_semaphore()
        peers = [self.dev(z=self.zz(d)) for d in range(1, self.nz)]
        peers += [self.dev(x=self.xx(d)) for d in range(1, self.nx)]
        peers += [self.dev(b=self.bb(d)) for d in range(1, self.nb)]
        peers += [self.dev(c=1 - self.c)]
        for peer in peers:
            pl.semaphore_signal(sem, inc=1, device_id=peer, device_id_type=MESH)
        pl.semaphore_wait(sem, len(peers))


def steps(nz):
    return [(way, far) for far in range(1, nz) for way in (1, -1)]


class Sends:
    def __init__(self, send_sem, recv_sem, keys, place):
        self.send_sem, self.recv_sem, self.place = send_sem, recv_sem, place
        self.at = {k: i for i, k in enumerate(keys)}
        self.like = {}
        self.started = []
        self.when = ()

    def make(self, key, src, dst, dev):
        i = self.at[key]
        return pltpu.make_async_remote_copy(
            src_ref=src,
            dst_ref=dst,
            send_sem=self.send_sem.at[i],
            recv_sem=self.recv_sem.at[i],
            device_id=dev,
            device_id_type=MESH,
        )

    def go(self, key, src, dst, dev, like=None):
        self.make(key, src, dst, dev).start()
        self.like[key] = dst if like is None else like
        self.started.append((key, self.when))

    def waiter(self, key):
        ref = self.like[key]
        ref = ref() if callable(ref) else ref
        return self.make(key, ref, ref, self.place.dev(c=1 - self.place.c))

    def arrived(self, key):
        self.waiter(key).wait_recv()

    def finish(self):
        for key, whens in self.started:

            def wait(key=key):
                self.waiter(key).wait_send()

            if whens:
                met = whens[0]()
                for when in whens[1:]:
                    met = jnp.logical_and(met, when())
                pl.when(met)(wait)
            else:
                wait()

    def only(self, when):
        def run(f):
            outer = self.when
            self.when = outer + (when,)

            @pl.when(when())
            def _():
                f()

            self.when = outer

        return run


def call(kernel, outs, scratch, cid, *args):
    return pl.pallas_call(
        kernel,
        out_shape=outs,
        in_specs=[pl.BlockSpec(memory_space=pltpu.VMEM)] * len(args),
        out_specs=[pl.BlockSpec(memory_space=pltpu.VMEM)] * len(outs),
        scratch_shapes=scratch,
        compiler_params=pltpu.CompilerParams(collective_id=cid, has_side_effects=True),
    )(*args)


def has(p, way, far):
    return p.z >= far if way == 1 else p.z + far < p.nz


def feeds(p, way):
    return p.z + 1 < p.nz if way == 1 else p.z >= 1


def gather_weights_keys(nb, nx, nz):
    keys = []
    for a in (0, 1):
        keys += [(a, "c", 0)]
        for hop in [(0, 0)] + steps(nz):
            if hop[1]:
                keys += [(a, "z", hop), (a, "cz", hop)]
                for dy in range(1, nb):
                    keys += [(a, "y", hop, dy), (a, "cy", hop, dy)]
            for dx in range(1, nx):
                keys += [(a, "x", hop, dx), (a, "cx", hop, dx)]
                for dy in range(1, nb):
                    keys += [(a, "d", hop, dx, dy), (a, "cd", hop, dx, dy)]
    return keys


def gather_weights(nb, nf, codebook, value_weight):
    nz, nx = PLANES, nf // (PLANES * CORES)
    keys = gather_weights_keys(nb, nx, nz)
    rows, width = codebook.shape
    vrows, bins = value_weight.shape

    def kernel(cb, vw, cb_out, vw_out, send_sem, recv_sem):
        p = Place(nb, nf)
        p.barrier()
        s = Sends(send_sem, recv_sem, keys, p)
        arrays = ((0, cb, cb_out), (1, vw, vw_out))

        def spot(out, z, x, h):
            return out.at[z, x, p.c, h]

        def relay(key, out, at_z, at_x, at_h, **to):
            ref = spot(out, at_z, at_x, at_h)
            s.go(key, ref, ref, p.dev(**to), lambda: out.at[0, 0, 0, 0])

        for a, own, out in arrays:
            here = spot(out, p.z, p.x, p.b)
            for way in (1, -1):

                @s.only(lambda way=way: feeds(p, way))
                def _(a=a, own=own, out=out, here=here, way=way):
                    s.go((a, "z", (way, 1)), own.at[p.b], here, p.dev(z=p.z + way), lambda: out.at[0, 0, 0, 0])

            for dx in range(1, nx):
                s.go((a, "x", (0, 0), dx), own.at[p.b], here, p.dev(x=p.xx(dx)))
            s.go((a, "c", 0), own, out.at[p.z, p.x, p.c], p.dev(c=1 - p.c))
        for a, own, out in arrays:
            out[p.z, p.x, p.c] = own[...]

        def from_z(hop):
            way, far = hop
            z = p.z - way * far
            for a, own, out in arrays:
                s.arrived((a, "z", hop))
                if far + 1 < nz:

                    @s.only(lambda way=way: feeds(p, way))
                    def _(a=a, out=out):
                        relay((a, "z", (way, far + 1)), out, z, p.x, p.b, z=p.z + way)

                for dx in range(1, nx):
                    relay((a, "x", hop, dx), out, z, p.x, p.b, x=p.xx(dx))
                for dy in range(1, nb):
                    relay((a, "y", hop, dy), out, z, p.x, p.b, b=p.bb(dy))
                relay((a, "cz", hop), out, z, p.x, p.b, c=1 - p.c)

        def from_plane(hop):
            way, far = hop
            z = p.z - way * far
            for a, own, out in arrays:
                for dx in range(1, nx):
                    x = p.xx(-dx)
                    s.arrived((a, "x", hop, dx))
                    if far % 2 == 0:
                        for dy in range(1, nb):
                            relay((a, "d", hop, dx, dy), out, z, x, p.b, b=p.bb(dy))
                    relay((a, "cx", hop, dx), out, z, x, p.b, c=1 - p.c)
                if far:
                    for dy in range(1, nb):
                        h = p.bb(-dy)
                        s.arrived((a, "y", hop, dy))
                        if far % 2:
                            for dx in range(1, nx):
                                relay((a, "d", hop, dx, dy), out, z, p.x, h, x=p.xx(dx))
                        relay((a, "cy", hop, dy), out, z, p.x, h, c=1 - p.c)

        def from_diagonal(hop):
            way, far = hop
            for a, own, out in arrays:
                for dx in range(1, nx):
                    for dy in range(1, nb):
                        s.arrived((a, "d", hop, dx, dy))
                        relay(
                            (a, "cd", hop, dx, dy),
                            out,
                            p.z - way * far,
                            p.xx(-dx),
                            p.bb(-dy),
                            c=1 - p.c,
                        )

        def from_core(hop):
            for key in keys:
                if key[1] in ("cz", "cx", "cy", "cd") and key[2] == hop:
                    s.arrived(key)

        def under(hop, f):
            if hop[1]:
                s.only(lambda: has(p, *hop))(lambda: f(hop))
            else:
                f(hop)

        hops = [(0, 0)] + steps(nz)
        by_far = [[h for h in hops if h[1] == far] for far in range(nz)]
        for far in range(nz + 2):
            if 1 <= far < nz:
                for hop in by_far[far]:
                    under(hop, from_z)
            if 1 <= far <= nz:
                for hop in by_far[far - 1]:
                    under(hop, from_plane)
            if far >= 2:
                for hop in by_far[far - 2]:
                    under(hop, from_diagonal)
        for a in (0, 1):
            s.arrived((a, "c", 0))
        for hop in hops:
            under(hop, from_core)
        s.finish()

    cb_out, vw_out = call(
        kernel,
        [
            jax.ShapeDtypeStruct((nz, nx, CORES, nb, rows // nb, width), BF16),
            jax.ShapeDtypeStruct((nz, nx, CORES, nb, vrows // nb, bins), BF16),
        ],
        [pltpu.SemaphoreType.DMA((len(keys),)), pltpu.SemaphoreType.DMA((len(keys),))],
        1,
        codebook.reshape(nb, rows // nb, width),
        value_weight.reshape(nb, vrows // nb, bins),
    )
    return cb_out.reshape(nf * rows, width), vw_out.reshape(nf * vrows, bins)


def gather_grads(nb, nf, pre_grad, active, delta_t, value_delta):
    nz, nx = PLANES, nf // (PLANES * CORES)
    rows, width = pre_grad.shape
    bins = value_delta.shape[1]
    half = delta_t.shape[1]
    hops = [(0, 0)] + steps(nz)
    keys = [("c", 0)]
    for hop in hops:
        if hop[1]:
            keys += [("z", hop), ("cz", hop)]
        for dx in range(1, nx):
            keys += [("x", hop, dx), ("cx", hop, dx)]
    keys += [(k, dy) for dy in range(1, nb) for k in ("act", "delta", "value")]

    def kernel(pg, act, dt, vd, pg_out, act_out, dt_out, vd_out, send_sem, recv_sem):
        p = Place(nb, nf)
        p.barrier()
        s = Sends(send_sem, recv_sem, keys, p)
        here, like = pg_out.at[p.z, p.x, p.c], pg_out.at[0, 0, 0]
        mine = pl.ds(pl.multiple_of(p.b * rows, rows), rows)
        for way in (1, -1):

            @s.only(lambda way=way: feeds(p, way))
            def _(way=way):
                s.go(("z", (way, 1)), pg, here, p.dev(z=p.z + way), like)

        for dx in range(1, nx):
            s.go(("x", (0, 0), dx), pg, here, p.dev(x=p.xx(dx)))
        for dy in range(1, nb):
            to = p.bb(dy)
            s.go(("act", dy), act, act_out.at[p.b], p.dev(b=to))
            s.go(("delta", dy), dt.at[to], dt_out.at[:, mine], p.dev(b=to))
            s.go(("value", dy), vd, vd_out.at[p.b], p.dev(b=to))
        s.go(("c", 0), pg, here, p.dev(c=1 - p.c))
        pg_out[p.z, p.x, p.c] = pg[...]
        act_out[p.b] = act[...]
        dt_out[:, mine] = dt[p.b]
        vd_out[p.b] = vd[...]

        def from_z(hop):
            way, far = hop
            ref = pg_out.at[p.z - way * far, p.x, p.c]
            s.arrived(("z", hop))
            if far + 1 < nz:

                @s.only(lambda way=way: feeds(p, way))
                def _():
                    s.go(("z", (way, far + 1)), ref, ref, p.dev(z=p.z + way), like)

            for dx in range(1, nx):
                s.go(("x", hop, dx), ref, ref, p.dev(x=p.xx(dx)), like)
            s.go(("cz", hop), ref, ref, p.dev(c=1 - p.c), like)

        def from_plane(hop):
            way, far = hop
            for dx in range(1, nx):
                s.arrived(("x", hop, dx))
                ref = pg_out.at[p.z - way * far, p.xx(-dx), p.c]
                s.go(("cx", hop, dx), ref, ref, p.dev(c=1 - p.c), like)

        def from_core(hop):
            for key in keys:
                if key[0] in ("cz", "cx") and key[1] == hop:
                    s.arrived(key)

        def under(hop, f):
            if hop[1]:
                s.only(lambda: has(p, *hop))(lambda: f(hop))
            else:
                f(hop)

        for far in range(nz + 1):
            for hop in hops:
                if far and hop[1] == far:
                    under(hop, from_z)
            for hop in hops:
                if hop[1] == far - 1:
                    under(hop, from_plane)
        for key in keys:
            if key[0] in ("act", "delta", "value", "c"):
                s.arrived(key)
        for hop in hops:
            under(hop, from_core)
        s.finish()

    pieces, act_all, dt_all, vd_all = call(
        kernel,
        [
            jax.ShapeDtypeStruct((nz, nx, CORES, rows, width), BF16),
            jax.ShapeDtypeStruct((nb, rows, width), BF16),
            jax.ShapeDtypeStruct((half, nb * rows), BF16),
            jax.ShapeDtypeStruct((nb, rows, bins), BF16),
        ],
        [pltpu.SemaphoreType.DMA((len(keys),)), pltpu.SemaphoreType.DMA((len(keys),))],
        2,
        pre_grad,
        active,
        delta_t,
        value_delta,
    )
    return (
        pieces.reshape(nf * rows, width),
        act_all.reshape(nb * rows, width),
        dt_all,
        vd_all.reshape(nb * rows, bins),
    )


def reduce_grads(nb, nf, trunk, proj_weight, pieces, code, value):
    nz, nx = PLANES, nf // (PLANES * CORES)
    depth = trunk.shape[0]
    width = pieces.shape[1]
    block = next(n for n in (192, 96, 64, 32, 16) if depth % n == 0)
    blocks = depth // block
    lanes = 256
    cuts = 2 if code.shape[3] % 32 == 0 else 1
    crows = code.shape[3] // cuts
    fused = len(value) == 2
    bins = value[-1].shape[-1]
    vrows = width // (nf * nb) if fused else value[0].shape[4]
    chunks = range(cuts + 1)
    keys = [("p", i, dy) for i in range(blocks) for dy in range(1, nb)]
    for a in chunks:
        keys += [(a, "c")] + [(a, "x", d) for d in range(1, nx)]
        keys += [(a, "z", d) for d in range(1, nz)] + [(a, "y", d) for d in range(1, nb)]

    def kernel(tr, pw, pg, cd, *rest):
        factors, rest = rest[: len(value)], rest[len(value) :]
        (tr_out, pj_out, cd_out, vl_out), rest = rest[:4], rest[4:]
        send_sem, recv_sem = rest[-2:]
        vl = rest[-3] if fused else factors[0]
        p = Place(nb, nf)
        p.barrier()
        s = Sends(send_sem, recv_sem, keys, p)
        arrays = []
        for a in chunks:
            if a < cuts:
                part = pl.ds(a * crows, crows)
                own, out = cd.at[:, :, :, part], cd_out.at[:, part]
            else:
                own, out = vl.at[:, :, :, p.b], vl_out
            arrays.append((a, own, out) + tuple(rest[6 * a : 6 * a + 6]))
        for a, own, out, core, *_ in arrays:
            if a == cuts and fused:
                product = lax.dot_general(
                    factors[0][...],
                    factors[1][...],
                    (((0,), (0,)), ((), ())),
                    preferred_element_type=F32,
                )
                vl[...] = product.astype(BF16).reshape(nz, nx, CORES, nb, vrows, bins)
            s.go((a, "c"), own.at[:, :, 1 - p.c], core, p.dev(c=1 - p.c))

        def multiply(i):
            rows = pl.ds(i * block, block)

            def tile(n, carry):
                cols = pl.ds(pl.multiple_of(n * lanes, lanes), lanes)
                pj_out[p.b, rows, cols] = jnp.dot(
                    tr[rows, :], pg[:, cols], preferred_element_type=F32
                ).astype(BF16)
                return carry

            lax.fori_loop(0, width // lanes, tile, 0)
            for dy in range(1, nb):
                ref = pj_out.at[p.b, rows]
                s.go(("p", i, dy), ref, ref, p.dev(b=p.bb(dy)))

        def columns(n, carry):
            cols = pl.ds(pl.multiple_of(n * lanes, lanes), lanes)
            tr_out[:, cols] = lax.dot_general(
                pw[...], pg[cols, :], (((1,), (1,)), ((), ())), preferred_element_type=F32
            ).astype(BF16)
            return carry

        multiply(0)
        for a, own, out, core, xin, xsend, acc, zin, zsend in arrays:
            s.arrived((a, "c"))
            for dx in range(1, nx):
                x = p.xx(dx)
                for z in range(nz):
                    both = own[z, x, p.c].astype(F32) + core[z, x].astype(F32)
                    xsend[dx - 1, z] = both.astype(BF16)
                s.go((a, "x", dx), xsend.at[dx - 1], xin.at[dx - 1], p.dev(x=x))
            for z in range(nz):
                acc[z] = own[z, p.x, p.c].astype(F32) + core[z, p.x].astype(F32)
        for i in range(1, blocks):
            multiply(i)
        for a, own, out, core, xin, xsend, acc, zin, zsend in arrays:
            for dx in range(1, nx):
                s.arrived((a, "x", dx))
                acc[...] += xin[dx - 1].astype(F32)
            for dz in [2, 1, 3]:
                z = p.zz(dz)
                zsend[dz - 1] = acc[z].astype(BF16)
                s.go((a, "z", dz), zsend.at[dz - 1], zin.at[dz - 1], p.dev(z=z))
        for a, own, out, core, xin, xsend, acc, zin, zsend in arrays:
            if a == 0:
                lax.fori_loop(0, pieces.shape[0] // lanes, columns, 0)
            total = acc[p.z]
            for dz in range(1, nz):
                s.arrived((a, "z", dz))
                total = total + zin[dz - 1].astype(F32)
            out[p.b] = total.astype(BF16)
            for dy in range(1, nb):
                s.go((a, "y", dy), out.at[p.b], out.at[p.b], p.dev(b=p.bb(dy)))
        for key in keys:
            if key[0] == "p" or key[1] == "y":
                s.arrived(key)
        s.finish()

    def buffers(r, k):
        return [
            pltpu.VMEM((nz, nx, r, k), BF16),
            pltpu.VMEM((max(nx - 1, 1), nz, r, k), BF16),
            pltpu.VMEM((max(nx - 1, 1), nz, r, k), BF16),
            pltpu.VMEM((nz, r, k), F32),
            pltpu.VMEM((nz - 1, r, k), BF16),
            pltpu.VMEM((nz - 1, r, k), BF16),
        ]

    return call(
        kernel,
        [
            jax.ShapeDtypeStruct((depth, pieces.shape[0]), BF16),
            jax.ShapeDtypeStruct((nb, depth, width), BF16),
            jax.ShapeDtypeStruct((nb, crows * cuts, width), BF16),
            jax.ShapeDtypeStruct((nb, vrows, bins), BF16),
        ],
        buffers(crows, width) * cuts
        + buffers(vrows, bins)
        + [pltpu.VMEM((nz, nx, CORES, nb, vrows, bins), BF16)] * fused
        + [pltpu.SemaphoreType.DMA((len(keys),)), pltpu.SemaphoreType.DMA((len(keys),))],
        3,
        trunk,
        proj_weight,
        pieces,
        code,
        *value,
    )


def dot(a, b, dims):
    return lax.dot_general(a, b, (dims, ((), ())), preferred_element_type=F32)


class Slots(Sends):
    def __init__(self, send_sem, recv_sem, send_at, recv_at, place):
        super().__init__(send_sem, recv_sem, (), place)
        self.send_at, self.recv_at = send_at, recv_at

    def make(self, key, src, dst, dev):
        return pltpu.make_async_remote_copy(
            src_ref=src,
            dst_ref=dst,
            send_sem=self.send_sem.at[self.send_at[key]],
            recv_sem=self.recv_sem.at[self.recv_at[key]],
            device_id=dev,
            device_id_type=MESH,
        )


def number(keys, first, apart=()):
    at, names = {}, {}
    for key in keys:
        name = key
        if key[0] not in apart:
            name = tuple((0, k[1]) if isinstance(k, tuple) and k[1] > 1 else k for k in key)
        at[key] = first + names.setdefault(name, len(names))
    return at, first + len(names)


def fits(nb, nf, codebook, value_weight, depth, pos):
    nx = nf // (PLANES * CORES)
    rows, width = codebook.shape
    vrows = value_weight.shape[0]
    half, vhalf = rows // nb, vrows // nb
    return (
        nb > 1
        and nb * half == rows
        and nb * vhalf == vrows
        and half % 64 == 0
        and vhalf % 32 == 0
        and CORES * rows == 256
        and nx * CORES * vrows == 256
        and width == PLANES * 256
        and depth % 192 == 0
        and pos * CORES == 256
    )


EARLY = (
    ("sz", 1), ("sz", 0), ("sx", 0), ("sx", 2), ("sz", 2),
    ("sx", 1), ("z", 1, 1), ("x0", 0), ("z", 0, 1), ("z", 2, 1),
    ("x0", 1), ("x0", 2), ("core", 0, 1), ("z", 1, 2), ("z", 0, 2),
    ("core", 0, 2), ("zx", 0, 1), ("z", 2, 2), ("x", 1, 1), ("z", 0, 3),
    ("zy", 0, 1), ("z", 1, 3), ("d", 0, 0), ("zx", 0, 2), ("x", 2, 1),
    ("z", 2, 3), ("core", 0, 0), ("core", 1, 2), ("zx", 0, 3), ("x", 1, 3),
    ("x", 1, 2), ("core", 1, 1), ("core", 2, 1), ("zxy", 0, 1), ("core", 1, 0),
    ("score", 0), ("x", 2, 2), ("core", 2, 2), ("zy", 0, 2), ("zy", 0, 3),
    ("core", 3, 1), ("zxy", 0, 2), ("core", 2, 0), ("score", 1), ("x", 2, 3),
    ("core", 3, 2), ("zxy", 0, 3), ("core", 3, 0), ("score", 2), ("score", 3),
)
LATE = (
    ("pg", 0), ("pg", 1), ("pg", 2), ("pg", 3), ("z", 1, 1),
    ("z", 2, 1), ("z", 1, 2), ("x", 1, 0), ("z", 2, 2), ("z", 3, 1),
    ("z", 1, 3), ("x", 0, 0), ("z", 0, 1), ("x", 2, 0), ("code",),
    ("x", 2, 2), ("z", 2, 3), ("x", 1, 1), ("z", 3, 2), ("val",),
    ("x", 1, 2), ("rsx", 2), ("rsx", 0), ("x", 2, 1), ("zx", 0, 1),
    ("x", 1, 3), ("x", 2, 3), ("rsx", 1), ("proj", 2), ("x", 3, 2),
    ("z", 3, 3), ("z", 0, 2), ("proj", 1), ("rsx", 4), ("x", 3, 0),
    ("rsx", 3), ("zx", 0, 2), ("rsz", 2), ("rsz", 0), ("x", 3, 1),
    ("z", 0, 3), ("zx", 0, 3), ("proj", 0), ("rsz", 1), ("fin", 2),
    ("fin", 1), ("rsy", 2), ("x", 3, 3), ("rsz", 4), ("proj", 3),
    ("rsz", 3), ("col",), ("rsy", 0), ("rsy", 1), ("rsy", 4),
    ("rsy", 3), ("fin", 0), ("fin", 3),
)
CROSS_FIRST = (0,)


def fused(nb, nf, trunk, pre_act, proj_weight, codebook, value_weight, target, low, frac):
    nz, nx = PLANES, nf // (PLANES * CORES)
    pos, width = pre_act.shape
    rows, vrows = codebook.shape[0], value_weight.shape[0]
    bins = value_weight.shape[1]
    depth, total_pos = trunk.shape
    half, vhalf = rows // nb, vrows // nb
    cw = 256
    pieces = width // cw
    cuts = 4
    deep = nb * pos
    ck = half // cuts
    hops = [(0, 0)] + steps(nz)
    by_far = [[h for h in hops if h[1] == far] for far in range(nz)]

    early = []
    for a in range(3):
        for hop in hops:
            early += [("core", a, hop)]
            if hop[1]:
                early += [("z", a, hop)]
            if a == 0 and hop[1]:
                early += [("zy", a, hop, dy) for dy in range(1, nb)]
                for dx in range(1, nx):
                    early += [("zx", a, hop, dx)]
                    early += [("zxy", a, hop, dx, dy) for dy in range(1, nb)]
            else:
                early += [("x", a, hop, dx) for dx in range(1, nx)]
                if a == 0:
                    early += [("d", a, hop, dx, dy) for dx in range(1, nx) for dy in range(1, nb)]
    swap = [(k, dy) for dy in range(1, nb) for k in ("act", "tgt", "stat", "value")]
    swap += [("b", n, dy) for n in range(pieces) for dy in range(1, nb)]
    late = []
    for n in range(pieces):
        for hop in hops:
            late += [("gc", n, hop)]
            if hop[1]:
                late += [("gz", n, hop)]
            if hop[1] == 0 or n not in CROSS_FIRST:
                late += [("gx", n, hop, dx) for dx in range(1, nx)]
            else:
                late += [("gzx", n, hop, dx) for dx in range(1, nx)]
        late += [("p", n, dy) for dy in range(1, nb)]
    for a in range(cuts + 1):
        late += [("rc", a)] + [("rx", a, d) for d in range(1, nx)]
        late += [("rz", a, d) for d in range(1, nz)] + [("ry", a, d) for d in range(1, nb)]
    swap_at, base = number(swap, 0)
    early_send, sends = number(early, base, ("z", "zx"))
    early_recv, recvs = number(early, base)
    late_send, last = number(late, base, ("gz", "gzx"))
    sends = max(sends, last)
    late_recv, recvs = number(late, recvs)
    early_send.update(swap_at)
    early_recv.update(swap_at)
    late_send.update(swap_at)
    late_recv.update(swap_at)

    def kernel(
        pre_in,
        cb_in,
        vw_in,
        tgt_in,
        lo_in,
        fr_in,
        tr_in,
        pw_in,
        trg,
        pj,
        cd,
        vl,
        cb,
        vw,
        pre,
        tgt,
        lo,
        fr,
        tr,
        pw,
        cb_all,
        vw_all,
        gate,
        act_all,
        tgt_all,
        stat,
        back_out,
        back_in,
        logit,
        top,
        vlog,
        delta,
        vd_all,
        dt_all,
        pg,
        part,
        vpart,
        pj_all,
        cd_all,
        vl_all,
        *rest,
    ):
        local_sem, send_sem, recv_sem = rest[-3:]
        p = Place(nb, nf)
        inputs = (cb_in, vw_in, pre_in, tgt_in, lo_in, fr_in, tr_in, pw_in)
        loads = [
            pltpu.make_async_copy(src, dst, local_sem.at[i])
            for i, (src, dst) in enumerate(zip(inputs, (cb, vw, pre, tgt, lo, fr, tr, pw)))
        ]
        for load in loads:
            load.start()
        p.barrier()
        for load in loads[:3]:
            load.wait()
        s = Slots(send_sem, recv_sem, early_send, early_recv, p)
        g = Slots(send_sem, recv_sem, late_send, late_recv, p)

        def under(s, far, f):
            for hop in by_far[far]:
                if far:
                    s.only(lambda hop=hop: has(p, *hop))(lambda: f(hop))
                else:
                    f(hop)

        sub = half // 2
        shards = (
            (vw, vw_all, vhalf, 0, vhalf),
            (cb, cb_all, half, 0, sub),
            (cb, cb_all, half, sub, sub),
        )

        def like(a):
            own, out, piece, skip, size = shards[a]
            at = (0, 0, 0) if a else (0, 0, 0, 0)
            return lambda: out.at[at + (pl.ds(skip, size),)]

        def spot(a, z, x, h):
            own, out, piece, skip, size = shards[a]
            at = (z, x, p.c) if a else (z, x, p.c, h)
            return out.at[at + (pl.ds(skip, size),)]

        def relay(key, at_z, at_x, at_h, **to):
            ref = spot(key[1], at_z, at_x, at_h)
            s.go(key, ref, ref, p.dev(**to), like(key[1]))

        def publish(key, **to):
            own, out, piece, skip, size = shards[key[1]]
            src = own.at[pl.ds(pl.multiple_of(p.b * piece + skip, size), size)]
            s.go(key, src, spot(key[1], p.z, p.x, p.b), p.dev(**to), like(key[1]))

        def farther(kind, a, z, x, far, extra, ways):
            for way in ways:

                @s.only(lambda way=way: feeds(p, way))
                def _():
                    relay((kind, a, (way, far)) + extra, z, x, p.b, z=p.z + way)

        def send_x(a):
            for dx in range(1, nx):
                publish(("x", a, (0, 0), dx), x=p.xx(dx))

        def send_z(a):
            for way in (1, -1):

                @s.only(lambda way=way: feeds(p, way))
                def _():
                    publish(("z", a, (way, 1)), z=p.z + way)

        for name, a in EARLY[:6]:
            (send_x if name == "sx" else send_z)(a)
        cb_all[p.z, p.x, p.c] = cb[pl.ds(pl.multiple_of(p.b * half, half), half), :]
        vw_all[p.z, p.x, p.c] = vw[...].reshape(nb, vhalf, bins)

        def activate(i, carry):
            cols = pl.ds(pl.multiple_of(i * cw, cw), cw)
            v = pre[:, cols].astype(F32)
            sigma = jax.nn.sigmoid(v)
            active = v * sigma
            act_all[p.b, :, cols] = active.astype(BF16)
            gate[:, cols] = sigma * (1.0 + v * (1.0 - sigma))
            return carry

        lax.fori_loop(0, width // cw, activate, 0)
        for load in loads[3:6]:
            load.wait()
        tgt_all[p.b] = tgt[...]
        for dy in range(1, nb):
            for name, ref in (("act", act_all.at[p.b]), ("tgt", tgt_all.at[p.b])):
                g.go((name, dy), ref, ref, p.dev(b=p.bb(dy)))
        top[...] = jnp.full(top.shape, -jnp.inf, F32)
        vlog[...] = jnp.zeros(vlog.shape, F32)

        def from_x0(a):
            for dx in range(1, nx):
                s.arrived(("x", a, (0, 0), dx))
                if a == 0:
                    x = p.xx(-dx)
                    farther("zx", a, p.z, x, 1, (dx,), (1, -1))
                    for dy in range(1, nb):
                        relay(("d", a, (0, 0), dx, dy), p.z, x, p.b, b=p.bb(dy))

        def from_z(a, far):
            def run(hop):
                z = p.z - hop[0] * far
                s.arrived(("z", a, hop))
                if far + 1 < nz:
                    farther("z", a, z, p.x, far + 1, (), hop[:1])
                if a:
                    for dx in range(1, nx):
                        relay(("x", a, hop, dx), z, p.x, p.b, x=p.xx(dx))
                else:
                    for dy in range(1, nb):
                        relay(("zy", a, hop, dy), z, p.x, p.b, b=p.bb(dy))

            under(s, far, run)

        def from_zx(a, far):
            def run(hop):
                z = p.z - hop[0] * far
                for dx in range(1, nx):
                    s.arrived(("zx", a, hop, dx))
                    x = p.xx(-dx)
                    if far + 1 < nz:
                        farther("zx", a, z, x, far + 1, (dx,), hop[:1])
                    for dy in range(1, nb):
                        relay(("zxy", a, hop, dx, dy), z, x, p.b, b=p.bb(dy))

            under(s, far, run)

        def from_x(a, far):
            under(s, far, lambda hop: [s.arrived(("x", a, hop, dx)) for dx in range(1, nx)])

        def landed(kind):
            def wait(a, far):
                def run(hop):
                    for key in early:
                        if key[:3] == (kind, a, hop):
                            s.arrived(key)

                under(s, far, run)

            return wait

        def to_other(far, a):
            own, out, piece, skip, size = shards[a]
            part = pl.ds(skip, size)

            def run(hop):
                z = p.z - hop[0] * far
                ref = out.at[z, :, p.c, part] if a else out.at[z, :, p.c, :, part]
                held = lambda: out.at[0, :, 0, part] if a else out.at[0, :, 0, :, part]
                s.go(("core", a, hop), ref, ref, p.dev(c=1 - p.c), held)

            under(s, far, run)

        def near(j):
            up = (0, 1, 2, 3)[j], (1, 0, 2, 3)[j], (2, 3, 1, 0)[j], (3, 2, 1, 0)[j]
            z = jnp.where(p.z == 0, up[0], up[3])
            z = jnp.where(p.z == 1, up[1], z)
            return jnp.where(p.z == 2, up[2], z)

        def score(j):
            z = near(j)
            for a in range(3):
                landed("core")(a, j)

            plane = nx * CORES * half
            if j == 0:
                for dy in range(1, nb):
                    g.arrived(("act", dy))
            block = dot(
                cb_all[z].reshape(plane, width), act_all[...].reshape(deep, width), ((1,), (1,))
            )
            logit[pl.ds(pl.multiple_of(z * plane, plane), plane), :] = block
            top[...] = jnp.maximum(top[...], jnp.max(block, axis=0, keepdims=True))
            at = pl.ds(pl.multiple_of(z * 256, 256), 256)
            vlog[...] += dot(act_all[p.b, :, at], vw_all[z].reshape(256, bins), ((1,), (0,)))

        acts = dict(
            x0=from_x0, z=from_z, zx=from_zx, x=from_x, d=landed("d"), zy=landed("zy"),
            zxy=landed("zxy"), core=to_other, score=score,
        )
        for name, *where in EARLY[6:]:
            acts[name](*where)
        blocks = nf * half // 256
        best = top[...]

        def grow(i, total):
            at = pl.ds(pl.multiple_of(i * 256, 256), 256)
            e = jnp.exp(logit[at, :] - best)
            logit[at, :] = e
            return total + jnp.sum(e, axis=0, keepdims=True)

        mass = lax.fori_loop(0, blocks, grow, jnp.zeros((1, deep), F32))
        stat[p.b, 0] = jnp.broadcast_to(best, (8, deep))
        stat[p.b, 1] = jnp.broadcast_to(mass, (8, deep))
        for dy in range(1, nb):
            ref = stat.at[p.b]
            g.go(("stat", dy), ref, ref, p.dev(b=p.bb(dy)))
        s.finish()
        high = jnp.max(vlog[...], axis=1, keepdims=True)
        grown = jnp.exp(vlog[...] - high)
        probs = grown * (1.0 / jnp.sum(grown, axis=1, keepdims=True))
        ids = lax.broadcasted_iota(jnp.int32, (pos, bins), 1).astype(F32)
        column = jnp.broadcast_to(lo[...].astype(F32), (pos, pos)).T[:, :1]
        share = jnp.broadcast_to(fr[...].astype(F32) / 1024.0, (pos, pos)).T[:, :1]
        want = jnp.where(ids == column, 1.0 - share, 0.0)
        want = want + jnp.where(ids == column + 1.0, share, 0.0)
        vd_all[p.b] = (probs - want).astype(BF16)

        for dy in range(1, nb):
            g.arrived(("stat", dy))
            g.arrived(("tgt", dy))
        peak = stat[0, 0, :1]
        for b in range(1, nb):
            peak = jnp.maximum(peak, stat[b, 0, :1])
        mass = jnp.zeros((1, deep), F32)
        for b in range(nb):
            mass = mass + stat[b, 1, :1] * jnp.exp(stat[b, 0, :1] - peak)
        scale = jnp.exp(best - peak) * (1.0 / mass)
        aim = jnp.concatenate([tgt_all[b] for b in range(nb)], axis=1)
        group = 256 // half
        row = lax.broadcasted_iota(jnp.int32, (256, deep), 0)
        code_ids = lax.div(row, half) * rows + lax.rem(row, half) + p.b * half

        def differ(i, carry):
            at = pl.ds(pl.multiple_of(i * 256, 256), 256)
            hot = jnp.where(code_ids + i * (group * rows) == aim, 1.0, 0.0)
            d = logit[at, :] * scale - hot
            delta[:, at] = d.T.astype(BF16)
            dt_all[pl.ds(i * group, group)] = d.astype(BF16).reshape(group, half, deep)
            return carry

        lax.fori_loop(0, blocks, differ, 0)

        def back_from(b, n):
            cols = pl.ds(n * cw, cw)
            left = delta[pl.ds(pl.multiple_of(b * pos, pos), pos), :]
            return dot(left, cb_all[:, :, :, :, cols].reshape(nf * half, cw), ((1,), (0,)))

        for n in range(pieces):
            for dy in range(1, nb):
                back_out[dy - 1, n] = back_from(p.bb(dy), n).astype(BF16)
                g.go(
                    ("b", n, dy), back_out.at[dy - 1, n], back_in.at[dy - 1, n], p.dev(b=p.bb(dy))
                )
        for dy in range(1, nb):
            ref = vd_all.at[p.b]
            g.go(("value", dy), ref, ref, p.dev(b=p.bb(dy)))

        def pass_on(n, at_z, at_x, key, **to):
            ref = pg.at[n, at_z, at_x, p.c]
            g.go(key, ref, ref, p.dev(**to), lambda: pg.at[n, 0, 0, 0])

        def onward(n, kind, z, x, far, extra, ways):
            for way in ways:

                @g.only(lambda way=way: feeds(p, way))
                def _():
                    pass_on(n, z, x, (kind, n, (way, far)) + extra, z=p.z + way)

        def across(n, hop):
            for dx in range(1, nx):
                pass_on(n, p.z - hop[0] * hop[1], p.x, ("gx", n, hop, dx), x=p.xx(dx))

        def to_core(n, hop):
            ref = pg.at[n, p.z - hop[0] * hop[1], :, p.c]
            g.go(("gc", n, hop), ref, ref, p.dev(c=1 - p.c), lambda: pg.at[n, 0, :, 0])

        def head(n):
            cols = pl.ds(n * cw, cw)
            back = back_from(p.b, n)
            back = back + dot(vd_all[p.b], vw_all[n].reshape(cw, bins), ((1,), (1,)))
            for dy in range(1, nb):
                g.arrived(("b", n, dy))
                back = back + back_in[dy - 1, n].astype(F32)
            pg[n, p.z, p.x, p.c] = (back * gate[:, cols]).astype(BF16)
            if n in CROSS_FIRST:
                across(n, (0, 0))
            onward(n, "gz", p.z, p.x, 1, (), (1, -1))
            if n not in CROSS_FIRST:
                across(n, (0, 0))

        def grad_z(n, far):
            def run(hop):
                z = p.z - hop[0] * far
                g.arrived(("gz", n, hop))
                if far + 1 < nz:
                    onward(n, "gz", z, p.x, far + 1, (), hop[:1])
                if n not in CROSS_FIRST:
                    across(n, hop)

            under(g, far, run)

        def grad_x(n, far):
            def run(hop):
                for dx in range(1, nx):
                    g.arrived(("gx", n, hop, dx))
                    if n in CROSS_FIRST:
                        onward(n, "gzx", p.z, p.xx(-dx), 1, (dx,), (1, -1))
                to_core(n, hop)

            under(g, far, run)

        def grad_zx(n, far):
            def run(hop):
                for dx in range(1, nx):
                    g.arrived(("gzx", n, hop, dx))
                    if far + 1 < nz:
                        onward(n, "gzx", p.z - hop[0] * far, p.xx(-dx), far + 1, (dx,), hop[:1])
                to_core(n, hop)

            under(g, far, run)

        arrays = []
        for a in range(cuts + 1):
            if a < cuts:
                own, out = part.at[:, :, :, pl.ds(a * ck, ck)], cd_all.at[:, pl.ds(a * ck, ck)]
            else:
                own, out = vpart.at[:, :, :, p.b], vl_all
            arrays.append((own, out) + tuple(rest[6 * a : 6 * a + 6]))

        def to_sum(a):
            own, out, core, *_ = arrays[a]
            g.go(("rc", a), own.at[:, :, 1 - p.c], core, p.dev(c=1 - p.c))

        def code():
            def block(i, carry):
                z = i // (width // cw)
                cols = pl.ds(pl.multiple_of((i % (width // cw)) * cw, cw), cw)
                left = dt_all[pl.ds(z * nx * CORES, nx * CORES)].reshape(nx * CORES * half, deep)
                right = act_all[:, :, cols].reshape(deep, cw)
                product = dot(left, right, ((1,), (0,)))
                part[z, :, :, :, cols] = product.astype(BF16).reshape(nx, CORES, half, cw)
                return carry

            lax.fori_loop(0, nz * (width // cw), block, 0)
            for a in range(cuts):
                to_sum(a)

        def val():
            for dy in range(1, nb):
                g.arrived(("value", dy))

            def block(z, carry):
                cols = pl.ds(pl.multiple_of(z * 256, 256), 256)
                left = act_all[:, :, cols].reshape(deep, 256)
                product = dot(left, vd_all[...].reshape(deep, bins), ((0,), (0,)))
                vpart[z] = product.astype(BF16).reshape(nx, CORES, nb, vhalf, bins)
                return carry

            lax.fori_loop(0, nz, block, 0)
            to_sum(cuts)

        def rsx(a):
            own, out, core, xin, xsend, acc, zin, zsend = arrays[a]
            g.arrived(("rc", a))
            for dx in range(1, nx):
                x = p.xx(dx)
                for z in range(nz):
                    both = own[z, x, p.c].astype(F32) + core[z, x].astype(F32)
                    xsend[dx - 1, z] = both.astype(BF16)
                g.go(("rx", a, dx), xsend.at[dx - 1], xin.at[dx - 1], p.dev(x=x))
            for z in range(nz):
                acc[z] = own[z, p.x, p.c].astype(F32) + core[z, p.x].astype(F32)

        def rsz(a):
            own, out, core, xin, xsend, acc, zin, zsend = arrays[a]
            for dx in range(1, nx):
                g.arrived(("rx", a, dx))
                acc[...] += xin[dx - 1].astype(F32)
            for dz in [2, 1, 3]:
                z = p.zz(dz)
                zsend[dz - 1] = acc[z].astype(BF16)
                g.go(("rz", a, dz), zsend.at[dz - 1], zin.at[dz - 1], p.dev(z=z))

        def rsy(a):
            own, out, core, xin, xsend, acc, zin, zsend = arrays[a]
            total = acc[p.z]
            for dz in range(1, nz):
                g.arrived(("rz", a, dz))
                total = total + zin[dz - 1].astype(F32)
            out[p.b] = total.astype(BF16)
            for dy in range(1, nb):
                g.go(("ry", a, dy), out.at[p.b], out.at[p.b], p.dev(b=p.bb(dy)))

        def proj(n):
            for far in range(nz):
                under(g, far, lambda hop: g.arrived(("gc", n, hop)))

            def block(i, carry):
                at = pl.ds(pl.multiple_of(i * 192, 192), 192)
                pj_all[p.b, n, at, :] = jnp.dot(
                    tr[at, :], pg[n].reshape(total_pos, cw), preferred_element_type=F32
                ).astype(BF16)
                return carry

            lax.fori_loop(0, depth // 192, block, 0)
            for dy in range(1, nb):
                ref = pj_all.at[p.b, n]
                g.go(("p", n, dy), ref, ref, p.dev(b=p.bb(dy)))

        def col():
            def block(i, carry):
                at = pl.ds(pl.multiple_of(i * 256, 256), 256)
                z, x = i // nx, i % nx
                total = 0.0
                for n in range(pieces):
                    there = pg[n, z, x].reshape(256, cw)
                    total = total + dot(pw[:, pl.ds(n * cw, cw)], there, ((1,), (1,)))
                trg[:, at] = total.astype(BF16)
                return carry

            lax.fori_loop(0, nz * nx, block, 0)

        def fin(n):
            for dy in range(1, nb):
                g.arrived(("p", n, dy))
            total = pj_all[0, n].astype(F32)
            for b in range(1, nb):
                total = total + pj_all[b, n].astype(F32)
            pj[:, pl.ds(n * cw, cw)] = total

        for load in loads[6:]:
            load.wait()
        acts = dict(
            pg=head, z=grad_z, x=grad_x, zx=grad_zx, code=code, val=val, rsx=rsx, rsz=rsz, rsy=rsy,
            proj=proj, col=col, fin=fin,
        )
        for name, *where in LATE:
            acts[name](*where)
        for a in range(cuts + 1):
            for dy in range(1, nb):
                g.arrived(("ry", a, dy))
        for b in range(nb):
            cd[pl.ds(b * half, half), :] = cd_all[b].astype(F32)
            vl[pl.ds(b * vhalf, vhalf), :] = vl_all[b].astype(F32)
        g.finish()

    def buffers(r, k):
        return [
            pltpu.VMEM((nz, nx, r, k), BF16),
            pltpu.VMEM((max(nx - 1, 1), nz, r, k), BF16),
            pltpu.VMEM((max(nx - 1, 1), nz, r, k), BF16),
            pltpu.VMEM((nz, r, k), F32),
            pltpu.VMEM((nz - 1, r, k), BF16),
            pltpu.VMEM((nz - 1, r, k), BF16),
        ]

    anywhere = pl.BlockSpec(memory_space=pl.ANY)
    stay = pl.BlockSpec(memory_space=pltpu.HBM)
    results = pl.pallas_call(
        kernel,
        out_shape=[
            jax.ShapeDtypeStruct((depth, total_pos), BF16),
            jax.ShapeDtypeStruct((depth, width), F32),
            jax.ShapeDtypeStruct((rows, width), F32),
            jax.ShapeDtypeStruct((vrows, bins), F32),
        ],
        in_specs=[stay] * 8,
        out_specs=[pl.BlockSpec(memory_space=pltpu.VMEM)] * 4,
        scratch_shapes=[
            pltpu.VMEM((rows, width), BF16),
            pltpu.VMEM((vrows, bins), BF16),
            pltpu.VMEM((pos, width), BF16),
            pltpu.VMEM((1, pos), jnp.int32),
            pltpu.VMEM((1, pos), jnp.int32),
            pltpu.VMEM((1, pos), jnp.int32),
            pltpu.VMEM((depth, total_pos), BF16),
            pltpu.VMEM((depth, width), BF16),
            pltpu.VMEM((nz, nx, CORES, half, width), BF16),
            pltpu.VMEM((nz, nx, CORES, nb, vhalf, bins), BF16),
            pltpu.VMEM((pos, width), F32),
            pltpu.VMEM((nb, pos, width), BF16),
            pltpu.VMEM((nb, 1, pos), jnp.int32),
            pltpu.VMEM((nb, 2, 8, deep), F32),
            pltpu.VMEM((nb - 1, pieces, pos, cw), BF16),
            pltpu.VMEM((nb - 1, pieces, pos, cw), BF16),
            pltpu.VMEM((nf * half, deep), F32),
            pltpu.VMEM((1, deep), F32),
            pltpu.VMEM((pos, bins), F32),
            pltpu.VMEM((deep, nf * half), BF16),
            pltpu.VMEM((nb, pos, bins), BF16),
            pltpu.VMEM((nf, half, nb * pos), BF16),
            pltpu.VMEM((pieces, nz, nx, CORES, pos, cw), BF16),
            pltpu.VMEM((nz, nx, CORES, half, width), BF16),
            pltpu.VMEM((nz, nx, CORES, nb, vhalf, bins), BF16),
            pltpu.VMEM((nb, pieces, depth, cw), BF16),
            pltpu.VMEM((nb, half, width), BF16),
            pltpu.VMEM((nb, vhalf, bins), BF16),
        ]
        + buffers(ck, width) * cuts
        + buffers(vhalf, bins)
        + [
            pltpu.SemaphoreType.DMA((8,)),
            pltpu.SemaphoreType.DMA((sends,)),
            pltpu.SemaphoreType.DMA((recvs,)),
        ],
        compiler_params=pltpu.CompilerParams(
            collective_id=4, has_side_effects=True, vmem_limit_bytes=44 << 20
        ),
    )(
        *(
            pltpu.with_memory_space_constraint(x, pltpu.HBM)
            for x in (
                pre_act, codebook, value_weight, target, low, frac, trunk, proj_weight,
            )
        )
    )

    def hand_over(*refs):
        copies = [
            pltpu.make_async_copy(refs[i], refs[4 + i], refs[8].at[i]) for i in range(4)
        ]
        for copy in copies:
            copy.start()
        for copy in copies:
            copy.wait()

    return pl.pallas_call(
        hand_over,
        out_shape=[jax.ShapeDtypeStruct(r.shape, r.dtype) for r in results],
        in_specs=[anywhere] * 4,
        out_specs=[stay] * 4,
        scratch_shapes=[pltpu.SemaphoreType.DMA((4,))],
        compiler_params=pltpu.CompilerParams(vmem_limit_bytes=1 << 20),
    )(*results)


def make_body(nb, nf):
    nz, nx = PLANES, nf // (PLANES * CORES)

    def body(
        trunk, pre_act, proj_weight, codebook, value_weight, code_target, value_bin, value_frac
    ):
        if fits(nb, nf, codebook, value_weight, trunk.shape[0], pre_act.shape[0]):
            row = (1, pre_act.shape[0])
            return fused(
                nb,
                nf,
                trunk,
                pre_act,
                proj_weight,
                codebook,
                value_weight,
                code_target.reshape(row),
                value_bin.reshape(row),
                value_frac.reshape(row),
            )
        all_codes, bins_weight = gather_weights(nb, nf, codebook, value_weight)
        rows, width = pre_act.shape
        num_codes = all_codes.shape[0]
        num_bins = bins_weight.shape[1]
        pre_value = pre_act.astype(F32)
        gate_sigma = jax.nn.sigmoid(pre_value)
        active = (pre_value * gate_sigma).astype(BF16)
        code_logits = jnp.einsum("rk,ck->rc", active, all_codes, preferred_element_type=F32)
        code_probs = jax.nn.softmax(code_logits, axis=-1)
        code_ids = lax.broadcasted_iota(jnp.int32, (1, num_codes), 1)
        one_hot = (code_target[:, None] == code_ids).astype(F32)
        code_delta = (code_probs - one_hot).astype(BF16)
        value_logits = jnp.dot(active, bins_weight, preferred_element_type=F32)
        value_probs = jax.nn.softmax(value_logits, axis=-1)
        bin_ids = lax.broadcasted_iota(jnp.int32, (1, num_bins), 1)
        fraction = value_frac.astype(F32)[:, None] / 1024.0
        target = jnp.where(bin_ids == value_bin[:, None], 1.0 - fraction, 0.0)
        target = target + jnp.where(bin_ids == value_bin[:, None] + 1, fraction, 0.0)
        value_delta = (value_probs - target).astype(BF16)
        backward = jnp.dot(code_delta, all_codes, preferred_element_type=F32)
        backward = backward + jnp.einsum(
            "rb,kb->rk", value_delta, bins_weight, preferred_element_type=F32
        )
        pre_grad = (backward * gate_sigma * (1.0 + pre_value * (1.0 - gate_sigma))).astype(BF16)
        own = codebook.shape[0] // nb
        delta_t = code_delta.T.reshape(nf, nb, own, rows).swapaxes(0, 1)
        delta_t = delta_t.reshape(nb, nf * own, rows)
        pieces, act_all, dt_all, vd_all = gather_grads(
            nb, nf, pre_grad, active, delta_t, value_delta
        )
        code_part = jnp.dot(dt_all, act_all, preferred_element_type=F32)
        code_part = code_part.astype(BF16).reshape(nz, nx, CORES, own, width)
        vown = value_weight.shape[0] // nb
        if vown % 16 == 0:
            value_part = (act_all, vd_all)
        else:
            value_part = jnp.einsum("rk,rb->kb", act_all, vd_all, preferred_element_type=F32)
            value_part = value_part.astype(BF16)
            value_part = (value_part.reshape(nz, nx, CORES, nb, vown, num_bins),)
        out_cols, proj_all, code_all, value_all = reduce_grads(
            nb, nf, trunk, proj_weight, pieces, code_part, value_part
        )
        proj_grad = jnp.sum(proj_all.astype(F32), axis=0)
        code_grad = code_all.reshape(nb * own, width).astype(F32)
        value_grad = value_all.reshape(nb * vown, num_bins).astype(F32)
        return (out_cols, proj_grad, code_grad, value_grad)

    return body


def solution(mesh):
    in_specs = (
        P("fsdp", "batch"),
        P(("batch", "fsdp"), None),
        P("fsdp", None),
        P("fsdp", None),
        P("fsdp", None),
        P(("batch", "fsdp")),
        P(("batch", "fsdp")),
        P(("batch", "fsdp")),
    )
    out_specs = (P("fsdp", "batch"), P("fsdp", None), P("fsdp", None), P("fsdp", None))
    body = make_body(mesh.shape["batch"], mesh.shape["fsdp"])
    return jax.shard_map(body, mesh=mesh, in_specs=in_specs, out_specs=out_specs, check_vma=False)
```

```python
import jax
import jax.numpy as jnp
from jax import lax
from jax.experimental import pallas as pl
from jax.experimental.pallas import tpu as pltpu
from jax.sharding import PartitionSpec as P

MESH = pl.DeviceIdType.MESH
BF16 = jnp.bfloat16
F32 = jnp.float32
CORES = 2
PLANES = 4


class Place:
    def __init__(self, nb, nf):
        self.nb, self.nz = nb, PLANES
        self.nx = nf // (PLANES * CORES)
        f = lax.axis_index("fsdp")
        self.b = lax.axis_index("batch")
        self.z = f // (self.nx * CORES)
        self.x = (f // CORES) % self.nx
        self.c = f % CORES

    def dev(self, b=None, z=None, x=None, c=None):
        b = self.b if b is None else b
        z = self.z if z is None else z
        x = self.x if x is None else x
        c = self.c if c is None else c
        return (b, (z * self.nx + x) * CORES + c)

    def zz(self, d):
        return lax.rem(self.z + d + self.nz, self.nz)

    def xx(self, d):
        return lax.rem(self.x + d + self.nx, self.nx)

    def bb(self, d):
        return lax.rem(self.b + d + self.nb, self.nb)

    def barrier(self):
        sem = pltpu.get_barrier_semaphore()
        peers = [self.dev(z=self.zz(d)) for d in range(1, self.nz)]
        peers += [self.dev(x=self.xx(d)) for d in range(1, self.nx)]
        peers += [self.dev(b=self.bb(d)) for d in range(1, self.nb)]
        peers += [self.dev(c=1 - self.c)]
        for peer in peers:
            pl.semaphore_signal(sem, inc=1, device_id=peer, device_id_type=MESH)
        pl.semaphore_wait(sem, len(peers))


def steps(nz):
    return [(way, far) for far in range(1, nz) for way in (1, -1)]


class Sends:
    def __init__(self, send_sem, recv_sem, keys, place):
        self.send_sem, self.recv_sem, self.place = send_sem, recv_sem, place
        self.at = {k: i for i, k in enumerate(keys)}
        self.like = {}
        self.started = []
        self.when = ()

    def make(self, key, src, dst, dev):
        i = self.at[key]
        return pltpu.make_async_remote_copy(
            src_ref=src,
            dst_ref=dst,
            send_sem=self.send_sem.at[i],
            recv_sem=self.recv_sem.at[i],
            device_id=dev,
            device_id_type=MESH,
        )

    def go(self, key, src, dst, dev, like=None):
        self.make(key, src, dst, dev).start()
        self.like[key] = dst if like is None else like
        self.started.append((key, self.when))

    def waiter(self, key):
        ref = self.like[key]
        ref = ref() if callable(ref) else ref
        return self.make(key, ref, ref, self.place.dev(c=1 - self.place.c))

    def arrived(self, key):
        self.waiter(key).wait_recv()

    def finish(self):
        for key, whens in self.started:

            def wait(key=key):
                self.waiter(key).wait_send()

            if whens:
                met = whens[0]()
                for when in whens[1:]:
                    met = jnp.logical_and(met, when())
                pl.when(met)(wait)
            else:
                wait()

    def only(self, when):
        def run(f):
            outer = self.when
            self.when = outer + (when,)

            @pl.when(when())
            def _():
                f()

            self.when = outer

        return run


def call(kernel, outs, scratch, cid, *args):
    return pl.pallas_call(
        kernel,
        out_shape=outs,
        in_specs=[pl.BlockSpec(memory_space=pltpu.VMEM)] * len(args),
        out_specs=[pl.BlockSpec(memory_space=pltpu.VMEM)] * len(outs),
        scratch_shapes=scratch,
        compiler_params=pltpu.CompilerParams(collective_id=cid, has_side_effects=True),
    )(*args)


def has(p, way, far):
    return p.z >= far if way == 1 else p.z + far < p.nz


def feeds(p, way):
    return p.z + 1 < p.nz if way == 1 else p.z >= 1


def gather_weights_keys(nb, nx, nz):
    keys = []
    for a in (0, 1):
        keys += [(a, "c", 0)]
        for hop in [(0, 0)] + steps(nz):
            if hop[1]:
                keys += [(a, "z", hop), (a, "cz", hop)]
                for dy in range(1, nb):
                    keys += [(a, "y", hop, dy), (a, "cy", hop, dy)]
            for dx in range(1, nx):
                keys += [(a, "x", hop, dx), (a, "cx", hop, dx)]
                for dy in range(1, nb):
                    keys += [(a, "d", hop, dx, dy), (a, "cd", hop, dx, dy)]
    return keys


def gather_weights(nb, nf, codebook, value_weight):
    nz, nx = PLANES, nf // (PLANES * CORES)
    keys = gather_weights_keys(nb, nx, nz)
    rows, width = codebook.shape
    vrows, bins = value_weight.shape

    def kernel(cb, vw, cb_out, vw_out, send_sem, recv_sem):
        p = Place(nb, nf)
        p.barrier()
        s = Sends(send_sem, recv_sem, keys, p)
        arrays = ((0, cb, cb_out), (1, vw, vw_out))

        def spot(out, z, x, h):
            return out.at[z, x, p.c, h]

        def relay(key, out, at_z, at_x, at_h, **to):
            ref = spot(out, at_z, at_x, at_h)
            s.go(key, ref, ref, p.dev(**to), lambda: out.at[0, 0, 0, 0])

        for a, own, out in arrays:
            here = spot(out, p.z, p.x, p.b)
            for way in (1, -1):

                @s.only(lambda way=way: feeds(p, way))
                def _(a=a, own=own, out=out, here=here, way=way):
                    s.go((a, "z", (way, 1)), own.at[p.b], here, p.dev(z=p.z + way), lambda: out.at[0, 0, 0, 0])

            for dx in range(1, nx):
                s.go((a, "x", (0, 0), dx), own.at[p.b], here, p.dev(x=p.xx(dx)))
            s.go((a, "c", 0), own, out.at[p.z, p.x, p.c], p.dev(c=1 - p.c))
        for a, own, out in arrays:
            out[p.z, p.x, p.c] = own[...]

        def from_z(hop):
            way, far = hop
            z = p.z - way * far
            for a, own, out in arrays:
                s.arrived((a, "z", hop))
                if far + 1 < nz:

                    @s.only(lambda way=way: feeds(p, way))
                    def _(a=a, out=out):
                        relay((a, "z", (way, far + 1)), out, z, p.x, p.b, z=p.z + way)

                for dx in range(1, nx):
                    relay((a, "x", hop, dx), out, z, p.x, p.b, x=p.xx(dx))
                for dy in range(1, nb):
                    relay((a, "y", hop, dy), out, z, p.x, p.b, b=p.bb(dy))
                relay((a, "cz", hop), out, z, p.x, p.b, c=1 - p.c)

        def from_plane(hop):
            way, far = hop
            z = p.z - way * far
            for a, own, out in arrays:
                for dx in range(1, nx):
                    x = p.xx(-dx)
                    s.arrived((a, "x", hop, dx))
                    if far % 2 == 0:
                        for dy in range(1, nb):
                            relay((a, "d", hop, dx, dy), out, z, x, p.b, b=p.bb(dy))
                    relay((a, "cx", hop, dx), out, z, x, p.b, c=1 - p.c)
                if far:
                    for dy in range(1, nb):
                        h = p.bb(-dy)
                        s.arrived((a, "y", hop, dy))
                        if far % 2:
                            for dx in range(1, nx):
                                relay((a, "d", hop, dx, dy), out, z, p.x, h, x=p.xx(dx))
                        relay((a, "cy", hop, dy), out, z, p.x, h, c=1 - p.c)

        def from_diagonal(hop):
            way, far = hop
            for a, own, out in arrays:
                for dx in range(1, nx):
                    for dy in range(1, nb):
                        s.arrived((a, "d", hop, dx, dy))
                        relay(
                            (a, "cd", hop, dx, dy),
                            out,
                            p.z - way * far,
                            p.xx(-dx),
                            p.bb(-dy),
                            c=1 - p.c,
                        )

        def from_core(hop):
            for key in keys:
                if key[1] in ("cz", "cx", "cy", "cd") and key[2] == hop:
                    s.arrived(key)

        def under(hop, f):
            if hop[1]:
                s.only(lambda: has(p, *hop))(lambda: f(hop))
            else:
                f(hop)

        hops = [(0, 0)] + steps(nz)
        by_far = [[h for h in hops if h[1] == far] for far in range(nz)]
        for far in range(nz + 2):
            if 1 <= far < nz:
                for hop in by_far[far]:
                    under(hop, from_z)
            if 1 <= far <= nz:
                for hop in by_far[far - 1]:
                    under(hop, from_plane)
            if far >= 2:
                for hop in by_far[far - 2]:
                    under(hop, from_diagonal)
        for a in (0, 1):
            s.arrived((a, "c", 0))
        for hop in hops:
            under(hop, from_core)
        s.finish()

    cb_out, vw_out = call(
        kernel,
        [
            jax.ShapeDtypeStruct((nz, nx, CORES, nb, rows // nb, width), BF16),
            jax.ShapeDtypeStruct((nz, nx, CORES, nb, vrows // nb, bins), BF16),
        ],
        [pltpu.SemaphoreType.DMA((len(keys),)), pltpu.SemaphoreType.DMA((len(keys),))],
        1,
        codebook.reshape(nb, rows // nb, width),
        value_weight.reshape(nb, vrows // nb, bins),
    )
    return cb_out.reshape(nf * rows, width), vw_out.reshape(nf * vrows, bins)


def gather_grads(nb, nf, pre_grad, active, delta_t, value_delta):
    nz, nx = PLANES, nf // (PLANES * CORES)
    rows, width = pre_grad.shape
    bins = value_delta.shape[1]
    half = delta_t.shape[1]
    hops = [(0, 0)] + steps(nz)
    keys = [("c", 0)]
    for hop in hops:
        if hop[1]:
            keys += [("z", hop), ("cz", hop)]
        for dx in range(1, nx):
            keys += [("x", hop, dx), ("cx", hop, dx)]
    keys += [(k, dy) for dy in range(1, nb) for k in ("act", "delta", "value")]

    def kernel(pg, act, dt, vd, pg_out, act_out, dt_out, vd_out, send_sem, recv_sem):
        p = Place(nb, nf)
        p.barrier()
        s = Sends(send_sem, recv_sem, keys, p)
        here, like = pg_out.at[p.z, p.x, p.c], pg_out.at[0, 0, 0]
        mine = pl.ds(pl.multiple_of(p.b * rows, rows), rows)
        for way in (1, -1):

            @s.only(lambda way=way: feeds(p, way))
            def _(way=way):
                s.go(("z", (way, 1)), pg, here, p.dev(z=p.z + way), like)

        for dx in range(1, nx):
            s.go(("x", (0, 0), dx), pg, here, p.dev(x=p.xx(dx)))
        for dy in range(1, nb):
            to = p.bb(dy)
            s.go(("act", dy), act, act_out.at[p.b], p.dev(b=to))
            s.go(("delta", dy), dt.at[to], dt_out.at[:, mine], p.dev(b=to))
            s.go(("value", dy), vd, vd_out.at[p.b], p.dev(b=to))
        s.go(("c", 0), pg, here, p.dev(c=1 - p.c))
        pg_out[p.z, p.x, p.c] = pg[...]
        act_out[p.b] = act[...]
        dt_out[:, mine] = dt[p.b]
        vd_out[p.b] = vd[...]

        def from_z(hop):
            way, far = hop
            ref = pg_out.at[p.z - way * far, p.x, p.c]
            s.arrived(("z", hop))
            if far + 1 < nz:

                @s.only(lambda way=way: feeds(p, way))
                def _():
                    s.go(("z", (way, far + 1)), ref, ref, p.dev(z=p.z + way), like)

            for dx in range(1, nx):
                s.go(("x", hop, dx), ref, ref, p.dev(x=p.xx(dx)), like)
            s.go(("cz", hop), ref, ref, p.dev(c=1 - p.c), like)

        def from_plane(hop):
            way, far = hop
            for dx in range(1, nx):
                s.arrived(("x", hop, dx))
                ref = pg_out.at[p.z - way * far, p.xx(-dx), p.c]
                s.go(("cx", hop, dx), ref, ref, p.dev(c=1 - p.c), like)

        def from_core(hop):
            for key in keys:
                if key[0] in ("cz", "cx") and key[1] == hop:
                    s.arrived(key)

        def under(hop, f):
            if hop[1]:
                s.only(lambda: has(p, *hop))(lambda: f(hop))
            else:
                f(hop)

        for far in range(nz + 1):
            for hop in hops:
                if far and hop[1] == far:
                    under(hop, from_z)
            for hop in hops:
                if hop[1] == far - 1:
                    under(hop, from_plane)
        for key in keys:
            if key[0] in ("act", "delta", "value", "c"):
                s.arrived(key)
        for hop in hops:
            under(hop, from_core)
        s.finish()

    pieces, act_all, dt_all, vd_all = call(
        kernel,
        [
            jax.ShapeDtypeStruct((nz, nx, CORES, rows, width), BF16),
            jax.ShapeDtypeStruct((nb, rows, width), BF16),
            jax.ShapeDtypeStruct((half, nb * rows), BF16),
            jax.ShapeDtypeStruct((nb, rows, bins), BF16),
        ],
        [pltpu.SemaphoreType.DMA((len(keys),)), pltpu.SemaphoreType.DMA((len(keys),))],
        2,
        pre_grad,
        active,
        delta_t,
        value_delta,
    )
    return (
        pieces.reshape(nf * rows, width),
        act_all.reshape(nb * rows, width),
        dt_all,
        vd_all.reshape(nb * rows, bins),
    )


def reduce_grads(nb, nf, trunk, proj_weight, pieces, code, value):
    nz, nx = PLANES, nf // (PLANES * CORES)
    depth = trunk.shape[0]
    width = pieces.shape[1]
    block = next(n for n in (192, 96, 64, 32, 16) if depth % n == 0)
    blocks = depth // block
    lanes = 256
    cuts = 2 if code.shape[3] % 32 == 0 else 1
    crows = code.shape[3] // cuts
    fused = len(value) == 2
    bins = value[-1].shape[-1]
    vrows = width // (nf * nb) if fused else value[0].shape[4]
    chunks = range(cuts + 1)
    keys = [("p", i, dy) for i in range(blocks) for dy in range(1, nb)]
    for a in chunks:
        keys += [(a, "c")] + [(a, "x", d) for d in range(1, nx)]
        keys += [(a, "z", d) for d in range(1, nz)] + [(a, "y", d) for d in range(1, nb)]

    def kernel(tr, pw, pg, cd, *rest):
        factors, rest = rest[: len(value)], rest[len(value) :]
        (tr_out, pj_out, cd_out, vl_out), rest = rest[:4], rest[4:]
        send_sem, recv_sem = rest[-2:]
        vl = rest[-3] if fused else factors[0]
        p = Place(nb, nf)
        p.barrier()
        s = Sends(send_sem, recv_sem, keys, p)
        arrays = []
        for a in chunks:
            if a < cuts:
                part = pl.ds(a * crows, crows)
                own, out = cd.at[:, :, :, part], cd_out.at[:, part]
            else:
                own, out = vl.at[:, :, :, p.b], vl_out
            arrays.append((a, own, out) + tuple(rest[6 * a : 6 * a + 6]))
        for a, own, out, core, *_ in arrays:
            if a == cuts and fused:
                product = lax.dot_general(
                    factors[0][...],
                    factors[1][...],
                    (((0,), (0,)), ((), ())),
                    preferred_element_type=F32,
                )
                vl[...] = product.astype(BF16).reshape(nz, nx, CORES, nb, vrows, bins)
            s.go((a, "c"), own.at[:, :, 1 - p.c], core, p.dev(c=1 - p.c))

        def multiply(i):
            rows = pl.ds(i * block, block)

            def tile(n, carry):
                cols = pl.ds(pl.multiple_of(n * lanes, lanes), lanes)
                pj_out[p.b, rows, cols] = jnp.dot(
                    tr[rows, :], pg[:, cols], preferred_element_type=F32
                ).astype(BF16)
                return carry

            lax.fori_loop(0, width // lanes, tile, 0)
            for dy in range(1, nb):
                ref = pj_out.at[p.b, rows]
                s.go(("p", i, dy), ref, ref, p.dev(b=p.bb(dy)))

        def columns(n, carry):
            cols = pl.ds(pl.multiple_of(n * lanes, lanes), lanes)
            tr_out[:, cols] = lax.dot_general(
                pw[...], pg[cols, :], (((1,), (1,)), ((), ())), preferred_element_type=F32
            ).astype(BF16)
            return carry

        multiply(0)
        for a, own, out, core, xin, xsend, acc, zin, zsend in arrays:
            s.arrived((a, "c"))
            for dx in range(1, nx):
                x = p.xx(dx)
                for z in range(nz):
                    both = own[z, x, p.c].astype(F32) + core[z, x].astype(F32)
                    xsend[dx - 1, z] = both.astype(BF16)
                s.go((a, "x", dx), xsend.at[dx - 1], xin.at[dx - 1], p.dev(x=x))
            for z in range(nz):
                acc[z] = own[z, p.x, p.c].astype(F32) + core[z, p.x].astype(F32)
        for i in range(1, blocks):
            multiply(i)
        for a, own, out, core, xin, xsend, acc, zin, zsend in arrays:
            for dx in range(1, nx):
                s.arrived((a, "x", dx))
                acc[...] += xin[dx - 1].astype(F32)
            for dz in [2, 1, 3]:
                z = p.zz(dz)
                zsend[dz - 1] = acc[z].astype(BF16)
                s.go((a, "z", dz), zsend.at[dz - 1], zin.at[dz - 1], p.dev(z=z))
        for a, own, out, core, xin, xsend, acc, zin, zsend in arrays:
            if a == 0:
                lax.fori_loop(0, pieces.shape[0] // lanes, columns, 0)
            total = acc[p.z]
            for dz in range(1, nz):
                s.arrived((a, "z", dz))
                total = total + zin[dz - 1].astype(F32)
            out[p.b] = total.astype(BF16)
            for dy in range(1, nb):
                s.go((a, "y", dy), out.at[p.b], out.at[p.b], p.dev(b=p.bb(dy)))
        for key in keys:
            if key[0] == "p" or key[1] == "y":
                s.arrived(key)
        s.finish()

    def buffers(r, k):
        return [
            pltpu.VMEM((nz, nx, r, k), BF16),
            pltpu.VMEM((max(nx - 1, 1), nz, r, k), BF16),
            pltpu.VMEM((max(nx - 1, 1), nz, r, k), BF16),
            pltpu.VMEM((nz, r, k), F32),
            pltpu.VMEM((nz - 1, r, k), BF16),
            pltpu.VMEM((nz - 1, r, k), BF16),
        ]

    return call(
        kernel,
        [
            jax.ShapeDtypeStruct((depth, pieces.shape[0]), BF16),
            jax.ShapeDtypeStruct((nb, depth, width), BF16),
            jax.ShapeDtypeStruct((nb, crows * cuts, width), BF16),
            jax.ShapeDtypeStruct((nb, vrows, bins), BF16),
        ],
        buffers(crows, width) * cuts
        + buffers(vrows, bins)
        + [pltpu.VMEM((nz, nx, CORES, nb, vrows, bins), BF16)] * fused
        + [pltpu.SemaphoreType.DMA((len(keys),)), pltpu.SemaphoreType.DMA((len(keys),))],
        3,
        trunk,
        proj_weight,
        pieces,
        code,
        *value,
    )


def dot(a, b, dims):
    return lax.dot_general(a, b, (dims, ((), ())), preferred_element_type=F32)


class Slots(Sends):
    def __init__(self, send_sem, recv_sem, send_at, recv_at, place):
        super().__init__(send_sem, recv_sem, (), place)
        self.send_at, self.recv_at = send_at, recv_at

    def join(self, key, like):
        self.like[key] = like
        self.started.append((key, ()))

    def make(self, key, src, dst, dev):
        return pltpu.make_async_remote_copy(
            src_ref=src,
            dst_ref=dst,
            send_sem=self.send_sem.at[self.send_at[key]],
            recv_sem=self.recv_sem.at[self.recv_at[key]],
            device_id=dev,
            device_id_type=MESH,
        )


def number(keys, first, apart=()):
    at, names = {}, {}
    for key in keys:
        name = key[:2] if key[0] in ("rz", "gc") else key
        if key[0] not in apart:
            name = tuple((0, k[1]) if isinstance(k, tuple) and k[1] > 1 else k for k in name)
        at[key] = first + names.setdefault(name, len(names))
    return at, first + len(names)


def fits(nb, nf, codebook, value_weight, depth, pos):
    nx = nf // (PLANES * CORES)
    rows, width = codebook.shape
    vrows = value_weight.shape[0]
    half, vhalf = rows // nb, vrows // nb
    return (
        nb > 1
        and nb * half == rows
        and nb * vhalf == vrows
        and half % 64 == 0
        and vhalf % 32 == 0
        and CORES * rows == 256
        and nx * CORES * vrows == 256
        and width == PLANES * 256
        and depth % 192 == 0
        and pos * CORES == 256
    )


EARLY = (
    ("sz", 1), ("sz", 0), ("sx", 0), ("sx", 2), ("sz", 2),
    ("sx", 1), ("z", 1, 1), ("x0", 0), ("z", 0, 1), ("z", 2, 1),
    ("x0", 1), ("x0", 2), ("core", 0, 1), ("z", 1, 2), ("z", 0, 2),
    ("core", 0, 2), ("zx", 0, 1), ("z", 2, 2), ("x", 1, 1), ("z", 0, 3),
    ("zy", 0, 1), ("z", 1, 3), ("d", 0, 0), ("zx", 0, 2), ("x", 2, 1),
    ("z", 2, 3), ("core", 0, 0), ("core", 1, 2), ("zx", 0, 3), ("x", 1, 3),
    ("x", 1, 2), ("core", 1, 1), ("core", 2, 1), ("zxy", 0, 1), ("core", 1, 0),
    ("score", 0), ("x", 2, 2), ("core", 2, 2), ("zy", 0, 2), ("zy", 0, 3),
    ("core", 3, 1), ("zxy", 0, 2), ("core", 2, 0), ("score", 1), ("x", 2, 3),
    ("core", 3, 2), ("zxy", 0, 3), ("core", 3, 0), ("score", 2), ("score", 3),
)
LATE = (
    ("pg", 0), ("pg", 1), ("pg", 2), ("pg", 3), ("z", 1, 1),
    ("z", 2, 1), ("z", 1, 2), ("x", 1, 0), ("z", 2, 2), ("z", 3, 1),
    ("z", 1, 3), ("x", 0, 0), ("z", 0, 1), ("x", 2, 0), ("code",),
    ("x", 2, 2), ("z", 2, 3), ("x", 1, 1), ("z", 3, 2), ("val",),
    ("x", 1, 2), ("rsx", 2), ("rsx", 0), ("x", 2, 1), ("zx", 0, 1),
    ("x", 1, 3), ("x", 2, 3), ("rsx", 1), ("proj", 2), ("x", 3, 2),
    ("z", 3, 3), ("z", 0, 2), ("proj", 1), ("rsx", 4), ("x", 3, 0),
    ("rsx", 3), ("zx", 0, 2), ("rsz", 2), ("rsz", 0), ("x", 3, 1),
    ("z", 0, 3), ("zx", 0, 3), ("proj", 0), ("rsz", 1), ("fin", 2),
    ("fin", 1), ("rsy", 2), ("x", 3, 3), ("rsz", 4), ("proj", 3),
    ("rsz", 3), ("col",), ("rsy", 0), ("rsy", 1), ("rsy", 4),
    ("rsy", 3), ("fin", 0), ("fin", 3),
)
CROSS_FIRST = (0,)


def fused(nb, nf, trunk, pre_act, proj_weight, codebook, value_weight, target, low, frac):
    nz, nx = PLANES, nf // (PLANES * CORES)
    pos, width = pre_act.shape
    rows, vrows = codebook.shape[0], value_weight.shape[0]
    bins = value_weight.shape[1]
    depth, total_pos = trunk.shape
    half, vhalf = rows // nb, vrows // nb
    cw = 256
    pieces = width // cw
    cuts = 4
    deep = nb * pos
    ck = half // cuts
    hops = [(0, 0)] + steps(nz)
    by_far = [[h for h in hops if h[1] == far] for far in range(nz)]

    early = []
    for a in range(3):
        for hop in hops:
            early += [("core", a, hop)]
            if hop[1]:
                early += [("z", a, hop)]
            if a == 0 and hop[1]:
                early += [("zy", a, hop, dy) for dy in range(1, nb)]
                for dx in range(1, nx):
                    early += [("zx", a, hop, dx)]
                    early += [("zxy", a, hop, dx, dy) for dy in range(1, nb)]
            else:
                early += [("x", a, hop, dx) for dx in range(1, nx)]
                if a == 0:
                    early += [("d", a, hop, dx, dy) for dx in range(1, nx) for dy in range(1, nb)]
    swap = [(k, dy) for dy in range(1, nb) for k in ("act", "tgt", "stat", "value")]
    swap += [("b", n, dy) for n in range(pieces) for dy in range(1, nb)]
    late = []
    for n in range(pieces):
        for hop in hops:
            late += [("gc", n, hop)]
            if hop[1]:
                late += [("gz", n, hop)]
            if hop[1] == 0 or n not in CROSS_FIRST:
                late += [("gx", n, hop, dx) for dx in range(1, nx)]
            else:
                late += [("gzx", n, hop, dx) for dx in range(1, nx)]
        late += [("p", n, dy) for dy in range(1, nb)]
    for a in range(cuts + 1):
        late += [("rc", a)] + [("rx", a, d) for d in range(1, nx)]
        late += [("rz", a, d) for d in range(1, nz)] + [("ry", a, d) for d in range(1, nb)]
    swap_at, base = number(swap, 0)
    early_send, sends = number(early, base, ("z", "zx"))
    early_recv, recvs = number(early, base)
    late_send, last = number(late, base, ("gz", "gzx"))
    sends = max(sends, last)
    late_recv, recvs = number(late, recvs)
    early_send.update(swap_at)
    early_recv.update(swap_at)
    late_send.update(swap_at)
    late_recv.update(swap_at)

    def kernel(
        pre_in,
        cb_in,
        vw_in,
        tgt_in,
        lo_in,
        fr_in,
        tr_in,
        pw_in,
        trg,
        pj,
        cd,
        vl,
        cb,
        vw,
        pre,
        tgt,
        lo,
        fr,
        tr,
        pw,
        cb_all,
        vw_all,
        gate,
        act_all,
        tgt_all,
        stat,
        back_out,
        back_in,
        logit,
        top,
        vlog,
        delta,
        vd_all,
        dt_all,
        pg,
        part,
        vpart,
        pj_all,
        cd_all,
        vl_all,
        *rest,
    ):
        local_sem, send_sem, recv_sem = rest[-3:]
        p = Place(nb, nf)
        inputs = (cb_in, vw_in, pre_in, tgt_in, lo_in, fr_in, tr_in, pw_in)
        loads = [
            pltpu.make_async_copy(src, dst, local_sem.at[i])
            for i, (src, dst) in enumerate(zip(inputs, (cb, vw, pre, tgt, lo, fr, tr, pw)))
        ]
        for load in loads:
            load.start()
        p.barrier()
        for load in loads[:3]:
            load.wait()
        s = Slots(send_sem, recv_sem, early_send, early_recv, p)
        g = Slots(send_sem, recv_sem, late_send, late_recv, p)

        def under(s, far, f):
            for hop in by_far[far]:
                if far:
                    s.only(lambda hop=hop: has(p, *hop))(lambda: f(hop))
                else:
                    f(hop)

        sub = half // 2
        shards = (
            (vw, vw_all, vhalf, 0, vhalf),
            (cb, cb_all, half, 0, sub),
            (cb, cb_all, half, sub, sub),
        )

        def like(a):
            own, out, piece, skip, size = shards[a]
            at = (0, 0, 0) if a else (0, 0, 0, 0)
            return lambda: out.at[at + (pl.ds(skip, size),)]

        def spot(a, z, x, h):
            own, out, piece, skip, size = shards[a]
            at = (z, x, p.c) if a else (z, x, p.c, h)
            return out.at[at + (pl.ds(skip, size),)]

        def relay(key, at_z, at_x, at_h, **to):
            ref = spot(key[1], at_z, at_x, at_h)
            s.go(key, ref, ref, p.dev(**to), like(key[1]))

        def publish(key, **to):
            own, out, piece, skip, size = shards[key[1]]
            src = own.at[pl.ds(pl.multiple_of(p.b * piece + skip, size), size)]
            s.go(key, src, spot(key[1], p.z, p.x, p.b), p.dev(**to), like(key[1]))

        def farther(kind, a, z, x, far, extra, ways):
            for way in ways:

                @s.only(lambda way=way: feeds(p, way))
                def _():
                    relay((kind, a, (way, far)) + extra, z, x, p.b, z=p.z + way)

        def send_x(a):
            for dx in range(1, nx):
                publish(("x", a, (0, 0), dx), x=p.xx(dx))

        def send_z(a):
            for way in (1, -1):

                @s.only(lambda way=way: feeds(p, way))
                def _():
                    publish(("z", a, (way, 1)), z=p.z + way)

        for name, a in EARLY[:6]:
            (send_x if name == "sx" else send_z)(a)
        cb_all[p.z, p.x, p.c] = cb[pl.ds(pl.multiple_of(p.b * half, half), half), :]
        vw_all[p.z, p.x, p.c] = vw[...].reshape(nb, vhalf, bins)

        def activate(i, carry):
            cols = pl.ds(pl.multiple_of(i * cw, cw), cw)
            v = pre[:, cols].astype(F32)
            sigma = jax.nn.sigmoid(v)
            active = v * sigma
            act_all[p.b, :, cols] = active.astype(BF16)
            gate[:, cols] = sigma * (1.0 + v * (1.0 - sigma))
            return carry

        lax.fori_loop(0, width // cw, activate, 0)
        for load in loads[3:6]:
            load.wait()
        tgt_all[p.b] = tgt[...]
        for dy in range(1, nb):
            for name, ref in (("act", act_all.at[p.b]), ("tgt", tgt_all.at[p.b])):
                g.go((name, dy), ref, ref, p.dev(b=p.bb(dy)))
        top[...] = jnp.full(top.shape, -jnp.inf, F32)
        vlog[...] = jnp.zeros(vlog.shape, F32)

        def from_x0(a):
            for dx in range(1, nx):
                s.arrived(("x", a, (0, 0), dx))
                if a == 0:
                    x = p.xx(-dx)
                    farther("zx", a, p.z, x, 1, (dx,), (1, -1))
                    for dy in range(1, nb):
                        relay(("d", a, (0, 0), dx, dy), p.z, x, p.b, b=p.bb(dy))

        def from_z(a, far):
            def run(hop):
                z = p.z - hop[0] * far
                s.arrived(("z", a, hop))
                if far + 1 < nz:
                    farther("z", a, z, p.x, far + 1, (), hop[:1])
                if a:
                    for dx in range(1, nx):
                        relay(("x", a, hop, dx), z, p.x, p.b, x=p.xx(dx))
                else:
                    for dy in range(1, nb):
                        relay(("zy", a, hop, dy), z, p.x, p.b, b=p.bb(dy))

            under(s, far, run)

        def from_zx(a, far):
            def run(hop):
                z = p.z - hop[0] * far
                for dx in range(1, nx):
                    s.arrived(("zx", a, hop, dx))
                    x = p.xx(-dx)
                    if far + 1 < nz:
                        farther("zx", a, z, x, far + 1, (dx,), hop[:1])
                    for dy in range(1, nb):
                        relay(("zxy", a, hop, dx, dy), z, x, p.b, b=p.bb(dy))

            under(s, far, run)

        def from_x(a, far):
            under(s, far, lambda hop: [s.arrived(("x", a, hop, dx)) for dx in range(1, nx)])

        def landed(kind):
            def wait(a, far):
                def run(hop):
                    for key in early:
                        if key[:3] == (kind, a, hop):
                            s.arrived(key)

                under(s, far, run)

            return wait

        def to_other(far, a):
            own, out, piece, skip, size = shards[a]
            part = pl.ds(skip, size)

            def run(hop):
                z = p.z - hop[0] * far
                ref = out.at[z, :, p.c, part] if a else out.at[z, :, p.c, :, part]
                held = lambda: out.at[0, :, 0, part] if a else out.at[0, :, 0, :, part]
                s.go(("core", a, hop), ref, ref, p.dev(c=1 - p.c), held)

            under(s, far, run)

        def near(j):
            up = (0, 1, 2, 3)[j], (1, 0, 2, 3)[j], (2, 3, 1, 0)[j], (3, 2, 1, 0)[j]
            z = jnp.where(p.z == 0, up[0], up[3])
            z = jnp.where(p.z == 1, up[1], z)
            return jnp.where(p.z == 2, up[2], z)

        def score(j):
            z = near(j)
            for a in range(3):
                landed("core")(a, j)

            plane = nx * CORES * half
            if j == 0:
                for dy in range(1, nb):
                    g.arrived(("act", dy))
            block = dot(
                cb_all[z].reshape(plane, width), act_all[...].reshape(deep, width), ((1,), (1,))
            )
            logit[pl.ds(pl.multiple_of(z * plane, plane), plane), :] = block
            top[...] = jnp.maximum(top[...], jnp.max(block, axis=0, keepdims=True))
            at = pl.ds(pl.multiple_of(z * 256, 256), 256)
            vlog[...] += dot(act_all[p.b, :, at], vw_all[z].reshape(256, bins), ((1,), (0,)))

        acts = dict(
            x0=from_x0, z=from_z, zx=from_zx, x=from_x, d=landed("d"), zy=landed("zy"),
            zxy=landed("zxy"), core=to_other, score=score,
        )
        for name, *where in EARLY[6:]:
            acts[name](*where)
        blocks = nf * half // 256
        best = top[...]

        def grow(i, total):
            at = pl.ds(pl.multiple_of(i * 256, 256), 256)
            e = jnp.exp(logit[at, :] - best)
            logit[at, :] = e
            return total + jnp.sum(e, axis=0, keepdims=True)

        mass = lax.fori_loop(0, blocks, grow, jnp.zeros((1, deep), F32))
        stat[p.b, 0] = jnp.broadcast_to(best, (8, deep))
        stat[p.b, 1] = jnp.broadcast_to(mass, (8, deep))
        for dy in range(1, nb):
            ref = stat.at[p.b]
            g.go(("stat", dy), ref, ref, p.dev(b=p.bb(dy)))
        s.finish()
        high = jnp.max(vlog[...], axis=1, keepdims=True)
        grown = jnp.exp(vlog[...] - high)
        probs = grown * (1.0 / jnp.sum(grown, axis=1, keepdims=True))
        ids = lax.broadcasted_iota(jnp.int32, (pos, bins), 1).astype(F32)
        column = jnp.broadcast_to(lo[...].astype(F32), (pos, pos)).T[:, :1]
        share = jnp.broadcast_to(fr[...].astype(F32) / 1024.0, (pos, pos)).T[:, :1]
        want = jnp.where(ids == column, 1.0 - share, 0.0)
        want = want + jnp.where(ids == column + 1.0, share, 0.0)
        vd_all[p.b] = (probs - want).astype(BF16)

        for dy in range(1, nb):
            g.arrived(("stat", dy))
            g.arrived(("tgt", dy))
        peak = stat[0, 0, :1]
        for b in range(1, nb):
            peak = jnp.maximum(peak, stat[b, 0, :1])
        mass = jnp.zeros((1, deep), F32)
        for b in range(nb):
            mass = mass + stat[b, 1, :1] * jnp.exp(stat[b, 0, :1] - peak)
        scale = jnp.exp(best - peak) * (1.0 / mass)
        aim = jnp.concatenate([tgt_all[b] for b in range(nb)], axis=1)
        group = 256 // half
        row = lax.broadcasted_iota(jnp.int32, (256, deep), 0)
        code_ids = lax.div(row, half) * rows + lax.rem(row, half) + p.b * half

        def differ(i, carry):
            at = pl.ds(pl.multiple_of(i * 256, 256), 256)
            hot = jnp.where(code_ids + i * (group * rows) == aim, 1.0, 0.0)
            d = logit[at, :] * scale - hot
            delta[:, at] = d.T.astype(BF16)
            dt_all[pl.ds(i * group, group)] = d.astype(BF16).reshape(group, half, deep)
            return carry

        lax.fori_loop(0, blocks, differ, 0)

        def back_from(b, n):
            cols = pl.ds(n * cw, cw)
            left = delta[pl.ds(pl.multiple_of(b * pos, pos), pos), :]
            return dot(left, cb_all[:, :, :, :, cols].reshape(nf * half, cw), ((1,), (0,)))

        for n in range(pieces):
            for dy in range(1, nb):
                back_out[dy - 1, n] = back_from(p.bb(dy), n).astype(BF16)
                g.go(
                    ("b", n, dy), back_out.at[dy - 1, n], back_in.at[dy - 1, n], p.dev(b=p.bb(dy))
                )
        for dy in range(1, nb):
            ref = vd_all.at[p.b]
            g.go(("value", dy), ref, ref, p.dev(b=p.bb(dy)))

        def pass_on(n, at_z, at_x, key, **to):
            ref = pg.at[n, at_z, at_x, p.c]
            g.go(key, ref, ref, p.dev(**to), lambda: pg.at[n, 0, 0, 0])

        def onward(n, kind, z, x, far, extra, ways):
            for way in ways:

                @g.only(lambda way=way: feeds(p, way))
                def _():
                    pass_on(n, z, x, (kind, n, (way, far)) + extra, z=p.z + way)

        def across(n, hop):
            for dx in range(1, nx):
                pass_on(n, p.z - hop[0] * hop[1], p.x, ("gx", n, hop, dx), x=p.xx(dx))

        def to_core(n, hop):
            ref = pg.at[n, p.z - hop[0] * hop[1], :, p.c]
            g.make(("gc", n, hop), ref, ref, p.dev(c=1 - p.c)).start()

        def head(n):
            cols = pl.ds(n * cw, cw)
            back = back_from(p.b, n)
            back = back + dot(vd_all[p.b], vw_all[n].reshape(cw, bins), ((1,), (1,)))
            for dy in range(1, nb):
                g.arrived(("b", n, dy))
                back = back + back_in[dy - 1, n].astype(F32)
            pg[n, p.z, p.x, p.c] = (back * gate[:, cols]).astype(BF16)
            if n in CROSS_FIRST:
                across(n, (0, 0))
            onward(n, "gz", p.z, p.x, 1, (), (1, -1))
            if n not in CROSS_FIRST:
                across(n, (0, 0))

        def grad_z(n, far):
            def run(hop):
                z = p.z - hop[0] * far
                g.arrived(("gz", n, hop))
                if far + 1 < nz:
                    onward(n, "gz", z, p.x, far + 1, (), hop[:1])
                if n not in CROSS_FIRST:
                    across(n, hop)

            under(g, far, run)

        def grad_x(n, far):
            def run(hop):
                for dx in range(1, nx):
                    g.arrived(("gx", n, hop, dx))
                    if n in CROSS_FIRST:
                        onward(n, "gzx", p.z, p.xx(-dx), 1, (dx,), (1, -1))
                to_core(n, hop)

            under(g, far, run)

        def grad_zx(n, far):
            def run(hop):
                for dx in range(1, nx):
                    g.arrived(("gzx", n, hop, dx))
                    if far + 1 < nz:
                        onward(n, "gzx", p.z - hop[0] * far, p.xx(-dx), far + 1, (dx,), hop[:1])
                to_core(n, hop)

            under(g, far, run)

        arrays = []
        for a in range(cuts + 1):
            if a < cuts:
                own, out = part.at[:, :, :, pl.ds(a * ck, ck)], cd_all.at[:, pl.ds(a * ck, ck)]
            else:
                own, out = vpart.at[:, :, :, p.b], vl_all
            arrays.append((own, out) + tuple(rest[6 * a : 6 * a + 6]))

        def to_sum(a):
            own, out, core, *_ = arrays[a]
            g.go(("rc", a), own.at[:, :, 1 - p.c], core, p.dev(c=1 - p.c))

        def code():
            def block(i, carry):
                z = i // (width // cw)
                cols = pl.ds(pl.multiple_of((i % (width // cw)) * cw, cw), cw)
                left = dt_all[pl.ds(z * nx * CORES, nx * CORES)].reshape(nx * CORES * half, deep)
                right = act_all[:, :, cols].reshape(deep, cw)
                product = dot(left, right, ((1,), (0,)))
                part[z, :, :, :, cols] = product.astype(BF16).reshape(nx, CORES, half, cw)
                return carry

            lax.fori_loop(0, nz * (width // cw), block, 0)
            for a in range(cuts):
                to_sum(a)

        def val():
            for dy in range(1, nb):
                g.arrived(("value", dy))

            def block(z, carry):
                cols = pl.ds(pl.multiple_of(z * 256, 256), 256)
                left = act_all[:, :, cols].reshape(deep, 256)
                product = dot(left, vd_all[...].reshape(deep, bins), ((0,), (0,)))
                vpart[z] = product.astype(BF16).reshape(nx, CORES, nb, vhalf, bins)
                return carry

            lax.fori_loop(0, nz, block, 0)
            to_sum(cuts)

        def rsx(a):
            own, out, core, xin, xsend, acc, zin, zsend = arrays[a]
            g.arrived(("rc", a))
            for dx in range(1, nx):
                x = p.xx(dx)
                for z in range(nz):
                    both = own[z, x, p.c].astype(F32) + core[z, x].astype(F32)
                    xsend[dx - 1, z] = both.astype(BF16)
                g.go(("rx", a, dx), xsend.at[dx - 1], xin.at[dx - 1], p.dev(x=x))
            for z in range(nz):
                acc[z] = own[z, p.x, p.c].astype(F32) + core[z, p.x].astype(F32)

        def rsz(a):
            own, out, core, xin, xsend, acc, zin, zsend = arrays[a]
            for dx in range(1, nx):
                g.arrived(("rx", a, dx))
                acc[...] += xin[dx - 1].astype(F32)
            for dz in [2, 1, 3]:
                z = p.zz(dz)
                zsend[dz - 1] = acc[z].astype(BF16)
                g.make(("rz", a, dz), zsend.at[dz - 1], zin.at[dz - 1], p.dev(z=z)).start()
            g.join(("rz", a, 1), zin)

        def rsy(a):
            own, out, core, xin, xsend, acc, zin, zsend = arrays[a]
            total = acc[p.z]
            g.arrived(("rz", a, 1))
            for dz in range(1, nz):
                total = total + zin[dz - 1].astype(F32)
            out[p.b] = total.astype(BF16)
            for dy in range(1, nb):
                g.go(("ry", a, dy), out.at[p.b], out.at[p.b], p.dev(b=p.bb(dy)))

        def proj(n):
            g.join(("gc", n, (0, 0)), lambda: pg.at[n, :, :, 0])
            g.arrived(("gc", n, (0, 0)))

            def block(i, carry):
                at = pl.ds(pl.multiple_of(i * 192, 192), 192)
                pj_all[p.b, n, at, :] = jnp.dot(
                    tr[at, :], pg[n].reshape(total_pos, cw), preferred_element_type=F32
                ).astype(BF16)
                return carry

            lax.fori_loop(0, depth // 192, block, 0)
            for dy in range(1, nb):
                ref = pj_all.at[p.b, n]
                g.go(("p", n, dy), ref, ref, p.dev(b=p.bb(dy)))

        def col():
            def block(i, carry):
                at = pl.ds(pl.multiple_of(i * 256, 256), 256)
                z, x = i // nx, i % nx
                total = 0.0
                for n in range(pieces):
                    there = pg[n, z, x].reshape(256, cw)
                    total = total + dot(pw[:, pl.ds(n * cw, cw)], there, ((1,), (1,)))
                trg[:, at] = total.astype(BF16)
                return carry

            lax.fori_loop(0, nz * nx, block, 0)

        def fin(n):
            for dy in range(1, nb):
                g.arrived(("p", n, dy))
            total = pj_all[0, n].astype(F32)
            for b in range(1, nb):
                total = total + pj_all[b, n].astype(F32)
            pj[:, pl.ds(n * cw, cw)] = total

        for load in loads[6:]:
            load.wait()
        acts = dict(
            pg=head, z=grad_z, x=grad_x, zx=grad_zx, code=code, val=val, rsx=rsx, rsz=rsz, rsy=rsy,
            proj=proj, col=col, fin=fin,
        )
        for name, *where in LATE:
            acts[name](*where)
        for a in range(cuts + 1):
            for dy in range(1, nb):
                g.arrived(("ry", a, dy))
        for b in range(nb):
            cd[pl.ds(b * half, half), :] = cd_all[b].astype(F32)
            vl[pl.ds(b * vhalf, vhalf), :] = vl_all[b].astype(F32)
        g.finish()

    def buffers(r, k):
        return [
            pltpu.VMEM((nz, nx, r, k), BF16),
            pltpu.VMEM((max(nx - 1, 1), nz, r, k), BF16),
            pltpu.VMEM((max(nx - 1, 1), nz, r, k), BF16),
            pltpu.VMEM((nz, r, k), F32),
            pltpu.VMEM((nz - 1, r, k), BF16),
            pltpu.VMEM((nz - 1, r, k), BF16),
        ]

    anywhere = pl.BlockSpec(memory_space=pl.ANY)
    stay = pl.BlockSpec(memory_space=pltpu.HBM)
    results = pl.pallas_call(
        kernel,
        out_shape=[
            jax.ShapeDtypeStruct((depth, total_pos), BF16),
            jax.ShapeDtypeStruct((depth, width), F32),
            jax.ShapeDtypeStruct((rows, width), F32),
            jax.ShapeDtypeStruct((vrows, bins), F32),
        ],
        in_specs=[stay] * 8,
        out_specs=[pl.BlockSpec(memory_space=pltpu.VMEM)] * 4,
        scratch_shapes=[
            pltpu.VMEM((rows, width), BF16),
            pltpu.VMEM((vrows, bins), BF16),
            pltpu.VMEM((pos, width), BF16),
            pltpu.VMEM((1, pos), jnp.int32),
            pltpu.VMEM((1, pos), jnp.int32),
            pltpu.VMEM((1, pos), jnp.int32),
            pltpu.VMEM((depth, total_pos), BF16),
            pltpu.VMEM((depth, width), BF16),
            pltpu.VMEM((nz, nx, CORES, half, width), BF16),
            pltpu.VMEM((nz, nx, CORES, nb, vhalf, bins), BF16),
            pltpu.VMEM((pos, width), F32),
            pltpu.VMEM((nb, pos, width), BF16),
            pltpu.VMEM((nb, 1, pos), jnp.int32),
            pltpu.VMEM((nb, 2, 8, deep), F32),
            pltpu.VMEM((nb - 1, pieces, pos, cw), BF16),
            pltpu.VMEM((nb - 1, pieces, pos, cw), BF16),
            pltpu.VMEM((nf * half, deep), F32),
            pltpu.VMEM((1, deep), F32),
            pltpu.VMEM((pos, bins), F32),
            pltpu.VMEM((deep, nf * half), BF16),
            pltpu.VMEM((nb, pos, bins), BF16),
            pltpu.VMEM((nf, half, nb * pos), BF16),
            pltpu.VMEM((pieces, nz, nx, CORES, pos, cw), BF16),
            pltpu.VMEM((nz, nx, CORES, half, width), BF16),
            pltpu.VMEM((nz, nx, CORES, nb, vhalf, bins), BF16),
            pltpu.VMEM((nb, pieces, depth, cw), BF16),
            pltpu.VMEM((nb, half, width), BF16),
            pltpu.VMEM((nb, vhalf, bins), BF16),
        ]
        + buffers(ck, width) * cuts
        + buffers(vhalf, bins)
        + [
            pltpu.SemaphoreType.DMA((8,)),
            pltpu.SemaphoreType.DMA((sends,)),
            pltpu.SemaphoreType.DMA((recvs,)),
        ],
        compiler_params=pltpu.CompilerParams(
            collective_id=4, has_side_effects=True, vmem_limit_bytes=44 << 20
        ),
    )(
        *(
            pltpu.with_memory_space_constraint(x, pltpu.HBM)
            for x in (
                pre_act, codebook, value_weight, target, low, frac, trunk, proj_weight,
            )
        )
    )

    def hand_over(*refs):
        copies = [
            pltpu.make_async_copy(refs[i], refs[4 + i], refs[8].at[i]) for i in range(4)
        ]
        for copy in copies:
            copy.start()
        for copy in copies:
            copy.wait()

    return pl.pallas_call(
        hand_over,
        out_shape=[jax.ShapeDtypeStruct(r.shape, r.dtype) for r in results],
        in_specs=[anywhere] * 4,
        out_specs=[stay] * 4,
        scratch_shapes=[pltpu.SemaphoreType.DMA((4,))],
        compiler_params=pltpu.CompilerParams(vmem_limit_bytes=1 << 20),
    )(*results)


def make_body(nb, nf):
    nz, nx = PLANES, nf // (PLANES * CORES)

    def body(
        trunk, pre_act, proj_weight, codebook, value_weight, code_target, value_bin, value_frac
    ):
        if fits(nb, nf, codebook, value_weight, trunk.shape[0], pre_act.shape[0]):
            row = (1, pre_act.shape[0])
            return fused(
                nb,
                nf,
                trunk,
                pre_act,
                proj_weight,
                codebook,
                value_weight,
                code_target.reshape(row),
                value_bin.reshape(row),
                value_frac.reshape(row),
            )
        all_codes, bins_weight = gather_weights(nb, nf, codebook, value_weight)
        rows, width = pre_act.shape
        num_codes = all_codes.shape[0]
        num_bins = bins_weight.shape[1]
        pre_value = pre_act.astype(F32)
        gate_sigma = jax.nn.sigmoid(pre_value)
        active = (pre_value * gate_sigma).astype(BF16)
        code_logits = jnp.einsum("rk,ck->rc", active, all_codes, preferred_element_type=F32)
        code_probs = jax.nn.softmax(code_logits, axis=-1)
        code_ids = lax.broadcasted_iota(jnp.int32, (1, num_codes), 1)
        one_hot = (code_target[:, None] == code_ids).astype(F32)
        code_delta = (code_probs - one_hot).astype(BF16)
        value_logits = jnp.dot(active, bins_weight, preferred_element_type=F32)
        value_probs = jax.nn.softmax(value_logits, axis=-1)
        bin_ids = lax.broadcasted_iota(jnp.int32, (1, num_bins), 1)
        fraction = value_frac.astype(F32)[:, None] / 1024.0
        target = jnp.where(bin_ids == value_bin[:, None], 1.0 - fraction, 0.0)
        target = target + jnp.where(bin_ids == value_bin[:, None] + 1, fraction, 0.0)
        value_delta = (value_probs - target).astype(BF16)
        backward = jnp.dot(code_delta, all_codes, preferred_element_type=F32)
        backward = backward + jnp.einsum(
            "rb,kb->rk", value_delta, bins_weight, preferred_element_type=F32
        )
        pre_grad = (backward * gate_sigma * (1.0 + pre_value * (1.0 - gate_sigma))).astype(BF16)
        own = codebook.shape[0] // nb
        delta_t = code_delta.T.reshape(nf, nb, own, rows).swapaxes(0, 1)
        delta_t = delta_t.reshape(nb, nf * own, rows)
        pieces, act_all, dt_all, vd_all = gather_grads(
            nb, nf, pre_grad, active, delta_t, value_delta
        )
        code_part = jnp.dot(dt_all, act_all, preferred_element_type=F32)
        code_part = code_part.astype(BF16).reshape(nz, nx, CORES, own, width)
        vown = value_weight.shape[0] // nb
        if vown % 16 == 0:
            value_part = (act_all, vd_all)
        else:
            value_part = jnp.einsum("rk,rb->kb", act_all, vd_all, preferred_element_type=F32)
            value_part = value_part.astype(BF16)
            value_part = (value_part.reshape(nz, nx, CORES, nb, vown, num_bins),)
        out_cols, proj_all, code_all, value_all = reduce_grads(
            nb, nf, trunk, proj_weight, pieces, code_part, value_part
        )
        proj_grad = jnp.sum(proj_all.astype(F32), axis=0)
        code_grad = code_all.reshape(nb * own, width).astype(F32)
        value_grad = value_all.reshape(nb * vown, num_bins).astype(F32)
        return (out_cols, proj_grad, code_grad, value_grad)

    return body


def solution(mesh):
    in_specs = (
        P("fsdp", "batch"),
        P(("batch", "fsdp"), None),
        P("fsdp", None),
        P("fsdp", None),
        P("fsdp", None),
        P(("batch", "fsdp")),
        P(("batch", "fsdp")),
        P(("batch", "fsdp")),
    )
    out_specs = (P("fsdp", "batch"), P("fsdp", None), P("fsdp", None), P("fsdp", None))
    body = make_body(mesh.shape["batch"], mesh.shape["fsdp"])
    return jax.shard_map(body, mesh=mesh, in_specs=in_specs, out_specs=out_specs, check_vma=False)
```

```python
import jax
import jax.numpy as jnp
from jax import lax
from jax.experimental import pallas as pl
from jax.experimental.pallas import tpu as pltpu
from jax.sharding import PartitionSpec as P

MESH = pl.DeviceIdType.MESH
BF16 = jnp.bfloat16
F32 = jnp.float32
CORES = 2
PLANES = 4


class Place:
    def __init__(self, nb, nf):
        self.nb, self.nz = nb, PLANES
        self.nx = nf // (PLANES * CORES)
        f = lax.axis_index("fsdp")
        self.b = lax.axis_index("batch")
        self.z = f // (self.nx * CORES)
        self.x = (f // CORES) % self.nx
        self.c = f % CORES

    def dev(self, b=None, z=None, x=None, c=None):
        b = self.b if b is None else b
        z = self.z if z is None else z
        x = self.x if x is None else x
        c = self.c if c is None else c
        return (b, (z * self.nx + x) * CORES + c)

    def zz(self, d):
        return lax.rem(self.z + d + self.nz, self.nz)

    def xx(self, d):
        return lax.rem(self.x + d + self.nx, self.nx)

    def bb(self, d):
        return lax.rem(self.b + d + self.nb, self.nb)

    def barrier(self):
        sem = pltpu.get_barrier_semaphore()
        peers = [self.dev(z=self.zz(d)) for d in range(1, self.nz)]
        peers += [self.dev(x=self.xx(d)) for d in range(1, self.nx)]
        peers += [self.dev(b=self.bb(d)) for d in range(1, self.nb)]
        peers += [self.dev(c=1 - self.c)]
        for peer in peers:
            pl.semaphore_signal(sem, inc=1, device_id=peer, device_id_type=MESH)
        pl.semaphore_wait(sem, len(peers))


def steps(nz):
    return [(way, far) for far in range(1, nz) for way in (1, -1)]


class Sends:
    def __init__(self, send_sem, recv_sem, keys, place):
        self.send_sem, self.recv_sem, self.place = send_sem, recv_sem, place
        self.at = {k: i for i, k in enumerate(keys)}
        self.like = {}
        self.started = []
        self.when = ()

    def make(self, key, src, dst, dev):
        i = self.at[key]
        return pltpu.make_async_remote_copy(
            src_ref=src,
            dst_ref=dst,
            send_sem=self.send_sem.at[i],
            recv_sem=self.recv_sem.at[i],
            device_id=dev,
            device_id_type=MESH,
        )

    def go(self, key, src, dst, dev, like=None):
        self.make(key, src, dst, dev).start()
        self.like[key] = dst if like is None else like
        self.started.append((key, self.when))

    def waiter(self, key):
        ref = self.like[key]
        ref = ref() if callable(ref) else ref
        return self.make(key, ref, ref, self.place.dev(c=1 - self.place.c))

    def arrived(self, key):
        self.waiter(key).wait_recv()

    def finish(self):
        for key, whens in self.started:

            def wait(key=key):
                self.waiter(key).wait_send()

            if whens:
                met = whens[0]()
                for when in whens[1:]:
                    met = jnp.logical_and(met, when())
                pl.when(met)(wait)
            else:
                wait()

    def only(self, when):
        def run(f):
            outer = self.when
            self.when = outer + (when,)

            @pl.when(when())
            def _():
                f()

            self.when = outer

        return run


def call(kernel, outs, scratch, cid, *args):
    return pl.pallas_call(
        kernel,
        out_shape=outs,
        in_specs=[pl.BlockSpec(memory_space=pltpu.VMEM)] * len(args),
        out_specs=[pl.BlockSpec(memory_space=pltpu.VMEM)] * len(outs),
        scratch_shapes=scratch,
        compiler_params=pltpu.CompilerParams(collective_id=cid, has_side_effects=True),
    )(*args)


def has(p, way, far):
    return p.z >= far if way == 1 else p.z + far < p.nz


def feeds(p, way):
    return p.z + 1 < p.nz if way == 1 else p.z >= 1


def gather_weights_keys(nb, nx, nz):
    keys = []
    for a in (0, 1):
        keys += [(a, "c", 0)]
        for hop in [(0, 0)] + steps(nz):
            if hop[1]:
                keys += [(a, "z", hop), (a, "cz", hop)]
                for dy in range(1, nb):
                    keys += [(a, "y", hop, dy), (a, "cy", hop, dy)]
            for dx in range(1, nx):
                keys += [(a, "x", hop, dx), (a, "cx", hop, dx)]
                for dy in range(1, nb):
                    keys += [(a, "d", hop, dx, dy), (a, "cd", hop, dx, dy)]
    return keys


def gather_weights(nb, nf, codebook, value_weight):
    nz, nx = PLANES, nf // (PLANES * CORES)
    keys = gather_weights_keys(nb, nx, nz)
    rows, width = codebook.shape
    vrows, bins = value_weight.shape

    def kernel(cb, vw, cb_out, vw_out, send_sem, recv_sem):
        p = Place(nb, nf)
        p.barrier()
        s = Sends(send_sem, recv_sem, keys, p)
        arrays = ((0, cb, cb_out), (1, vw, vw_out))

        def spot(out, z, x, h):
            return out.at[z, x, p.c, h]

        def relay(key, out, at_z, at_x, at_h, **to):
            ref = spot(out, at_z, at_x, at_h)
            s.go(key, ref, ref, p.dev(**to), lambda: out.at[0, 0, 0, 0])

        for a, own, out in arrays:
            here = spot(out, p.z, p.x, p.b)
            for way in (1, -1):

                @s.only(lambda way=way: feeds(p, way))
                def _(a=a, own=own, out=out, here=here, way=way):
                    s.go((a, "z", (way, 1)), own.at[p.b], here, p.dev(z=p.z + way), lambda: out.at[0, 0, 0, 0])

            for dx in range(1, nx):
                s.go((a, "x", (0, 0), dx), own.at[p.b], here, p.dev(x=p.xx(dx)))
            s.go((a, "c", 0), own, out.at[p.z, p.x, p.c], p.dev(c=1 - p.c))
        for a, own, out in arrays:
            out[p.z, p.x, p.c] = own[...]

        def from_z(hop):
            way, far = hop
            z = p.z - way * far
            for a, own, out in arrays:
                s.arrived((a, "z", hop))
                if far + 1 < nz:

                    @s.only(lambda way=way: feeds(p, way))
                    def _(a=a, out=out):
                        relay((a, "z", (way, far + 1)), out, z, p.x, p.b, z=p.z + way)

                for dx in range(1, nx):
                    relay((a, "x", hop, dx), out, z, p.x, p.b, x=p.xx(dx))
                for dy in range(1, nb):
                    relay((a, "y", hop, dy), out, z, p.x, p.b, b=p.bb(dy))
                relay((a, "cz", hop), out, z, p.x, p.b, c=1 - p.c)

        def from_plane(hop):
            way, far = hop
            z = p.z - way * far
            for a, own, out in arrays:
                for dx in range(1, nx):
                    x = p.xx(-dx)
                    s.arrived((a, "x", hop, dx))
                    if far % 2 == 0:
                        for dy in range(1, nb):
                            relay((a, "d", hop, dx, dy), out, z, x, p.b, b=p.bb(dy))
                    relay((a, "cx", hop, dx), out, z, x, p.b, c=1 - p.c)
                if far:
                    for dy in range(1, nb):
                        h = p.bb(-dy)
                        s.arrived((a, "y", hop, dy))
                        if far % 2:
                            for dx in range(1, nx):
                                relay((a, "d", hop, dx, dy), out, z, p.x, h, x=p.xx(dx))
                        relay((a, "cy", hop, dy), out, z, p.x, h, c=1 - p.c)

        def from_diagonal(hop):
            way, far = hop
            for a, own, out in arrays:
                for dx in range(1, nx):
                    for dy in range(1, nb):
                        s.arrived((a, "d", hop, dx, dy))
                        relay(
                            (a, "cd", hop, dx, dy),
                            out,
                            p.z - way * far,
                            p.xx(-dx),
                            p.bb(-dy),
                            c=1 - p.c,
                        )

        def from_core(hop):
            for key in keys:
                if key[1] in ("cz", "cx", "cy", "cd") and key[2] == hop:
                    s.arrived(key)

        def under(hop, f):
            if hop[1]:
                s.only(lambda: has(p, *hop))(lambda: f(hop))
            else:
                f(hop)

        hops = [(0, 0)] + steps(nz)
        by_far = [[h for h in hops if h[1] == far] for far in range(nz)]
        for far in range(nz + 2):
            if 1 <= far < nz:
                for hop in by_far[far]:
                    under(hop, from_z)
            if 1 <= far <= nz:
                for hop in by_far[far - 1]:
                    under(hop, from_plane)
            if far >= 2:
                for hop in by_far[far - 2]:
                    under(hop, from_diagonal)
        for a in (0, 1):
            s.arrived((a, "c", 0))
        for hop in hops:
            under(hop, from_core)
        s.finish()

    cb_out, vw_out = call(
        kernel,
        [
            jax.ShapeDtypeStruct((nz, nx, CORES, nb, rows // nb, width), BF16),
            jax.ShapeDtypeStruct((nz, nx, CORES, nb, vrows // nb, bins), BF16),
        ],
        [pltpu.SemaphoreType.DMA((len(keys),)), pltpu.SemaphoreType.DMA((len(keys),))],
        1,
        codebook.reshape(nb, rows // nb, width),
        value_weight.reshape(nb, vrows // nb, bins),
    )
    return cb_out.reshape(nf * rows, width), vw_out.reshape(nf * vrows, bins)


def gather_grads(nb, nf, pre_grad, active, delta_t, value_delta):
    nz, nx = PLANES, nf // (PLANES * CORES)
    rows, width = pre_grad.shape
    bins = value_delta.shape[1]
    half = delta_t.shape[1]
    hops = [(0, 0)] + steps(nz)
    keys = [("c", 0)]
    for hop in hops:
        if hop[1]:
            keys += [("z", hop), ("cz", hop)]
        for dx in range(1, nx):
            keys += [("x", hop, dx), ("cx", hop, dx)]
    keys += [(k, dy) for dy in range(1, nb) for k in ("act", "delta", "value")]

    def kernel(pg, act, dt, vd, pg_out, act_out, dt_out, vd_out, send_sem, recv_sem):
        p = Place(nb, nf)
        p.barrier()
        s = Sends(send_sem, recv_sem, keys, p)
        here, like = pg_out.at[p.z, p.x, p.c], pg_out.at[0, 0, 0]
        mine = pl.ds(pl.multiple_of(p.b * rows, rows), rows)
        for way in (1, -1):

            @s.only(lambda way=way: feeds(p, way))
            def _(way=way):
                s.go(("z", (way, 1)), pg, here, p.dev(z=p.z + way), like)

        for dx in range(1, nx):
            s.go(("x", (0, 0), dx), pg, here, p.dev(x=p.xx(dx)))
        for dy in range(1, nb):
            to = p.bb(dy)
            s.go(("act", dy), act, act_out.at[p.b], p.dev(b=to))
            s.go(("delta", dy), dt.at[to], dt_out.at[:, mine], p.dev(b=to))
            s.go(("value", dy), vd, vd_out.at[p.b], p.dev(b=to))
        s.go(("c", 0), pg, here, p.dev(c=1 - p.c))
        pg_out[p.z, p.x, p.c] = pg[...]
        act_out[p.b] = act[...]
        dt_out[:, mine] = dt[p.b]
        vd_out[p.b] = vd[...]

        def from_z(hop):
            way, far = hop
            ref = pg_out.at[p.z - way * far, p.x, p.c]
            s.arrived(("z", hop))
            if far + 1 < nz:

                @s.only(lambda way=way: feeds(p, way))
                def _():
                    s.go(("z", (way, far + 1)), ref, ref, p.dev(z=p.z + way), like)

            for dx in range(1, nx):
                s.go(("x", hop, dx), ref, ref, p.dev(x=p.xx(dx)), like)
            s.go(("cz", hop), ref, ref, p.dev(c=1 - p.c), like)

        def from_plane(hop):
            way, far = hop
            for dx in range(1, nx):
                s.arrived(("x", hop, dx))
                ref = pg_out.at[p.z - way * far, p.xx(-dx), p.c]
                s.go(("cx", hop, dx), ref, ref, p.dev(c=1 - p.c), like)

        def from_core(hop):
            for key in keys:
                if key[0] in ("cz", "cx") and key[1] == hop:
                    s.arrived(key)

        def under(hop, f):
            if hop[1]:
                s.only(lambda: has(p, *hop))(lambda: f(hop))
            else:
                f(hop)

        for far in range(nz + 1):
            for hop in hops:
                if far and hop[1] == far:
                    under(hop, from_z)
            for hop in hops:
                if hop[1] == far - 1:
                    under(hop, from_plane)
        for key in keys:
            if key[0] in ("act", "delta", "value", "c"):
                s.arrived(key)
        for hop in hops:
            under(hop, from_core)
        s.finish()

    pieces, act_all, dt_all, vd_all = call(
        kernel,
        [
            jax.ShapeDtypeStruct((nz, nx, CORES, rows, width), BF16),
            jax.ShapeDtypeStruct((nb, rows, width), BF16),
            jax.ShapeDtypeStruct((half, nb * rows), BF16),
            jax.ShapeDtypeStruct((nb, rows, bins), BF16),
        ],
        [pltpu.SemaphoreType.DMA((len(keys),)), pltpu.SemaphoreType.DMA((len(keys),))],
        2,
        pre_grad,
        active,
        delta_t,
        value_delta,
    )
    return (
        pieces.reshape(nf * rows, width),
        act_all.reshape(nb * rows, width),
        dt_all,
        vd_all.reshape(nb * rows, bins),
    )


def reduce_grads(nb, nf, trunk, proj_weight, pieces, code, value):
    nz, nx = PLANES, nf // (PLANES * CORES)
    depth = trunk.shape[0]
    width = pieces.shape[1]
    block = next(n for n in (192, 96, 64, 32, 16) if depth % n == 0)
    blocks = depth // block
    lanes = 256
    cuts = 2 if code.shape[3] % 32 == 0 else 1
    crows = code.shape[3] // cuts
    fused = len(value) == 2
    bins = value[-1].shape[-1]
    vrows = width // (nf * nb) if fused else value[0].shape[4]
    chunks = range(cuts + 1)
    keys = [("p", i, dy) for i in range(blocks) for dy in range(1, nb)]
    for a in chunks:
        keys += [(a, "c")] + [(a, "x", d) for d in range(1, nx)]
        keys += [(a, "z", d) for d in range(1, nz)] + [(a, "y", d) for d in range(1, nb)]

    def kernel(tr, pw, pg, cd, *rest):
        factors, rest = rest[: len(value)], rest[len(value) :]
        (tr_out, pj_out, cd_out, vl_out), rest = rest[:4], rest[4:]
        send_sem, recv_sem = rest[-2:]
        vl = rest[-3] if fused else factors[0]
        p = Place(nb, nf)
        p.barrier()
        s = Sends(send_sem, recv_sem, keys, p)
        arrays = []
        for a in chunks:
            if a < cuts:
                part = pl.ds(a * crows, crows)
                own, out = cd.at[:, :, :, part], cd_out.at[:, part]
            else:
                own, out = vl.at[:, :, :, p.b], vl_out
            arrays.append((a, own, out) + tuple(rest[6 * a : 6 * a + 6]))
        for a, own, out, core, *_ in arrays:
            if a == cuts and fused:
                product = lax.dot_general(
                    factors[0][...],
                    factors[1][...],
                    (((0,), (0,)), ((), ())),
                    preferred_element_type=F32,
                )
                vl[...] = product.astype(BF16).reshape(nz, nx, CORES, nb, vrows, bins)
            s.go((a, "c"), own.at[:, :, 1 - p.c], core, p.dev(c=1 - p.c))

        def multiply(i):
            rows = pl.ds(i * block, block)

            def tile(n, carry):
                cols = pl.ds(pl.multiple_of(n * lanes, lanes), lanes)
                pj_out[p.b, rows, cols] = jnp.dot(
                    tr[rows, :], pg[:, cols], preferred_element_type=F32
                ).astype(BF16)
                return carry

            lax.fori_loop(0, width // lanes, tile, 0)
            for dy in range(1, nb):
                ref = pj_out.at[p.b, rows]
                s.go(("p", i, dy), ref, ref, p.dev(b=p.bb(dy)))

        def columns(n, carry):
            cols = pl.ds(pl.multiple_of(n * lanes, lanes), lanes)
            tr_out[:, cols] = lax.dot_general(
                pw[...], pg[cols, :], (((1,), (1,)), ((), ())), preferred_element_type=F32
            ).astype(BF16)
            return carry

        multiply(0)
        for a, own, out, core, xin, xsend, acc, zin, zsend in arrays:
            s.arrived((a, "c"))
            for dx in range(1, nx):
                x = p.xx(dx)
                for z in range(nz):
                    both = own[z, x, p.c].astype(F32) + core[z, x].astype(F32)
                    xsend[dx - 1, z] = both.astype(BF16)
                s.go((a, "x", dx), xsend.at[dx - 1], xin.at[dx - 1], p.dev(x=x))
            for z in range(nz):
                acc[z] = own[z, p.x, p.c].astype(F32) + core[z, p.x].astype(F32)
        for i in range(1, blocks):
            multiply(i)
        for a, own, out, core, xin, xsend, acc, zin, zsend in arrays:
            for dx in range(1, nx):
                s.arrived((a, "x", dx))
                acc[...] += xin[dx - 1].astype(F32)
            for dz in [2, 1, 3]:
                z = p.zz(dz)
                zsend[dz - 1] = acc[z].astype(BF16)
                s.go((a, "z", dz), zsend.at[dz - 1], zin.at[dz - 1], p.dev(z=z))
        for a, own, out, core, xin, xsend, acc, zin, zsend in arrays:
            if a == 0:
                lax.fori_loop(0, pieces.shape[0] // lanes, columns, 0)
            total = acc[p.z]
            for dz in range(1, nz):
                s.arrived((a, "z", dz))
                total = total + zin[dz - 1].astype(F32)
            out[p.b] = total.astype(BF16)
            for dy in range(1, nb):
                s.go((a, "y", dy), out.at[p.b], out.at[p.b], p.dev(b=p.bb(dy)))
        for key in keys:
            if key[0] == "p" or key[1] == "y":
                s.arrived(key)
        s.finish()

    def buffers(r, k):
        return [
            pltpu.VMEM((nz, nx, r, k), BF16),
            pltpu.VMEM((max(nx - 1, 1), nz, r, k), BF16),
            pltpu.VMEM((max(nx - 1, 1), nz, r, k), BF16),
            pltpu.VMEM((nz, r, k), F32),
            pltpu.VMEM((nz - 1, r, k), BF16),
            pltpu.VMEM((nz - 1, r, k), BF16),
        ]

    return call(
        kernel,
        [
            jax.ShapeDtypeStruct((depth, pieces.shape[0]), BF16),
            jax.ShapeDtypeStruct((nb, depth, width), BF16),
            jax.ShapeDtypeStruct((nb, crows * cuts, width), BF16),
            jax.ShapeDtypeStruct((nb, vrows, bins), BF16),
        ],
        buffers(crows, width) * cuts
        + buffers(vrows, bins)
        + [pltpu.VMEM((nz, nx, CORES, nb, vrows, bins), BF16)] * fused
        + [pltpu.SemaphoreType.DMA((len(keys),)), pltpu.SemaphoreType.DMA((len(keys),))],
        3,
        trunk,
        proj_weight,
        pieces,
        code,
        *value,
    )


def dot(a, b, dims):
    return lax.dot_general(a, b, (dims, ((), ())), preferred_element_type=F32)


class Slots(Sends):
    def __init__(self, send_sem, recv_sem, send_at, recv_at, place):
        super().__init__(send_sem, recv_sem, (), place)
        self.send_at, self.recv_at = send_at, recv_at

    def join(self, key, like):
        self.like[key] = like
        self.started.append((key, ()))

    def make(self, key, src, dst, dev):
        return pltpu.make_async_remote_copy(
            src_ref=src,
            dst_ref=dst,
            send_sem=self.send_sem.at[self.send_at[key]],
            recv_sem=self.recv_sem.at[self.recv_at[key]],
            device_id=dev,
            device_id_type=MESH,
        )


def number(keys, first, apart=()):
    at, names = {}, {}
    for key in keys:
        name = key[:2] if key[0] in ("rz", "gc") else key
        if key[0] not in apart:
            name = tuple((0, k[1]) if isinstance(k, tuple) and k[1] > 1 else k for k in name)
        at[key] = first + names.setdefault(name, len(names))
    return at, first + len(names)


def fits(nb, nf, codebook, value_weight, depth, pos):
    nx = nf // (PLANES * CORES)
    rows, width = codebook.shape
    vrows = value_weight.shape[0]
    half, vhalf = rows // nb, vrows // nb
    return (
        nb > 1
        and nb * half == rows
        and nb * vhalf == vrows
        and half % 64 == 0
        and vhalf % 32 == 0
        and CORES * rows == 256
        and nx * CORES * vrows == 256
        and width == PLANES * 256
        and depth % 192 == 0
        and pos * CORES == 256
    )


EARLY = (
    ("sz", 1), ("sz", 0), ("sx", 0), ("sx", 2), ("sz", 2),
    ("sx", 1), ("z", 1, 1), ("x0", 0), ("z", 0, 1), ("z", 2, 1),
    ("x0", 1), ("x0", 2), ("core", 0, 1), ("z", 1, 2), ("z", 0, 2),
    ("core", 0, 2), ("zx", 0, 1), ("z", 2, 2), ("x", 1, 1), ("z", 0, 3),
    ("zy", 0, 1), ("z", 1, 3), ("d", 0, 0), ("zx", 0, 2), ("x", 2, 1),
    ("z", 2, 3), ("core", 0, 0), ("core", 1, 2), ("zx", 0, 3), ("x", 1, 3),
    ("x", 1, 2), ("core", 1, 1), ("core", 2, 1), ("zxy", 0, 1), ("core", 1, 0),
    ("score", 0), ("x", 2, 2), ("core", 2, 2), ("zy", 0, 2), ("zy", 0, 3),
    ("core", 3, 1), ("zxy", 0, 2), ("core", 2, 0), ("score", 1), ("x", 2, 3),
    ("core", 3, 2), ("zxy", 0, 3), ("core", 3, 0), ("score", 2), ("score", 3),
)
LATE = (
    ("pg", 0), ("pg", 1), ("pg", 2), ("pg", 3), ("z", 1, 1),
    ("z", 2, 1), ("z", 1, 2), ("x", 1, 0), ("z", 2, 2), ("z", 3, 1),
    ("z", 1, 3), ("x", 0, 0), ("z", 0, 1), ("x", 2, 0), ("code",),
    ("x", 2, 2), ("z", 2, 3), ("x", 1, 1), ("z", 3, 2), ("val",),
    ("x", 1, 2), ("rsx", 2), ("rsx", 0), ("x", 2, 1), ("zx", 0, 1),
    ("x", 1, 3), ("x", 2, 3), ("rsx", 1), ("proj", 2), ("x", 3, 2),
    ("z", 3, 3), ("z", 0, 2), ("proj", 1), ("rsx", 4), ("x", 3, 0),
    ("rsx", 3), ("zx", 0, 2), ("rsz", 2), ("rsz", 0), ("x", 3, 1),
    ("z", 0, 3), ("zx", 0, 3), ("proj", 0), ("rsz", 1), ("fin", 2),
    ("fin", 1), ("rsy", 2), ("x", 3, 3), ("rsz", 4), ("proj", 3),
    ("rsz", 3), ("rsy", 0), ("rsy", 1), ("col",), ("rsy", 4),
    ("rsy", 3), ("fin", 0), ("fin", 3),
)
CROSS_FIRST = (0,)


def fused(nb, nf, trunk, pre_act, proj_weight, codebook, value_weight, target, low, frac):
    nz, nx = PLANES, nf // (PLANES * CORES)
    pos, width = pre_act.shape
    rows, vrows = codebook.shape[0], value_weight.shape[0]
    bins = value_weight.shape[1]
    depth, total_pos = trunk.shape
    half, vhalf = rows // nb, vrows // nb
    cw = 256
    pieces = width // cw
    cuts = 4
    deep = nb * pos
    ck = half // cuts
    hops = [(0, 0)] + steps(nz)
    by_far = [[h for h in hops if h[1] == far] for far in range(nz)]

    early = []
    for a in range(3):
        for hop in hops:
            early += [("core", a, hop)]
            if hop[1]:
                early += [("z", a, hop)]
            if a == 0 and hop[1]:
                early += [("zy", a, hop, dy) for dy in range(1, nb)]
                for dx in range(1, nx):
                    early += [("zx", a, hop, dx)]
                    early += [("zxy", a, hop, dx, dy) for dy in range(1, nb)]
            else:
                early += [("x", a, hop, dx) for dx in range(1, nx)]
                if a == 0:
                    early += [("d", a, hop, dx, dy) for dx in range(1, nx) for dy in range(1, nb)]
    swap = [(k, dy) for dy in range(1, nb) for k in ("act", "tgt", "stat", "value")]
    swap += [("b", n, dy) for n in range(pieces) for dy in range(1, nb)]
    late = []
    for n in range(pieces):
        for hop in hops:
            late += [("gc", n, hop)]
            if hop[1]:
                late += [("gz", n, hop)]
            if hop[1] == 0 or n not in CROSS_FIRST:
                late += [("gx", n, hop, dx) for dx in range(1, nx)]
            else:
                late += [("gzx", n, hop, dx) for dx in range(1, nx)]
        late += [("p", n, dy) for dy in range(1, nb)]
    for a in range(cuts + 1):
        late += [("rc", a)] + [("rx", a, d) for d in range(1, nx)]
        late += [("rz", a, d) for d in range(1, nz)] + [("ry", a, d) for d in range(1, nb)]
    swap_at, base = number(swap, 0)
    early_send, sends = number(early, base, ("z", "zx"))
    early_recv, recvs = number(early, base)
    late_send, last = number(late, base, ("gz", "gzx"))
    sends = max(sends, last)
    late_recv, recvs = number(late, recvs)
    early_send.update(swap_at)
    early_recv.update(swap_at)
    late_send.update(swap_at)
    late_recv.update(swap_at)

    def kernel(
        pre_in,
        cb_in,
        vw_in,
        tgt_in,
        lo_in,
        fr_in,
        tr_in,
        pw_in,
        trg,
        pj,
        cd,
        vl,
        cb,
        vw,
        pre,
        tgt,
        lo,
        fr,
        tr,
        pw,
        cb_all,
        vw_all,
        gate,
        act_all,
        tgt_all,
        stat,
        back_out,
        back_in,
        logit,
        top,
        vlog,
        delta,
        vd_all,
        dt_all,
        pg,
        part,
        vpart,
        pj_all,
        cd_all,
        vl_all,
        *rest,
    ):
        local_sem, send_sem, recv_sem = rest[-3:]
        p = Place(nb, nf)
        inputs = (cb_in, vw_in, pre_in, tgt_in, lo_in, fr_in, tr_in, pw_in)
        loads = [
            pltpu.make_async_copy(src, dst, local_sem.at[i])
            for i, (src, dst) in enumerate(zip(inputs, (cb, vw, pre, tgt, lo, fr, tr, pw)))
        ]
        for load in loads:
            load.start()
        p.barrier()
        for load in loads[:3]:
            load.wait()
        s = Slots(send_sem, recv_sem, early_send, early_recv, p)
        g = Slots(send_sem, recv_sem, late_send, late_recv, p)

        def under(s, far, f):
            for hop in by_far[far]:
                if far:
                    s.only(lambda hop=hop: has(p, *hop))(lambda: f(hop))
                else:
                    f(hop)

        sub = half // 2
        shards = (
            (vw, vw_all, vhalf, 0, vhalf),
            (cb, cb_all, half, 0, sub),
            (cb, cb_all, half, sub, sub),
        )

        def like(a):
            own, out, piece, skip, size = shards[a]
            at = (0, 0, 0) if a else (0, 0, 0, 0)
            return lambda: out.at[at + (pl.ds(skip, size),)]

        def spot(a, z, x, h):
            own, out, piece, skip, size = shards[a]
            at = (z, x, p.c) if a else (z, x, p.c, h)
            return out.at[at + (pl.ds(skip, size),)]

        def relay(key, at_z, at_x, at_h, **to):
            ref = spot(key[1], at_z, at_x, at_h)
            s.go(key, ref, ref, p.dev(**to), like(key[1]))

        def publish(key, **to):
            own, out, piece, skip, size = shards[key[1]]
            src = own.at[pl.ds(pl.multiple_of(p.b * piece + skip, size), size)]
            s.go(key, src, spot(key[1], p.z, p.x, p.b), p.dev(**to), like(key[1]))

        def farther(kind, a, z, x, far, extra, ways):
            for way in ways:

                @s.only(lambda way=way: feeds(p, way))
                def _():
                    relay((kind, a, (way, far)) + extra, z, x, p.b, z=p.z + way)

        def send_x(a):
            for dx in range(1, nx):
                publish(("x", a, (0, 0), dx), x=p.xx(dx))

        def send_z(a):
            for way in (1, -1):

                @s.only(lambda way=way: feeds(p, way))
                def _():
                    publish(("z", a, (way, 1)), z=p.z + way)

        for name, a in EARLY[:6]:
            (send_x if name == "sx" else send_z)(a)
        cb_all[p.z, p.x, p.c] = cb[pl.ds(pl.multiple_of(p.b * half, half), half), :]
        vw_all[p.z, p.x, p.c] = vw[...].reshape(nb, vhalf, bins)

        def activate(i, carry):
            cols = pl.ds(pl.multiple_of(i * cw, cw), cw)
            v = pre[:, cols].astype(F32)
            sigma = jax.nn.sigmoid(v)
            active = v * sigma
            act_all[p.b, :, cols] = active.astype(BF16)
            gate[:, cols] = sigma * (1.0 + v * (1.0 - sigma))
            return carry

        lax.fori_loop(0, width // cw, activate, 0)
        for load in loads[3:6]:
            load.wait()
        tgt_all[p.b] = tgt[...]
        for dy in range(1, nb):
            for name, ref in (("act", act_all.at[p.b]), ("tgt", tgt_all.at[p.b])):
                g.go((name, dy), ref, ref, p.dev(b=p.bb(dy)))
        top[...] = jnp.full(top.shape, -jnp.inf, F32)
        vlog[...] = jnp.zeros(vlog.shape, F32)

        def from_x0(a):
            for dx in range(1, nx):
                s.arrived(("x", a, (0, 0), dx))
                if a == 0:
                    x = p.xx(-dx)
                    farther("zx", a, p.z, x, 1, (dx,), (1, -1))
                    for dy in range(1, nb):
                        relay(("d", a, (0, 0), dx, dy), p.z, x, p.b, b=p.bb(dy))

        def from_z(a, far):
            def run(hop):
                z = p.z - hop[0] * far
                s.arrived(("z", a, hop))
                if far + 1 < nz:
                    farther("z", a, z, p.x, far + 1, (), hop[:1])
                if a:
                    for dx in range(1, nx):
                        relay(("x", a, hop, dx), z, p.x, p.b, x=p.xx(dx))
                else:
                    for dy in range(1, nb):
                        relay(("zy", a, hop, dy), z, p.x, p.b, b=p.bb(dy))

            under(s, far, run)

        def from_zx(a, far):
            def run(hop):
                z = p.z - hop[0] * far
                for dx in range(1, nx):
                    s.arrived(("zx", a, hop, dx))
                    x = p.xx(-dx)
                    if far + 1 < nz:
                        farther("zx", a, z, x, far + 1, (dx,), hop[:1])
                    for dy in range(1, nb):
                        relay(("zxy", a, hop, dx, dy), z, x, p.b, b=p.bb(dy))

            under(s, far, run)

        def from_x(a, far):
            under(s, far, lambda hop: [s.arrived(("x", a, hop, dx)) for dx in range(1, nx)])

        def landed(kind):
            def wait(a, far):
                def run(hop):
                    for key in early:
                        if key[:3] == (kind, a, hop):
                            s.arrived(key)

                under(s, far, run)

            return wait

        def to_other(far, a):
            own, out, piece, skip, size = shards[a]
            part = pl.ds(skip, size)

            def run(hop):
                z = p.z - hop[0] * far
                ref = out.at[z, :, p.c, part] if a else out.at[z, :, p.c, :, part]
                held = lambda: out.at[0, :, 0, part] if a else out.at[0, :, 0, :, part]
                s.go(("core", a, hop), ref, ref, p.dev(c=1 - p.c), held)

            under(s, far, run)

        def near(j):
            up = (0, 1, 2, 3)[j], (1, 0, 2, 3)[j], (2, 3, 1, 0)[j], (3, 2, 1, 0)[j]
            z = jnp.where(p.z == 0, up[0], up[3])
            z = jnp.where(p.z == 1, up[1], z)
            return jnp.where(p.z == 2, up[2], z)

        def score(j):
            z = near(j)
            for a in range(3):
                landed("core")(a, j)

            plane = nx * CORES * half
            if j == 0:
                for dy in range(1, nb):
                    g.arrived(("act", dy))
            block = dot(
                cb_all[z].reshape(plane, width), act_all[...].reshape(deep, width), ((1,), (1,))
            )
            logit[pl.ds(pl.multiple_of(z * plane, plane), plane), :] = block
            top[...] = jnp.maximum(top[...], jnp.max(block, axis=0, keepdims=True))
            at = pl.ds(pl.multiple_of(z * 256, 256), 256)
            vlog[...] += dot(act_all[p.b, :, at], vw_all[z].reshape(256, bins), ((1,), (0,)))

        acts = dict(
            x0=from_x0, z=from_z, zx=from_zx, x=from_x, d=landed("d"), zy=landed("zy"),
            zxy=landed("zxy"), core=to_other, score=score,
        )
        for name, *where in EARLY[6:]:
            acts[name](*where)
        blocks = nf * half // 256
        best = top[...]

        def grow(i, total):
            at = pl.ds(pl.multiple_of(i * 256, 256), 256)
            e = jnp.exp(logit[at, :] - best)
            logit[at, :] = e
            return total + jnp.sum(e, axis=0, keepdims=True)

        mass = lax.fori_loop(0, blocks, grow, jnp.zeros((1, deep), F32))
        stat[p.b, 0] = jnp.broadcast_to(best, (8, deep))
        stat[p.b, 1] = jnp.broadcast_to(mass, (8, deep))
        for dy in range(1, nb):
            ref = stat.at[p.b]
            g.go(("stat", dy), ref, ref, p.dev(b=p.bb(dy)))
        s.finish()
        high = jnp.max(vlog[...], axis=1, keepdims=True)
        grown = jnp.exp(vlog[...] - high)
        probs = grown * (1.0 / jnp.sum(grown, axis=1, keepdims=True))
        ids = lax.broadcasted_iota(jnp.int32, (pos, bins), 1).astype(F32)
        column = jnp.broadcast_to(lo[...].astype(F32), (pos, pos)).T[:, :1]
        share = jnp.broadcast_to(fr[...].astype(F32) / 1024.0, (pos, pos)).T[:, :1]
        want = jnp.where(ids == column, 1.0 - share, 0.0)
        want = want + jnp.where(ids == column + 1.0, share, 0.0)
        vd_all[p.b] = (probs - want).astype(BF16)

        for dy in range(1, nb):
            g.arrived(("stat", dy))
            g.arrived(("tgt", dy))
        peak = stat[0, 0, :1]
        for b in range(1, nb):
            peak = jnp.maximum(peak, stat[b, 0, :1])
        mass = jnp.zeros((1, deep), F32)
        for b in range(nb):
            mass = mass + stat[b, 1, :1] * jnp.exp(stat[b, 0, :1] - peak)
        scale = jnp.exp(best - peak) * (1.0 / mass)
        aim = jnp.concatenate([tgt_all[b] for b in range(nb)], axis=1)
        group = 256 // half
        row = lax.broadcasted_iota(jnp.int32, (256, deep), 0)
        code_ids = lax.div(row, half) * rows + lax.rem(row, half) + p.b * half

        def differ(i, carry):
            at = pl.ds(pl.multiple_of(i * 256, 256), 256)
            hot = jnp.where(code_ids + i * (group * rows) == aim, 1.0, 0.0)
            d = logit[at, :] * scale - hot
            delta[:, at] = d.T.astype(BF16)
            dt_all[pl.ds(i * group, group)] = d.astype(BF16).reshape(group, half, deep)
            return carry

        lax.fori_loop(0, blocks, differ, 0)

        def back_from(b, n):
            cols = pl.ds(n * cw, cw)
            left = delta[pl.ds(pl.multiple_of(b * pos, pos), pos), :]
            return dot(left, cb_all[:, :, :, :, cols].reshape(nf * half, cw), ((1,), (0,)))

        for n in range(pieces):
            for dy in range(1, nb):
                back_out[dy - 1, n] = back_from(p.bb(dy), n).astype(BF16)
                g.go(
                    ("b", n, dy), back_out.at[dy - 1, n], back_in.at[dy - 1, n], p.dev(b=p.bb(dy))
                )
        for dy in range(1, nb):
            ref = vd_all.at[p.b]
            g.go(("value", dy), ref, ref, p.dev(b=p.bb(dy)))

        def pass_on(n, at_z, at_x, key, **to):
            ref = pg.at[n, at_z, at_x, p.c]
            g.go(key, ref, ref, p.dev(**to), lambda: pg.at[n, 0, 0, 0])

        def onward(n, kind, z, x, far, extra, ways):
            for way in ways:

                @g.only(lambda way=way: feeds(p, way))
                def _():
                    pass_on(n, z, x, (kind, n, (way, far)) + extra, z=p.z + way)

        def across(n, hop):
            for dx in range(1, nx):
                pass_on(n, p.z - hop[0] * hop[1], p.x, ("gx", n, hop, dx), x=p.xx(dx))

        def to_core(n, hop):
            ref = pg.at[n, p.z - hop[0] * hop[1], :, p.c]
            g.make(("gc", n, hop), ref, ref, p.dev(c=1 - p.c)).start()

        def head(n):
            cols = pl.ds(n * cw, cw)
            back = back_from(p.b, n)
            back = back + dot(vd_all[p.b], vw_all[n].reshape(cw, bins), ((1,), (1,)))
            for dy in range(1, nb):
                g.arrived(("b", n, dy))
                back = back + back_in[dy - 1, n].astype(F32)
            pg[n, p.z, p.x, p.c] = (back * gate[:, cols]).astype(BF16)
            if n in CROSS_FIRST:
                across(n, (0, 0))
            onward(n, "gz", p.z, p.x, 1, (), (1, -1))
            if n not in CROSS_FIRST:
                across(n, (0, 0))

        def grad_z(n, far):
            def run(hop):
                z = p.z - hop[0] * far
                g.arrived(("gz", n, hop))
                if far + 1 < nz:
                    onward(n, "gz", z, p.x, far + 1, (), hop[:1])
                if n not in CROSS_FIRST:
                    across(n, hop)

            under(g, far, run)

        def grad_x(n, far):
            def run(hop):
                for dx in range(1, nx):
                    g.arrived(("gx", n, hop, dx))
                    if n in CROSS_FIRST:
                        onward(n, "gzx", p.z, p.xx(-dx), 1, (dx,), (1, -1))
                to_core(n, hop)

            under(g, far, run)

        def grad_zx(n, far):
            def run(hop):
                for dx in range(1, nx):
                    g.arrived(("gzx", n, hop, dx))
                    if far + 1 < nz:
                        onward(n, "gzx", p.z - hop[0] * far, p.xx(-dx), far + 1, (dx,), hop[:1])
                to_core(n, hop)

            under(g, far, run)

        arrays = []
        for a in range(cuts + 1):
            if a < cuts:
                own, out = part.at[:, :, :, pl.ds(a * ck, ck)], cd_all.at[:, pl.ds(a * ck, ck)]
            else:
                own, out = vpart.at[:, :, :, p.b], vl_all
            arrays.append((own, out) + tuple(rest[6 * a : 6 * a + 6]))

        def to_sum(a):
            own, out, core, *_ = arrays[a]
            g.go(("rc", a), own.at[:, :, 1 - p.c], core, p.dev(c=1 - p.c))

        def code():
            def block(i, carry):
                z = i // (width // cw)
                cols = pl.ds(pl.multiple_of((i % (width // cw)) * cw, cw), cw)
                left = dt_all[pl.ds(z * nx * CORES, nx * CORES)].reshape(nx * CORES * half, deep)
                right = act_all[:, :, cols].reshape(deep, cw)
                product = dot(left, right, ((1,), (0,)))
                part[z, :, :, :, cols] = product.astype(BF16).reshape(nx, CORES, half, cw)
                return carry

            lax.fori_loop(0, nz * (width // cw), block, 0)
            for a in range(cuts):
                to_sum(a)

        def val():
            for dy in range(1, nb):
                g.arrived(("value", dy))

            def block(z, carry):
                cols = pl.ds(pl.multiple_of(z * 256, 256), 256)
                left = act_all[:, :, cols].reshape(deep, 256)
                product = dot(left, vd_all[...].reshape(deep, bins), ((0,), (0,)))
                vpart[z] = product.astype(BF16).reshape(nx, CORES, nb, vhalf, bins)
                return carry

            lax.fori_loop(0, nz, block, 0)
            to_sum(cuts)

        def rsx(a):
            own, out, core, xin, xsend, acc, zin, zsend = arrays[a]
            g.arrived(("rc", a))
            for dx in range(1, nx):
                x = p.xx(dx)
                for z in range(nz):
                    both = own[z, x, p.c].astype(F32) + core[z, x].astype(F32)
                    xsend[dx - 1, z] = both.astype(BF16)
                g.go(("rx", a, dx), xsend.at[dx - 1], xin.at[dx - 1], p.dev(x=x))
            for z in range(nz):
                acc[z] = own[z, p.x, p.c].astype(F32) + core[z, p.x].astype(F32)

        def rsz(a):
            own, out, core, xin, xsend, acc, zin, zsend = arrays[a]
            for dx in range(1, nx):
                g.arrived(("rx", a, dx))
                acc[...] += xin[dx - 1].astype(F32)
            for dz in [2, 1, 3]:
                z = p.zz(dz)
                zsend[dz - 1] = acc[z].astype(BF16)
                g.make(("rz", a, dz), zsend.at[dz - 1], zin.at[dz - 1], p.dev(z=z)).start()
            g.join(("rz", a, 1), zin)

        def rsy(a):
            own, out, core, xin, xsend, acc, zin, zsend = arrays[a]
            total = acc[p.z]
            g.arrived(("rz", a, 1))
            for dz in range(1, nz):
                total = total + zin[dz - 1].astype(F32)
            out[p.b] = total.astype(BF16)
            for dy in range(1, nb):
                g.go(("ry", a, dy), out.at[p.b], out.at[p.b], p.dev(b=p.bb(dy)))

        def proj(n):
            g.join(("gc", n, (0, 0)), lambda: pg.at[n, :, :, 0])
            g.arrived(("gc", n, (0, 0)))

            def block(i, carry):
                at = pl.ds(pl.multiple_of(i * 192, 192), 192)
                pj_all[p.b, n, at, :] = jnp.dot(
                    tr[at, :], pg[n].reshape(total_pos, cw), preferred_element_type=F32
                ).astype(BF16)
                return carry

            lax.fori_loop(0, depth // 192, block, 0)
            for dy in range(1, nb):
                ref = pj_all.at[p.b, n]
                g.go(("p", n, dy), ref, ref, p.dev(b=p.bb(dy)))

        def col():
            def block(i, carry):
                at = pl.ds(pl.multiple_of(i * 256, 256), 256)
                z, x = i // nx, i % nx
                total = 0.0
                for n in range(pieces):
                    there = pg[n, z, x].reshape(256, cw)
                    total = total + dot(pw[:, pl.ds(n * cw, cw)], there, ((1,), (1,)))
                trg[:, at] = total.astype(BF16)
                return carry

            lax.fori_loop(0, nz * nx, block, 0)

        def fin(n):
            for dy in range(1, nb):
                g.arrived(("p", n, dy))
            total = pj_all[0, n].astype(F32)
            for b in range(1, nb):
                total = total + pj_all[b, n].astype(F32)
            pj[:, pl.ds(n * cw, cw)] = total

        for load in loads[6:]:
            load.wait()
        acts = dict(
            pg=head, z=grad_z, x=grad_x, zx=grad_zx, code=code, val=val, rsx=rsx, rsz=rsz, rsy=rsy,
            proj=proj, col=col, fin=fin,
        )
        for name, *where in LATE:
            acts[name](*where)
        for a in range(cuts + 1):
            for dy in range(1, nb):
                g.arrived(("ry", a, dy))
        for b in range(nb):
            cd[pl.ds(b * half, half), :] = cd_all[b].astype(F32)
            vl[pl.ds(b * vhalf, vhalf), :] = vl_all[b].astype(F32)
        g.finish()

    def buffers(r, k):
        return [
            pltpu.VMEM((nz, nx, r, k), BF16),
            pltpu.VMEM((max(nx - 1, 1), nz, r, k), BF16),
            pltpu.VMEM((max(nx - 1, 1), nz, r, k), BF16),
            pltpu.VMEM((nz, r, k), F32),
            pltpu.VMEM((nz - 1, r, k), BF16),
            pltpu.VMEM((nz - 1, r, k), BF16),
        ]

    anywhere = pl.BlockSpec(memory_space=pl.ANY)
    stay = pl.BlockSpec(memory_space=pltpu.HBM)
    results = pl.pallas_call(
        kernel,
        out_shape=[
            jax.ShapeDtypeStruct((depth, total_pos), BF16),
            jax.ShapeDtypeStruct((depth, width), F32),
            jax.ShapeDtypeStruct((rows, width), F32),
            jax.ShapeDtypeStruct((vrows, bins), F32),
        ],
        in_specs=[stay] * 8,
        out_specs=[pl.BlockSpec(memory_space=pltpu.VMEM)] * 4,
        scratch_shapes=[
            pltpu.VMEM((rows, width), BF16),
            pltpu.VMEM((vrows, bins), BF16),
            pltpu.VMEM((pos, width), BF16),
            pltpu.VMEM((1, pos), jnp.int32),
            pltpu.VMEM((1, pos), jnp.int32),
            pltpu.VMEM((1, pos), jnp.int32),
            pltpu.VMEM((depth, total_pos), BF16),
            pltpu.VMEM((depth, width), BF16),
            pltpu.VMEM((nz, nx, CORES, half, width), BF16),
            pltpu.VMEM((nz, nx, CORES, nb, vhalf, bins), BF16),
            pltpu.VMEM((pos, width), F32),
            pltpu.VMEM((nb, pos, width), BF16),
            pltpu.VMEM((nb, 1, pos), jnp.int32),
            pltpu.VMEM((nb, 2, 8, deep), F32),
            pltpu.VMEM((nb - 1, pieces, pos, cw), BF16),
            pltpu.VMEM((nb - 1, pieces, pos, cw), BF16),
            pltpu.VMEM((nf * half, deep), F32),
            pltpu.VMEM((1, deep), F32),
            pltpu.VMEM((pos, bins), F32),
            pltpu.VMEM((deep, nf * half), BF16),
            pltpu.VMEM((nb, pos, bins), BF16),
            pltpu.VMEM((nf, half, nb * pos), BF16),
            pltpu.VMEM((pieces, nz, nx, CORES, pos, cw), BF16),
            pltpu.VMEM((nz, nx, CORES, half, width), BF16),
            pltpu.VMEM((nz, nx, CORES, nb, vhalf, bins), BF16),
            pltpu.VMEM((nb, pieces, depth, cw), BF16),
            pltpu.VMEM((nb, half, width), BF16),
            pltpu.VMEM((nb, vhalf, bins), BF16),
        ]
        + buffers(ck, width) * cuts
        + buffers(vhalf, bins)
        + [
            pltpu.SemaphoreType.DMA((8,)),
            pltpu.SemaphoreType.DMA((sends,)),
            pltpu.SemaphoreType.DMA((recvs,)),
        ],
        compiler_params=pltpu.CompilerParams(
            collective_id=4, has_side_effects=True, vmem_limit_bytes=44 << 20
        ),
    )(
        *(
            pltpu.with_memory_space_constraint(x, pltpu.HBM)
            for x in (
                pre_act, codebook, value_weight, target, low, frac, trunk, proj_weight,
            )
        )
    )

    def hand_over(*refs):
        copies = [
            pltpu.make_async_copy(refs[i], refs[4 + i], refs[8].at[i]) for i in range(4)
        ]
        for copy in copies:
            copy.start()
        for copy in copies:
            copy.wait()

    return pl.pallas_call(
        hand_over,
        out_shape=[jax.ShapeDtypeStruct(r.shape, r.dtype) for r in results],
        in_specs=[anywhere] * 4,
        out_specs=[stay] * 4,
        scratch_shapes=[pltpu.SemaphoreType.DMA((4,))],
        compiler_params=pltpu.CompilerParams(vmem_limit_bytes=1 << 20),
    )(*results)


def make_body(nb, nf):
    nz, nx = PLANES, nf // (PLANES * CORES)

    def body(
        trunk, pre_act, proj_weight, codebook, value_weight, code_target, value_bin, value_frac
    ):
        if fits(nb, nf, codebook, value_weight, trunk.shape[0], pre_act.shape[0]):
            row = (1, pre_act.shape[0])
            return fused(
                nb,
                nf,
                trunk,
                pre_act,
                proj_weight,
                codebook,
                value_weight,
                code_target.reshape(row),
                value_bin.reshape(row),
                value_frac.reshape(row),
            )
        all_codes, bins_weight = gather_weights(nb, nf, codebook, value_weight)
        rows, width = pre_act.shape
        num_codes = all_codes.shape[0]
        num_bins = bins_weight.shape[1]
        pre_value = pre_act.astype(F32)
        gate_sigma = jax.nn.sigmoid(pre_value)
        active = (pre_value * gate_sigma).astype(BF16)
        code_logits = jnp.einsum("rk,ck->rc", active, all_codes, preferred_element_type=F32)
        code_probs = jax.nn.softmax(code_logits, axis=-1)
        code_ids = lax.broadcasted_iota(jnp.int32, (1, num_codes), 1)
        one_hot = (code_target[:, None] == code_ids).astype(F32)
        code_delta = (code_probs - one_hot).astype(BF16)
        value_logits = jnp.dot(active, bins_weight, preferred_element_type=F32)
        value_probs = jax.nn.softmax(value_logits, axis=-1)
        bin_ids = lax.broadcasted_iota(jnp.int32, (1, num_bins), 1)
        fraction = value_frac.astype(F32)[:, None] / 1024.0
        target = jnp.where(bin_ids == value_bin[:, None], 1.0 - fraction, 0.0)
        target = target + jnp.where(bin_ids == value_bin[:, None] + 1, fraction, 0.0)
        value_delta = (value_probs - target).astype(BF16)
        backward = jnp.dot(code_delta, all_codes, preferred_element_type=F32)
        backward = backward + jnp.einsum(
            "rb,kb->rk", value_delta, bins_weight, preferred_element_type=F32
        )
        pre_grad = (backward * gate_sigma * (1.0 + pre_value * (1.0 - gate_sigma))).astype(BF16)
        own = codebook.shape[0] // nb
        delta_t = code_delta.T.reshape(nf, nb, own, rows).swapaxes(0, 1)
        delta_t = delta_t.reshape(nb, nf * own, rows)
        pieces, act_all, dt_all, vd_all = gather_grads(
            nb, nf, pre_grad, active, delta_t, value_delta
        )
        code_part = jnp.dot(dt_all, act_all, preferred_element_type=F32)
        code_part = code_part.astype(BF16).reshape(nz, nx, CORES, own, width)
        vown = value_weight.shape[0] // nb
        if vown % 16 == 0:
            value_part = (act_all, vd_all)
        else:
            value_part = jnp.einsum("rk,rb->kb", act_all, vd_all, preferred_element_type=F32)
            value_part = value_part.astype(BF16)
            value_part = (value_part.reshape(nz, nx, CORES, nb, vown, num_bins),)
        out_cols, proj_all, code_all, value_all = reduce_grads(
            nb, nf, trunk, proj_weight, pieces, code_part, value_part
        )
        proj_grad = jnp.sum(proj_all.astype(F32), axis=0)
        code_grad = code_all.reshape(nb * own, width).astype(F32)
        value_grad = value_all.reshape(nb * vown, num_bins).astype(F32)
        return (out_cols, proj_grad, code_grad, value_grad)

    return body


def solution(mesh):
    in_specs = (
        P("fsdp", "batch"),
        P(("batch", "fsdp"), None),
        P("fsdp", None),
        P("fsdp", None),
        P("fsdp", None),
        P(("batch", "fsdp")),
        P(("batch", "fsdp")),
        P(("batch", "fsdp")),
    )
    out_specs = (P("fsdp", "batch"), P("fsdp", None), P("fsdp", None), P("fsdp", None))
    body = make_body(mesh.shape["batch"], mesh.shape["fsdp"])
    return jax.shard_map(body, mesh=mesh, in_specs=in_specs, out_specs=out_specs, check_vma=False)
```
